32 devices in a mesh: replica: 16 (over z, x, core), shard: 2 (over y).
Axes of the slice: x: 2, y: 2, z: 4, core: 2. Of those that a mesh axis runs over, the one named last changes fastest.
Arguments:
- inputs: bfloat16 [32768, 768], P(('replica', 'shard')), may hold values from -6 to 6
- segments: int32 [32, 1024], P(('replica', 'shard')), may hold values from 0 to 15, never falling along the last dimension, each value on 1 to 512 neighbouring positions
- w_qkv: bfloat16 [768, 2304], P('shard'), may hold values from -0.21875 to 0.21875
- b_qv: bfloat16 [1536], P('shard'), may hold values from -3 to 3
- w_out: bfloat16 [768, 768], P('shard'), may hold values from -0.875 to 0.875
- b_out: bfloat16 [768], P('shard'), may hold values from -3 to 3
- attn_gain: bfloat16 [768], P('shard'), may hold values from 0.5 to 1.5
- attn_shift: bfloat16 [768], P('shard'), may hold values from -3 to 3
- w_up: bfloat16 [768, 3072], P('shard'), may hold values from -0.21875 to 0.21875
- b_up: bfloat16 [3072], P('shard'), may hold values from -3 to 3
- w_down: bfloat16 [3072, 768], P('shard'), may hold values from -0.109375 to 0.109375
- b_down: bfloat16 [768], P('shard'), may hold values from -3 to 3
- ffn_gain: bfloat16 [768], P('shard'), may hold values from 0.5 to 1.5
- ffn_shift: bfloat16 [768], P('shard'), may hold values from -3 to 3
- cotangent: bfloat16 [32768, 768], P(('replica', 'shard')), may hold values from -6 to 6
Outputs:
- layer_output: bfloat16 [32768, 768], P(('replica', 'shard'))
- input_grad: bfloat16 [32768, 768], P(('replica', 'shard'))
- w_qkv_grad: float32 [768, 2304], P('shard')
- b_qv_grad: float32 [1536], P('shard')
- w_out_grad: float32 [768, 768], P('shard')
- b_out_grad: float32 [768], P('shard')
- attn_gain_grad: float32 [768], P('shard')
- attn_shift_grad: float32 [768], P('shard')
- w_up_grad: float32 [768, 3072], P('shard')
- b_up_grad: float32 [3072], P('shard')
- w_down_grad: float32 [3072, 768], P('shard')
- b_down_grad: float32 [768], P('shard')
- ffn_gain_grad: float32 [768], P('shard')
- ffn_shift_grad: float32 [768], P('shard')
The draws below stay inside these ranges and needn't reach their ends.
Inputs may be any that keep to these rules, and one draw needn't show every extreme that they name: `segments`: within each sequence the document numbers never fall; each document has 1 to 512 tokens and one document of each sequence has exactly 512.
All inputs are finite; a program needn't handle non-finite values.
Results may differ from the reference program's by a relative error of at most 0.019.
Values may be sent and summed in bfloat16 or wider, within the bound.
No kernel may reach another device: no remote copies, remote signals or barrier semaphores. Data moves between devices by JAX's collectives and lax.ppermute only.
A program may use at most 192 MiB of HBM per device.

```python
import math
import jax
import jax.numpy as jnp
import numpy as np
from jax import lax

D = 768
HEADS = 12
HEAD_DIM = 64
FF = 3072
LEN = 1024
DOCS = 16
MOST = 512
SEQS = 32
TOKENS = 32768


def level_of(rng, shape, split, smallest, top_value):
    loudness, own = 1.0, jax.random.fold_in(rng, 6)
    for axis_at, blocks in split:
        heights = jnp.exp(jax.random.uniform(jax.random.fold_in(own, axis_at), (blocks,), jnp.float32, smallest / len(split), top_value / len(split)))
        loudness = loudness * jnp.repeat(heights, shape[axis_at] // blocks).reshape([-1 if axis == axis_at else 1 for axis in range(len(shape))])
    return loudness


def split_up(amount, total, bound, lean):
    portions = [(1 << 20) // math.isqrt(grade ** lean) + 1 for grade in range(2, amount + 1)]
    spare, holding = total - bound - (amount - 1), [1] * (amount - 1)
    while spare > 0:
        movable = [i for i in range(amount - 1) if holding[i] < bound]
        mass, left = sum([portions[i] for i in movable]), spare
        for i in movable:
            addition = min(bound - holding[i], max(1, left * portions[i] // mass), spare)
            holding[i] = holding[i] + addition
            spare = spare - addition
    return np.array([bound] + holding)


def ragged_sizes(stream_key, number_of, total, limit, lean):
    if number_of == 2:
        one = jax.random.randint(stream_key, (), max(1, total - limit), min(limit, total - 1) + 1)
        return jnp.stack([one, total - one])
    lengths = jnp.asarray(split_up(number_of, total, limit, lean), jnp.int32)
    couples = (number_of - 1) // 2
    donor, taker = lengths[1:1 + 2 * couples:2], lengths[2:2 + 2 * couples:2]
    margin = jnp.minimum(donor - 1, limit - taker)
    shifted = jax.random.randint(jax.random.fold_in(stream_key, 1), (couples,), 0, 1 << 20) % (margin + 1)
    lengths = lengths.at[1:1 + 2 * couples:2].set(donor - shifted).at[2:2 + 2 * couples:2].set(taker + shifted)
    return lengths[jax.random.permutation(jax.random.fold_in(stream_key, 2), number_of)]


def noise(stream_key, shape, deviation, most, pieces=(), kind=jnp.bfloat16):
    values = deviation * jax.random.normal(stream_key, shape, jnp.float32)
    if pieces:
        values = values * level_of(stream_key, shape, pieces, -0.22, 0.18)
    return jnp.clip(values, -most, most).astype(kind)


def setup_inputs(seed: int = 0) -> dict:
    seeds = jax.random.split(jax.random.key(seed), 16)
    inputs = noise(seeds[0], (TOKENS, D), 1.0, 6.0, ((0, 32),))
    segments = jax.vmap(lambda own: jnp.searchsorted(jnp.cumsum(ragged_sizes(own, DOCS, LEN, MOST, 2)), jnp.arange(LEN), side="right"))(jax.random.split(seeds[1], SEQS)).reshape((SEQS, LEN)).astype(jnp.int32)
    w_qkv = noise(seeds[2], (D, 3 * D), D ** -0.5, 0.21875, ((0, 2),))
    b_qv = noise(seeds[3], (2 * D,), 0.5, 3.0, ((0, 2),))
    w_out = noise(seeds[4], (D, D), (D // 16) ** -0.5, 0.875, ((0, 2),))
    b_out = noise(seeds[5], (D,), 0.5, 3.0, ((0, 2),))
    attn_gain = jnp.clip(1.0 + 0.1 * jax.random.normal(seeds[6], (D,), jnp.float32), 0.5, 1.5).astype(jnp.bfloat16)
    attn_shift = noise(seeds[7], (D,), 0.5, 3.0, ((0, 2),))
    w_up = noise(seeds[8], (D, FF), D ** -0.5, 0.21875, ((0, 2),))
    b_up = noise(seeds[9], (FF,), 0.5, 3.0, ((0, 2),))
    w_down = noise(seeds[10], (FF, D), FF ** -0.5, 0.109375, ((0, 2),))
    b_down = noise(seeds[11], (D,), 0.5, 3.0, ((0, 2),))
    ffn_gain = jnp.clip(1.0 + 0.1 * jax.random.normal(seeds[12], (D,), jnp.float32), 0.5, 1.5).astype(jnp.bfloat16)
    ffn_shift = noise(seeds[13], (D,), 0.5, 3.0, ((0, 2),))
    cotangent = noise(seeds[14], (TOKENS, D), 1.0, 6.0, ((0, 32),))
    return {"inputs": inputs, "segments": segments, "w_qkv": w_qkv, "b_qv": b_qv, "w_out": w_out, "b_out": b_out, "attn_gain": attn_gain, "attn_shift": attn_shift, "w_up": w_up, "b_up": b_up, "w_down": w_down, "b_down": b_down, "ffn_gain": ffn_gain, "ffn_shift": ffn_shift, "cotangent": cotangent}


EPSILON = 1e-12
MASKED_SCORE = -1000000000.0

@jax.custom_vjp
def low(v):
    return lax.optimization_barrier(v.astype(jnp.bfloat16)).astype(jnp.float32)

@jax.custom_vjp
def low_back(v):
    return v

def low_keep(v):
    return (low(v), None)

def low_pass(kept, grad):
    return (grad,)

def back_keep(v):
    return (v, None)

def back_low(kept, grad):
    return (low(grad),)
low.defvjp(low_keep, low_pass)
low_back.defvjp(back_keep, back_low)

def both_ways(value):
    return low(low_back(value))

def matmul(left, right):
    return jnp.dot(left, right, precision=lax.Precision.HIGHEST)

def layer_norm(hidden, gain, shift):
    average = lax.optimization_barrier(jnp.mean(hidden, axis=-1, keepdims=True))
    centered = hidden - average
    variance = lax.optimization_barrier(jnp.mean(centered * centered, axis=-1, keepdims=True))
    return centered * lax.rsqrt(variance + EPSILON) * gain + shift

def one_sequence(params, seq_tokens, seq_segments):
    w_qkv, b_qv, w_out, b_out, attn_gain, attn_shift, w_up, b_up, w_down, b_down, ffn_gain, ffn_shift = params
    qkv_bias = jnp.concatenate([b_qv[:D], jnp.zeros_like(b_qv[:D]), b_qv[D:]])
    projected = both_ways(matmul(seq_tokens, w_qkv) + qkv_bias)
    query_rows = projected[:, :D].reshape(LEN, HEADS, HEAD_DIM)
    key_rows = projected[:, D:2 * D].reshape(LEN, HEADS, HEAD_DIM)
    value_rows = projected[:, 2 * D:].reshape(LEN, HEADS, HEAD_DIM)
    raw_scores = jnp.einsum('qhd,khd->hqk', query_rows, key_rows, precision=lax.Precision.HIGHEST) * HEAD_DIM ** (-0.5)
    scores = low_back(raw_scores)
    same_doc = seq_segments[:, None] == seq_segments[None, :]
    masked = jnp.where(same_doc[None], scores, MASKED_SCORE)
    attn_probs = low(jax.nn.softmax(masked, axis=-1))
    context = jnp.einsum('hqk,khd->qhd', attn_probs, value_rows, precision=lax.Precision.HIGHEST)
    context = both_ways(context.reshape(LEN, D))
    attended = low_back(matmul(context, w_out) + b_out)
    normed_one = layer_norm(seq_tokens + attended, attn_gain, attn_shift)
    up_proj = low_back(matmul(low(normed_one), w_up) + b_up)
    activated = low(jax.nn.gelu(up_proj, approximate=False))
    down_proj = low_back(matmul(activated, w_down) + b_down)
    return layer_norm(normed_one + down_proj, ffn_gain, ffn_shift)

def reference(inputs, segments, w_qkv, b_qv, w_out, b_out, attn_gain, attn_shift, w_up, b_up, w_down, b_down, ffn_gain, ffn_shift, cotangent):
    params = tuple((weight.astype(jnp.float32) for weight in (w_qkv, b_qv, w_out, b_out, attn_gain, attn_shift, w_up, b_up, w_down, b_down, ffn_gain, ffn_shift)))
    seq_inputs = inputs.astype(jnp.float32).reshape(SEQS, LEN, D)
    seq_cotangent = cotangent.astype(jnp.float32).reshape(SEQS, LEN, D)
    block = jax.checkpoint(one_sequence)

    def forward(weights, tokens_all):

        def apply_one(operands):
            return block(weights, operands[0], operands[1])
        return lax.map(apply_one, (tokens_all, segments))
    outputs, pullback = jax.vjp(forward, params, seq_inputs)
    weight_grads, tokens_grad = pullback(seq_cotangent)
    return (outputs.reshape(TOKENS, D).astype(jnp.bfloat16), tokens_grad.reshape(TOKENS, D).astype(jnp.bfloat16), weight_grads[0], weight_grads[1], weight_grads[2], weight_grads[3], weight_grads[4], weight_grads[5], weight_grads[6], weight_grads[7], weight_grads[8], weight_grads[9], weight_grads[10], weight_grads[11])
```

```python
import functools

import jax
import jax.numpy as jnp
from jax import lax
from jax.experimental import pallas as pl
from jax.experimental.pallas import tpu as pltpu
from jax.sharding import PartitionSpec as P

D = 768
HEADS = 12
HEAD_DIM = 64
LEN = 1024
PAIRS = HEADS // 2
WIDE = 2 * HEAD_DIM
KEY_TILE = 128
FORWARD_ROWS = 512
BACKWARD_ROWS = 256
BIG = float(2**30)
EPSILON = 1e-12
F32 = jnp.float32
LOW = jnp.bfloat16


def layer_norm(hidden, gain, shift):
    average = jnp.mean(hidden, axis=-1, keepdims=True)
    centered = hidden - average
    variance = jnp.mean(centered * centered, axis=-1, keepdims=True)
    return centered * lax.rsqrt(variance + EPSILON) * gain + shift


def gelu_exact(value):
    return jax.nn.gelu(value, approximate=False)


def matmul(left, right):
    return jnp.dot(left, right, preferred_element_type=F32)


def matmul_right_t(left, right):
    return lax.dot_general(left, right, (((1,), (1,)), ((), ())), preferred_element_type=F32)


def matmul_left_t(left, right):
    return lax.dot_general(left, right, (((0,), (0,)), ((), ())), preferred_element_type=F32)


def as_float(value):
    return value.astype(F32)


def key_ranges(segments, rows):
    tiles = segments.reshape(LEN // rows, rows)
    below = jnp.sum(segments[None, :] < tiles[:, :1], axis=1, dtype=jnp.int32)
    upto = jnp.sum(segments[None, :] <= tiles[:, -1:], axis=1, dtype=jnp.int32)
    start = below // KEY_TILE
    count = (upto + KEY_TILE - 1) // KEY_TILE - start
    return jnp.concatenate([start, count])


def document_features(segments):
    lane = jnp.arange(WIDE, dtype=jnp.int32) % HEAD_DIM
    hot = segments[:, None] == lane[None, :]
    query_side = jnp.where((lane < 16) & hot, 1.0, 0.0).astype(LOW)
    key_side = jnp.where(
        lane < 16, jnp.where(hot, 0.0, -BIG), jnp.where(lane < 19, 1.0, 0.0)
    ).astype(LOW)
    return query_side, key_side


def attention_forward_body(
    ranges, packed, feature_q, feature_k, context, log_total, key_a, key_b, value_a, value_b
):
    rows = FORWARD_ROWS
    tiles = LEN // rows
    left = lax.broadcasted_iota(jnp.int32, (LEN, WIDE), 1) < HEAD_DIM
    keys, values = packed[:, WIDE : 2 * WIDE], packed[:, 2 * WIDE :]
    side = feature_k[...]
    ones = jnp.ones_like(values)
    key_a[...] = jnp.where(left, keys, side)
    key_b[...] = jnp.where(left, side, keys)
    value_a[...] = jnp.where(left, values, ones)
    value_b[...] = jnp.where(left, ones, values)
    left_q = lax.broadcasted_iota(jnp.int32, (rows, WIDE), 1) < HEAD_DIM

    def tile(index, carry):
        here = pl.ds(pl.multiple_of(index * rows, rows), rows)
        queries = packed[here, :WIDE] * jnp.asarray(HEAD_DIM**-0.5, LOW)
        side_q = feature_q[here, :]
        query_a = jnp.where(left_q, queries, side_q)
        query_b = jnp.where(left_q, side_q, queries)
        start = pl.multiple_of(ranges[index] * KEY_TILE, KEY_TILE)

        def over(width):
            def run():
                span = pl.ds(start, width)

                def head(query, key, value):
                    scores = matmul_right_t(query, key[span, :])
                    row_max = jnp.max(scores, axis=1, keepdims=True)
                    terms = jnp.exp(scores - row_max).astype(LOW)
                    return matmul(terms, value[span, :]), row_max

                out_a, max_a = head(query_a, key_a, value_a)
                out_b, max_b = head(query_b, key_b, value_b)
                totals = jnp.where(left_q, out_b, out_a)
                log_total[here, :] = jnp.where(left_q, max_b, max_a) + jnp.log(totals)
                inverse = pltpu.roll(1.0 / totals, HEAD_DIM, 1)
                context[here, :] = (jnp.where(left_q, out_a, out_b) * inverse).astype(LOW)

            return run

        lax.switch(
            ranges[tiles + index] - 1, [over(KEY_TILE * (n + 1)) for n in range(LEN // KEY_TILE)]
        )
        return carry

    lax.fori_loop(0, tiles, tile, 0)


def attention_forward(ranges, packed, feature_q, feature_k):
    whole = pl.BlockSpec((LEN, WIDE), lambda h, r: (0, 0))
    out = pl.BlockSpec((LEN, WIDE), lambda h, r: (0, h))
    return pl.pallas_call(
        attention_forward_body,
        out_shape=(jax.ShapeDtypeStruct((LEN, D), LOW), jax.ShapeDtypeStruct((LEN, D), F32)),
        grid_spec=pltpu.PrefetchScalarGridSpec(
            num_scalar_prefetch=1,
            grid=(PAIRS,),
            in_specs=[pl.BlockSpec((LEN, 3 * WIDE), lambda h, r: (0, h)), whole, whole],
            out_specs=[out, out],
            scratch_shapes=[pltpu.VMEM((LEN, WIDE), LOW)] * 4,
        ),
        name="attention_forward",
    )(ranges, packed, feature_q, feature_k)


def attention_backward_body(
    ranges,
    packed,
    context,
    d_context,
    log_total,
    feature_q,
    feature_k,
    d_packed,
    bias_sums,
    key_a,
    key_b,
    value_a,
    value_b,
    key_t,
    d_key,
    d_value,
):
    rows = BACKWARD_ROWS
    tiles = LEN // rows
    lane = lax.broadcasted_iota(jnp.int32, (LEN, WIDE), 1)
    left = lane < HEAD_DIM
    keys, values = packed[:, WIDE : 2 * WIDE], packed[:, 2 * WIDE :]
    side = feature_k[...]
    ones = jnp.where(lane % HEAD_DIM < 3, 1.0, 0.0).astype(LOW)
    key_a[...] = jnp.where(left, keys, side)
    key_b[...] = jnp.where(left, side, keys)
    value_a[...] = jnp.where(left, values, ones)
    value_b[...] = jnp.where(left, ones, values)
    key_t[...] = keys.T
    d_key[...] = jnp.zeros_like(d_key)
    d_value[...] = jnp.zeros_like(d_value)
    lane_q = lax.broadcasted_iota(jnp.int32, (rows, WIDE), 1)
    left_q = lane_q < HEAD_DIM
    inner = lane_q % HEAD_DIM
    zero = jnp.zeros((rows, WIDE), LOW)

    def spread(value, base):
        high = as_float(value.astype(LOW))
        rest = value - high
        middle = as_float(rest.astype(LOW))
        tail = rest - middle
        return jnp.where(
            inner == base,
            high,
            jnp.where(inner == base + 1, middle, jnp.where(inner == base + 2, tail, 0.0)),
        ).astype(LOW)

    def tile(index, sums):
        here = pl.ds(pl.multiple_of(index * rows, rows), rows)
        queries = packed[here, :WIDE] * jnp.asarray(HEAD_DIM**-0.5, LOW)
        side_q = feature_q[here, :] + spread(-log_total[here, :], 16)
        query_a = jnp.where(left_q, queries, side_q)
        query_b = jnp.where(left_q, side_q, queries)
        grad = d_context[here, :]
        product = as_float(grad) * as_float(context[here, :])
        dot_a = jnp.sum(jnp.where(left_q, product, 0.0), axis=1, keepdims=True)
        dot_b = jnp.sum(jnp.where(left_q, 0.0, product), axis=1, keepdims=True)
        side_g = spread(-jnp.where(left_q, dot_b, dot_a), 0)
        grad_a = jnp.where(left_q, grad, side_g)
        grad_b = jnp.where(left_q, side_g, grad)
        grad_both = jnp.concatenate(
            [jnp.where(left_q, grad, zero), jnp.where(left_q, zero, grad)], axis=0
        )
        query_both = jnp.concatenate(
            [jnp.where(left_q, queries, zero), jnp.where(left_q, zero, queries)], axis=0
        )
        start = pl.multiple_of(ranges[index] * KEY_TILE, KEY_TILE)

        def over(width):
            def run():
                span = pl.ds(start, width)

                def head(query, g, key, value):
                    probs = jnp.exp(matmul_right_t(key[span, :], query))
                    d_probs = matmul_right_t(value[span, :], g)
                    return probs.astype(LOW), (probs * d_probs).astype(LOW)

                probs_a, d_scores_a = head(query_a, grad_a, key_a, value_a)
                probs_b, d_scores_b = head(query_b, grad_b, key_b, value_b)
                d_value[span, :] += matmul(
                    jnp.concatenate([probs_a, probs_b], axis=1), grad_both
                )
                d_key[span, :] += matmul(
                    jnp.concatenate([d_scores_a, d_scores_b], axis=1), query_both
                )
                d_query_t = jnp.concatenate(
                    [
                        matmul(key_t[:HEAD_DIM, span], d_scores_a),
                        matmul(key_t[HEAD_DIM:, span], d_scores_b),
                    ],
                    axis=0,
                )
                d_packed[here, :WIDE] = (d_query_t.T * HEAD_DIM**-0.5).astype(LOW)

            return run

        lax.switch(
            ranges[tiles + index] - 1, [over(KEY_TILE * (n + 1)) for n in range(LEN // KEY_TILE)]
        )
        return sums + jnp.sum(as_float(d_packed[here, :WIDE]), axis=0, keepdims=True)

    sums = lax.fori_loop(0, tiles, tile, jnp.zeros((1, WIDE), F32))
    d_value_low = d_value[...].astype(LOW)
    d_packed[:, WIDE : 2 * WIDE] = d_key[...].astype(LOW)
    d_packed[:, 2 * WIDE :] = d_value_low
    bias_sums[0:1, :] = sums
    bias_sums[1:2, :] = jnp.sum(as_float(d_value_low), axis=0, keepdims=True)


def attention_backward(ranges, packed, context, d_context, log_total, feature_q, feature_k, pairs):
    whole = pl.BlockSpec((LEN, WIDE), lambda h, r: (0, 0))
    last = ranges.shape[0] - 1

    def column(width):
        return pl.BlockSpec((LEN, width), lambda h, r: (0, r[last] + h))

    return pl.pallas_call(
        attention_backward_body,
        out_shape=(
            jax.ShapeDtypeStruct((LEN, pairs * 3 * WIDE), LOW),
            jax.ShapeDtypeStruct((2, pairs * WIDE), F32),
        ),
        grid_spec=pltpu.PrefetchScalarGridSpec(
            num_scalar_prefetch=1,
            grid=(pairs,),
            in_specs=[column(3 * WIDE), column(WIDE), column(WIDE), column(WIDE), whole, whole],
            out_specs=[
                pl.BlockSpec((LEN, 3 * WIDE), lambda h, r: (0, h)),
                pl.BlockSpec((2, WIDE), lambda h, r: (0, h)),
            ],
            scratch_shapes=[pltpu.VMEM((LEN, WIDE), LOW)] * 4
            + [pltpu.VMEM((WIDE, LEN), LOW)]
            + [pltpu.VMEM((LEN, WIDE), F32)] * 2,
        ),
        name="attention_backward",
    )(ranges, packed, context, d_context, log_total, feature_q, feature_k)


class Place:
    def __init__(self, replicas, shards):
        self.replicas, self.shards = replicas, shards
        replica = lax.axis_index("replica")
        self.core = replica % 2
        self.x = replica // 2 % 2
        self.z = replica // 4
        self.depth = replicas // 4
        self.y = lax.axis_index("shard")


def swap(value, axis, size, mask):
    return lax.ppermute(value, axis, [(i, i ^ mask) for i in range(size)])


def pick(options, index):
    chosen = options[-1]
    for at in range(len(options) - 2, -1, -1):
        chosen = jnp.where(index == at, options[at], chosen)
    return chosen


def rows_of(value, block, size):
    return lax.dynamic_slice_in_dim(value, block * size, size, 0)


def gather_shards(pieces, at):
    found = {0: pieces}
    mask = 1
    while mask < at.shards:
        for d in range(mask):
            found[d | mask] = swap(found[d], "shard", at.shards, mask)
        mask *= 2
    return [found[d] for d in range(at.shards)]


def gather_weight(weight, at):
    half = weight.shape[0] // 2
    found = gather_shards(rows_of(weight, at.core, half), at)
    whole = [weight]
    for d in range(1, at.shards):
        other = swap(found[d], "replica", at.replicas, 1)
        whole.append(
            jnp.concatenate([pick([found[d], other], at.core), pick([other, found[d]], at.core)])
        )
    return jnp.concatenate([pick(whole, at.y ^ j) for j in range(at.shards)])


def reduce_shards(parts, at):
    mask = at.shards // 2
    while mask:
        parts = [
            (as_float(parts[d]) + as_float(swap(parts[d | mask], "shard", at.shards, mask))).astype(
                parts[d].dtype
            )
            for d in range(mask)
        ]
        mask //= 2
    return parts[0]


def reduce_gradient(send, keep, at):
    m = keep.shape[0] // at.shards
    got = swap(send, "replica", at.replicas, 1)
    parts = []
    for d in range(at.shards):
        block = at.y ^ d
        parts.append((as_float(rows_of(keep, block, m)) + as_float(rows_of(got, block, m))).astype(LOW))
    mine = reduce_shards(parts, at)
    half = m // 2
    got = swap(rows_of(mine, 1 - at.x, half), "replica", at.replicas, 2)
    mine = (as_float(rows_of(mine, at.x, half)) + as_float(got)).astype(LOW)
    piece = half // at.depth
    total = as_float(rows_of(mine, at.z, piece))
    for d in range(1, at.depth):
        total += as_float(
            swap(rows_of(mine, at.z ^ d, piece), "replica", at.replicas, 4 * d)
        )
    total = total.astype(LOW)
    found = [total] + [swap(total, "replica", at.replicas, 4 * d) for d in range(1, at.depth)]
    mine = jnp.concatenate([pick(found, at.z ^ j) for j in range(at.depth)])
    other = swap(mine, "replica", at.replicas, 2)
    mine_core = swap(mine, "replica", at.replicas, 1)
    other_core = swap(other, "replica", at.replicas, 1)
    own = jnp.concatenate([pick([mine, other], at.x), pick([other, mine], at.x)])
    partner = jnp.concatenate(
        [pick([mine_core, other_core], at.x), pick([other_core, mine_core], at.x)]
    )
    return as_float(pick([own, partner], at.core)), as_float(pick([partner, own], at.core))


def reduce_small(values, at):
    mine = reduce_shards([lax.dynamic_index_in_dim(values, at.y ^ d, 0, False) for d in range(at.shards)], at)
    mask = 1
    while mask < at.replicas:
        mine = mine + swap(mine, "replica", at.replicas, mask)
        mask *= 2
    return mine


def halves(left, right, at, columns):
    half = columns // 2
    return tuple(
        matmul_left_t(left, lax.dynamic_slice_in_dim(right, block * half, half, 1))
        for block in (1 - at.core, at.core)
    )


def pair_major(matrix):
    lead = matrix.shape[:-1]
    parts = matrix.reshape(lead + (3, PAIRS, WIDE))
    return jnp.swapaxes(parts, -3, -2).reshape(lead + (3 * D,))


def local(
    replicas,
    shards,
    inputs,
    segments,
    w_qkv,
    b_qv,
    w_out,
    b_out,
    attn_gain,
    attn_shift,
    w_up,
    b_up,
    w_down,
    b_down,
    ffn_gain,
    ffn_shift,
    cotangent,
):
    at = Place(replicas, shards)
    segments = segments.reshape(LEN)
    feature_q, feature_k = document_features(segments)

    vectors = (b_qv, b_out, attn_gain, attn_shift, b_up, b_down, ffn_gain, ffn_shift)
    sizes = [v.shape[0] for v in vectors]
    small = gather_shards(jnp.concatenate(vectors), at)
    small = as_float(jnp.stack([pick(small, at.y ^ j) for j in range(shards)]))
    full, offset = [], 0
    for size in sizes:
        full.append(small[:, offset : offset + size].reshape(-1))
        offset += size
    full_bqv, full_bout, full_again, full_ashift, full_bup, full_bdown, full_fgain, full_fshift = full

    full_qkv = pair_major(gather_weight(w_qkv, at))
    qkv_bias = pair_major(jnp.concatenate([full_bqv[:D], jnp.zeros((D,), F32), full_bqv[D:]]))
    full_wout = gather_weight(w_out, at)
    full_wup = gather_weight(w_up, at)
    full_wdown = gather_weight(w_down, at)

    projected = (matmul(inputs, full_qkv) + qkv_bias).astype(LOW)
    context, log_total = attention_forward(
        key_ranges(segments, FORWARD_ROWS), projected, feature_q, feature_k
    )
    attended = matmul(context, full_wout) + full_bout
    residual_one = as_float(inputs) + attended
    normed_one, norm_one_pull = jax.vjp(layer_norm, residual_one, full_again, full_ashift)
    normed_low = normed_one.astype(LOW)
    up_proj = matmul(normed_low, full_wup) + full_bup
    activated_float, gelu_pull = jax.vjp(gelu_exact, up_proj)
    activated = activated_float.astype(LOW)
    down_proj = matmul(activated, full_wdown) + full_bdown
    residual_two = normed_one + down_proj
    output_float, norm_two_pull = jax.vjp(layer_norm, residual_two, full_fgain, full_fshift)
    layer_output = output_float.astype(LOW)

    d_sum_two, grad_ffn_gain, grad_ffn_shift = norm_two_pull(as_float(cotangent))
    d_down = d_sum_two.astype(LOW)
    down_send, down_keep = halves(activated, d_down, at, D)
    grad_w_down = reduce_gradient(down_send.astype(LOW), down_keep, at)
    grad_b_down = jnp.sum(d_down, axis=0, dtype=F32)
    d_activated = matmul_right_t(d_down, full_wdown)
    d_up = gelu_pull(d_activated)[0].astype(LOW)
    up_send, up_keep = halves(normed_low, d_up, at, 4 * D)
    grad_w_up = reduce_gradient(up_send.astype(LOW), up_keep, at)
    grad_b_up = jnp.sum(d_up, axis=0, dtype=F32)
    d_normed_one = d_sum_two + matmul_right_t(d_up, full_wup)
    d_sum_one, grad_attn_gain, grad_attn_shift = norm_one_pull(d_normed_one)
    d_attended = d_sum_one.astype(LOW)
    out_send, out_keep = halves(context, d_attended, at, D)
    grad_w_out = reduce_gradient(out_send.astype(LOW), out_keep, at)
    grad_b_out = jnp.sum(d_attended, axis=0, dtype=F32)
    d_context = matmul_right_t(d_attended, full_wout).astype(LOW)

    ranges = key_ranges(segments, BACKWARD_ROWS)
    pairs = PAIRS // 2
    input_grad = d_sum_one
    shares, sums = [], []
    for block in (1 - at.core, at.core):
        d_packed, bias_sums = attention_backward(
            jnp.concatenate([ranges, (block * pairs).reshape(1)]),
            projected,
            context,
            d_context,
            log_total,
            feature_q,
            feature_k,
            pairs,
        )
        shares.append(matmul_left_t(inputs, d_packed))
        sums.append(bias_sums)
        half = lax.dynamic_slice_in_dim(full_qkv, block * pairs * 3 * WIDE, pairs * 3 * WIDE, 1)
        input_grad = input_grad + matmul_right_t(d_packed, half)
    input_grad = input_grad.astype(LOW)
    grad_qkv = reduce_gradient(shares[0].astype(LOW), shares[1], at)
    grad_qkv = jnp.concatenate(grad_qkv, axis=1)
    grad_qkv = jnp.swapaxes(grad_qkv.reshape(-1, PAIRS, 3, WIDE), 1, 2).reshape(-1, 3 * D)
    sums = pick(
        [jnp.concatenate(sums[::-1], axis=1), jnp.concatenate(sums, axis=1)], at.core
    )

    grads = (
        sums.reshape(-1),
        grad_b_out,
        grad_attn_gain,
        grad_attn_shift,
        grad_b_up,
        grad_b_down,
        grad_ffn_gain,
        grad_ffn_shift,
    )
    packed = jnp.concatenate([g.reshape(shards, -1) for g in grads], axis=1)
    packed = reduce_small(packed.reshape(shards, -1, 128), at).reshape(-1)
    owned, offset = [], 0
    for size in sizes:
        owned.append(packed[offset : offset + size])
        offset += size
    return (
        layer_output,
        input_grad,
        grad_qkv,
        owned[0],
        jnp.concatenate(grad_w_out, axis=1),
        owned[1],
        owned[2],
        owned[3],
        jnp.concatenate(grad_w_up, axis=1),
        owned[4],
        jnp.concatenate(grad_w_down, axis=1),
        owned[5],
        owned[6],
        owned[7],
    )


def solution(mesh):
    tokens, matrix, vector = P(("replica", "shard"), None), P("shard", None), P("shard")
    weights = (matrix, vector, matrix, vector, vector, vector)
    weights += (matrix, vector, matrix, vector, vector, vector)
    return jax.shard_map(
        functools.partial(local, mesh.shape["replica"], mesh.shape["shard"]),
        mesh=mesh,
        in_specs=(tokens, tokens) + weights + (tokens,),
        out_specs=(tokens, tokens) + weights,
        check_vma=False,
    )
```

```python
import functools

import jax
import jax.numpy as jnp
from jax import lax
from jax.experimental import pallas as pl
from jax.experimental.pallas import tpu as pltpu
from jax.sharding import PartitionSpec as P

D = 768
FF = 3072
HEADS = 12
HEAD_DIM = 64
LEN = 1024
PAIRS = HEADS // 2
HALF_PAIRS = PAIRS // 2
WIDE = 2 * HEAD_DIM
TRIPLE = 3 * WIDE
KEY_TILE = 128
FORWARD_ROWS = 128
BACKWARD_ROWS = 256
TOKEN_ROWS = 256
CHUNK = 384
BIG = float(2**30)
EPSILON = 1e-12
F32 = jnp.float32
LOW = jnp.bfloat16
B_QV, B_OUT, ATTN_GAIN, ATTN_SHIFT = 0, 2 * D, 3 * D, 4 * D
B_UP, B_DOWN, FFN_GAIN, FFN_SHIFT = 5 * D, 5 * D + FF, 6 * D + FF, 7 * D + FF
VECTORS = 8 * D + FF
CORE, X, Z, Y = 0, 1, 2, 3


def matmul(left, right):
    return jnp.dot(left, right, preferred_element_type=F32)


def matmul_right_t(left, right):
    return lax.dot_general(left, right, (((1,), (1,)), ((), ())), preferred_element_type=F32)


def matmul_left_t(left, right):
    return lax.dot_general(left, right, (((0,), (0,)), ((), ())), preferred_element_type=F32)


def as_float(value):
    return value.astype(F32)


def rounded(value):
    return value.astype(LOW)


def shape(dims, kind=LOW):
    return jax.ShapeDtypeStruct(dims, kind)


def constant(dims):
    return pl.BlockSpec(dims, lambda *at: (0,) * len(dims))


def tokens(width):
    return pl.BlockSpec((TOKEN_ROWS, width), lambda i, *place: (i, 0))


ANYWHERE = pl.BlockSpec(memory_space=pl.ANY)


def call(body, name, out_shape, grid, in_specs, out_specs, scratch=(), flops=0, exps=0):
    return pl.pallas_call(
        body,
        out_shape=out_shape,
        grid_spec=pltpu.PrefetchScalarGridSpec(
            num_scalar_prefetch=1,
            grid=grid,
            in_specs=in_specs,
            out_specs=out_specs,
            scratch_shapes=list(scratch),
        ),
        cost_estimate=pl.CostEstimate(flops=flops, transcendentals=exps, bytes_accessed=1 << 20),
        name=name,
    )


def piece_rows(place, count, own_rows):
    half = own_rows // 2
    core, y = place[CORE], place[Y]
    found = [pl.multiple_of(y * own_rows, half)]
    for d in range(1, (count + 1) // 2):
        base = jnp.bitwise_xor(y, d) * own_rows
        found.append(pl.multiple_of(base + core * half, half))
        found.append(pl.multiple_of(base + (1 - core) * half, half))
    return found


def assemble(place, pieces, buffer, semaphores):
    starts = piece_rows(place, len(pieces), pieces[0].shape[0])
    return [
        pltpu.make_async_copy(
            piece, buffer.at[pl.ds(start, piece.shape[0]), :], semaphores.at[at]
        )
        for at, (piece, start) in enumerate(zip(pieces, starts))
    ]


def start_all(copies):
    for copy in copies:
        copy.start()


def wait_all(copies):
    for copy in copies:
        copy.wait()


def project_body(place, inputs, vectors, *refs):
    pieces, (projected, weight) = refs[:-2], refs[-2:]
    count = len(pieces) // 3
    starts = piece_rows(place, count, pieces[0].shape[0])
    for part in range(3):
        for at in range(count):
            block = pieces[part * count + at]
            rows = pl.ds(starts[at], block.shape[0])
            for j in range(2):
                lanes = slice(j * TRIPLE + part * WIDE, j * TRIPLE + (part + 1) * WIDE)
                weight[rows, lanes] = block[:, j * WIDE : (j + 1) * WIDE]
    first = pl.program_id(0) * 2 * WIDE
    bias = []
    for j in range(2):
        at = pl.multiple_of(first + j * WIDE, WIDE)
        bias.append(vectors[:, pl.ds(B_QV + at, WIDE)])
        bias.append(jnp.zeros((1, WIDE), F32))
        bias.append(vectors[:, pl.ds(B_QV + D + at, WIDE)])
    bias = jnp.concatenate(bias, axis=1)
    projected[...] = rounded(matmul(inputs[...], weight[...]) + bias)


def project(place, inputs, vectors, pieces):
    steps = PAIRS // 2
    column = pl.BlockSpec((LEN, 2 * TRIPLE), lambda i, p: (0, i))
    specs, operands = [], []
    for part in range(3):
        for piece in pieces:
            specs.append(
                pl.BlockSpec(
                    (piece.shape[0], 2 * WIDE), lambda i, p, part=part: (0, part * steps + i)
                )
            )
            operands.append(piece)
    return call(
        project_body,
        "project",
        (shape((LEN, 3 * D)), shape((D, 3 * D))),
        (steps,),
        [constant((LEN, D)), constant((1, VECTORS))] + specs,
        [column, pl.BlockSpec((D, 2 * TRIPLE), lambda i, p: (0, i))],
        flops=2 * LEN * D * 3 * D,
    )(place, inputs, vectors, *operands)


def key_ranges(segments, rows):
    tiles = segments.reshape(LEN // rows, rows)
    below = jnp.sum(segments[None, :] < tiles[:, :1], axis=1, dtype=jnp.int32)
    upto = jnp.sum(segments[None, :] <= tiles[:, -1:], axis=1, dtype=jnp.int32)
    start = below // KEY_TILE
    count = (upto + KEY_TILE - 1) // KEY_TILE - start
    return jnp.concatenate([start, count])
def document_features(segments):
    lane = jnp.arange(WIDE, dtype=jnp.int32) % HEAD_DIM
    hot = segments[:, None] == lane[None, :]
    q = jnp.where((lane < 16) & hot, 1.0, 0.0).astype(LOW)
    k = jnp.where(lane < 16, jnp.where(hot, 0.0, -BIG), jnp.where(lane < 19, 1.0, 0.0)).astype(LOW)
    return q,k
def stack_heads(pair, side_a, side_b, left):
    zero=jnp.zeros_like(pair)
    a=jnp.concatenate([jnp.where(left,pair,zero),side_a],axis=1)
    b=jnp.concatenate([jnp.where(left,zero,pair),side_b],axis=1)
    return jnp.concatenate([a,b],axis=0)


def fwd_body(ranges, packed, feature_q, feature_k, context, log_total, key_side, value_t, *, group):
    tiles=LEN//FORWARD_ROWS
    for g in range(group):
        at=3*WIDE*g
        key_side[g,:,:WIDE]=packed[:,at+WIDE:at+2*WIDE]
        key_side[g,:,WIDE:]=feature_k[...]
        value_t[g,:WIDE,:]=packed[:,at+2*WIDE:at+3*WIDE].T
        value_t[g,WIDE:,:]=jnp.ones((16,LEN),LOW)
    left=lax.broadcasted_iota(jnp.int32,(FORWARD_ROWS,WIDE),1)<HEAD_DIM
    def tile(index,carry):
        here=pl.ds(pl.multiple_of(index*FORWARD_ROWS,FORWARD_ROWS),FORWARD_ROWS)
        side=feature_q[here,:]
        zero=jnp.zeros_like(side)
        sa=jnp.where(left,side,zero); sb=jnp.where(left,zero,side)
        stats=[stack_heads(packed[here,3*WIDE*g:3*WIDE*g+WIDE]*jnp.asarray(HEAD_DIM**-0.5,LOW),sa,sb,left) for g in range(group)]
        start=pl.multiple_of(ranges[index]*KEY_TILE,KEY_TILE)
        def over(width):
            def run():
                span=pl.ds(start,width)
                ss=[matmul_right_t(key_side[g,span,:],stats[g]) for g in range(group)]
                for g in range(group):
                    s=ss[g]
                    m=jnp.max(s,axis=0,keepdims=True)
                    p=jnp.exp(s-m).astype(LOW)
                    o=matmul(value_t[g,:,span],p)
                    total=o[WIDE:WIDE+1,:]
                    inv=1.0/total
                    lse=m+jnp.log(total)
                    log_total[g,0:1,here]=lse[:,:FORWARD_ROWS]
                    log_total[g,1:2,here]=lse[:,FORWARD_ROWS:]
                    both=jnp.concatenate([o[:HEAD_DIM,:FORWARD_ROWS]*inv[:,:FORWARD_ROWS],o[HEAD_DIM:WIDE,FORWARD_ROWS:]*inv[:,FORWARD_ROWS:]],axis=0)
                    context[here,g*WIDE:(g+1)*WIDE]=both.T.astype(LOW)
            return run
        lax.switch(ranges[tiles+index]-1,[over(KEY_TILE*(n+1)) for n in range(LEN//KEY_TILE)])
        return carry
    lax.fori_loop(0,tiles,tile,0)

def attn_fwd(r,packed,fq,fk,group=2):
    whole=pl.BlockSpec((LEN,WIDE),lambda h,r:(0,0))
    return pl.pallas_call(lambda *a: fwd_body(*a,group=group),
        out_shape=(jax.ShapeDtypeStruct((LEN,D),LOW),jax.ShapeDtypeStruct((PAIRS,2,LEN),F32)),
        grid_spec=pltpu.PrefetchScalarGridSpec(num_scalar_prefetch=1,grid=(PAIRS//group,),
          in_specs=[pl.BlockSpec((LEN,3*WIDE*group),lambda h,r:(0,h)),whole,whole],
          out_specs=[pl.BlockSpec((LEN,WIDE*group),lambda h,r:(0,h)),pl.BlockSpec((group,2,LEN),lambda h,r:(h,0,0))],
          scratch_shapes=[pltpu.VMEM((group,LEN,2*WIDE),LOW),pltpu.VMEM((group,WIDE+16,LEN),LOW)]),
        name="attention_forward")(r,packed,fq,fk)

def bwd_body(ranges,packed,context,d_context,log_total,feature_q,feature_k,d_packed,bias_sums,key_side,value_side,key_t,d_key,d_value,*,group):
    tiles=LEN//BACKWARD_ROWS
    lane=lax.broadcasted_iota(jnp.int32,(LEN,WIDE),1)
    ones=jnp.where(lane%HEAD_DIM<3,1.0,0.0).astype(LOW)
    for g in range(group):
        at=3*WIDE*g
        keys=packed[:,at+WIDE:at+2*WIDE]
        key_side[g,:,:WIDE]=keys
        key_side[g,:,WIDE:]=feature_k[...]
        value_side[g,:,:WIDE]=packed[:,at+2*WIDE:at+3*WIDE]
        value_side[g,:,WIDE:]=ones
        key_t[g]=keys.T
    d_key[...]=jnp.zeros_like(d_key); d_value[...]=jnp.zeros_like(d_value)
    lane_q=lax.broadcasted_iota(jnp.int32,(BACKWARD_ROWS,WIDE),1)
    left=lane_q<HEAD_DIM; inner=lane_q%HEAD_DIM
    zero=jnp.zeros((BACKWARD_ROWS,WIDE),LOW)
    def spread(value,base):
        high=as_float(value.astype(LOW)); rest=value-high
        middle=as_float(rest.astype(LOW)); tail=rest-middle
        return jnp.where(inner==base,high,jnp.where(inner==base+1,middle,jnp.where(inner==base+2,tail,0.0))).astype(LOW)
    def tile(index,sums):
        here=pl.ds(pl.multiple_of(index*BACKWARD_ROWS,BACKWARD_ROWS),BACKWARD_ROWS)
        hot=feature_q[here,:]
        qs=[];gs=[]
        for g in range(group):
            queries=packed[here,3*WIDE*g:3*WIDE*g+WIDE]*jnp.asarray(HEAD_DIM**-0.5,LOW)
            logs=log_total[g,:,here]
            cols=jnp.concatenate([logs,jnp.zeros((6,BACKWARD_ROWS),F32)],axis=0).T
            lse=jnp.where(left,cols[:,0:1],cols[:,1:2])
            side=hot+spread(-lse,16)
            qs.append(stack_heads(queries,jnp.where(left,side,zero),jnp.where(left,zero,side),left))
            grad=d_context[here,g*WIDE:(g+1)*WIDE]
            product=as_float(grad)*as_float(context[here,g*WIDE:(g+1)*WIDE])
            dot_a=jnp.sum(jnp.where(left,product,0.0),axis=1,keepdims=True)
            dot_b=jnp.sum(jnp.where(left,0.0,product),axis=1,keepdims=True)
            side_g=spread(-jnp.where(left,dot_a,dot_b),0)
            gs.append(stack_heads(grad,jnp.where(left,side_g,zero),jnp.where(left,zero,side_g),left))
        start=pl.multiple_of(ranges[index]*KEY_TILE,KEY_TILE)
        def over(width):
            def run():
                span=pl.ds(start,width)
                for g in range(group):
                    p=jnp.exp(matmul_right_t(key_side[g,span,:],qs[g]))
                    dp=matmul_right_t(value_side[g,span,:],gs[g])
                    pb=p.astype(LOW); ds=(p*dp).astype(LOW)
                    d_value[g,span,:]+=matmul(pb,gs[g][:,:WIDE])
                    d_key[g,span,:]+=matmul(ds,qs[g][:,:WIDE])
                    dq=matmul(key_t[g,:,span],ds)
                    dq=jnp.concatenate([dq[:HEAD_DIM,:BACKWARD_ROWS],dq[HEAD_DIM:,BACKWARD_ROWS:]],axis=0)
                    d_packed[here,3*WIDE*g:3*WIDE*g+WIDE]=(dq.T*HEAD_DIM**-0.5).astype(LOW)
            return run
        lax.switch(ranges[tiles+index]-1,[over(KEY_TILE*(n+1)) for n in range(LEN//KEY_TILE)])
        return tuple(sums[g]+jnp.sum(as_float(d_packed[here,3*WIDE*g:3*WIDE*g+WIDE]),axis=0,keepdims=True) for g in range(group))
    sums=lax.fori_loop(0,tiles,tile,(jnp.zeros((1,WIDE),F32),)*group)
    for g in range(group):
        at=3*WIDE*g
        low=d_value[g].astype(LOW)
        d_packed[:,at+WIDE:at+2*WIDE]=d_key[g].astype(LOW)
        d_packed[:,at+2*WIDE:at+3*WIDE]=low
        bias_sums[0:1,g*WIDE:(g+1)*WIDE]=sums[g]
        bias_sums[1:2,g*WIDE:(g+1)*WIDE]=jnp.sum(as_float(low),axis=0,keepdims=True)

def attn_bwd(r,packed,ctx,dctx,lse,fq,fk,pairs,group=2):
    whole=pl.BlockSpec((LEN,WIDE),lambda h,r:(0,0))
    last=r.shape[0]-1
    col=lambda w: pl.BlockSpec((LEN,w*group),lambda h,r:(0,r[last]+h))
    return pl.pallas_call(lambda *a: bwd_body(*a,group=group),
        out_shape=(jax.ShapeDtypeStruct((LEN,pairs*3*WIDE),LOW),jax.ShapeDtypeStruct((2,pairs*WIDE),F32)),
        grid_spec=pltpu.PrefetchScalarGridSpec(num_scalar_prefetch=1,grid=(pairs//group,),
          in_specs=[col(3*WIDE),col(WIDE),col(WIDE),pl.BlockSpec((group,2,LEN),lambda h,r:(r[last]+h,0,0)),whole,whole],
          out_specs=[pl.BlockSpec((LEN,3*WIDE*group),lambda h,r:(0,h)),pl.BlockSpec((2,WIDE*group),lambda h,r:(0,h))],
          scratch_shapes=[pltpu.VMEM((group,LEN,2*WIDE),LOW)]*2+[pltpu.VMEM((group,WIDE,LEN),LOW)]+[pltpu.VMEM((group,LEN,WIDE),F32)]*2),
        name="attention_backward")(r,packed,ctx,dctx,lse,fq,fk)


def normalize(hidden):
    average = jnp.mean(hidden, axis=-1, keepdims=True)
    centered = hidden - average
    variance = jnp.mean(centered * centered, axis=-1, keepdims=True)
    inverse = lax.rsqrt(variance + EPSILON)
    return centered * inverse, inverse


def normalize_back(grad, normal, inverse):
    first = jnp.mean(grad, axis=-1, keepdims=True)
    second = jnp.mean(grad * normal, axis=-1, keepdims=True)
    return (grad - first - normal * second) * inverse


def column_sum(value):
    return jnp.sum(value, axis=0, keepdims=True)


def up_body(place, context, inputs, vectors, *refs):
    count = (len(refs) - 9) // 2
    out_pieces, up_pieces = refs[:count], refs[count : 2 * count]
    normal, inverse, low, activated, slope, w_out, w_up, out_sem, up_sem = refs[2 * count :]
    out_copies = assemble(place, out_pieces, w_out, out_sem)
    up_copies = assemble(place, up_pieces, w_up, up_sem)
    step = pl.program_id(0)

    @pl.when(step == 0)
    def _():
        start_all(out_copies)
        start_all(up_copies)
        wait_all(out_copies)

    attended = matmul(context[...], w_out[...]) + vectors[:, B_OUT : B_OUT + D]
    value, scale = normalize(as_float(inputs[...]) + attended)
    normal[...] = value
    inverse[...] = jnp.broadcast_to(scale, inverse.shape)
    normed = rounded(
        value * vectors[:, ATTN_GAIN : ATTN_GAIN + D] + vectors[:, ATTN_SHIFT : ATTN_SHIFT + D]
    )
    low[...] = normed

    @pl.when(step == 0)
    def _():
        wait_all(up_copies)

    for at in range(0, FF, D):
        up = matmul(normed, w_up[:, at : at + D]) + vectors[:, B_UP + at : B_UP + at + D]
        below = 0.5 + 0.5 * lax.erf(up * (0.5**0.5))
        density = jnp.exp(-0.5 * up * up) * 0.3989422804014327
        activated[:, at : at + D] = rounded(up * below)
        slope[:, at : at + D] = rounded(below + up * density)


def up_block(place, context, inputs, vectors, out_pieces, up_pieces):
    count = len(out_pieces)
    return call(
        up_body,
        "out_norm_up",
        (
            shape((LEN, D), F32),
            shape((LEN, WIDE), F32),
            shape((LEN, D)),
            shape((LEN, FF)),
            shape((LEN, FF)),
        ),
        (LEN // TOKEN_ROWS,),
        [tokens(D), tokens(D), constant((1, VECTORS))] + [ANYWHERE] * (2 * count),
        [tokens(D), tokens(WIDE), tokens(D), tokens(FF), tokens(FF)],
        [
            pltpu.VMEM((D, D), LOW),
            pltpu.VMEM((D, FF), LOW),
            pltpu.SemaphoreType.DMA((count,)),
            pltpu.SemaphoreType.DMA((count,)),
        ],
        flops=2 * LEN * D * (D + FF),
        exps=2 * LEN * FF,
    )(place, context, inputs, vectors, *out_pieces, *up_pieces)


def down_body(place, activated, slope, normal, cotangent, vectors, *refs):
    count = len(refs) - 7
    pieces = refs[:count]
    output, d_sum, d_down, d_up, sums, w_down, sem = refs[count:]
    copies = assemble(place, pieces, w_down, sem)
    step = pl.program_id(0)

    @pl.when(step == 0)
    def _():
        start_all(copies)
        sums[...] = jnp.zeros_like(sums)
        wait_all(copies)

    down = matmul(activated[...], w_down[...]) + vectors[:, B_DOWN : B_DOWN + D]
    gain = vectors[:, ATTN_GAIN : ATTN_GAIN + D]
    normed = normal[...] * gain + vectors[:, ATTN_SHIFT : ATTN_SHIFT + D]
    value, scale = normalize(normed + down)
    gain = vectors[:, FFN_GAIN : FFN_GAIN + D]
    output[...] = rounded(value * gain + vectors[:, FFN_SHIFT : FFN_SHIFT + D])
    grad = as_float(cotangent[...])
    sums[:, :D] += column_sum(grad * value)
    sums[:, D : 2 * D] += column_sum(grad)
    d_two = normalize_back(grad * gain, value, scale)
    d_sum[...] = d_two
    d_low = rounded(d_two)
    d_down[...] = d_low
    sums[:, 2 * D : 3 * D] += column_sum(as_float(d_low))
    for at in range(0, FF, D):
        d_activated = matmul_right_t(d_low, w_down[at : at + D, :])
        part = rounded(d_activated * as_float(slope[:, at : at + D]))
        d_up[:, at : at + D] = part
        sums[:, 3 * D + at : 4 * D + at] += column_sum(as_float(part))


def down_block(place, activated, slope, normal, cotangent, vectors, pieces):
    count = len(pieces)
    return call(
        down_body,
        "down_norm_back",
        (
            shape((LEN, D)),
            shape((LEN, D), F32),
            shape((LEN, D)),
            shape((LEN, FF)),
            shape((1, 3 * D + FF), F32),
        ),
        (LEN // TOKEN_ROWS,),
        [tokens(FF), tokens(FF), tokens(D), tokens(D), constant((1, VECTORS))]
        + [ANYWHERE] * count,
        [tokens(D), tokens(D), tokens(D), tokens(FF), constant((1, 3 * D + FF))],
        [pltpu.VMEM((FF, D), LOW), pltpu.SemaphoreType.DMA((count,))],
        flops=4 * LEN * D * FF,
    )(place, activated, slope, normal, cotangent, vectors, *pieces)


def back_body(place, d_up, d_sum_two, normal, inverse, vectors, *refs):
    count = (len(refs) - 8) // 2
    up_pieces, out_pieces = refs[:count], refs[count : 2 * count]
    d_sum, d_attended, d_context, sums, w_up, w_out, up_sem, out_sem = refs[2 * count :]
    up_copies = assemble(place, up_pieces, w_up, up_sem)
    out_copies = assemble(place, out_pieces, w_out, out_sem)
    step = pl.program_id(0)

    @pl.when(step == 0)
    def _():
        start_all(up_copies)
        start_all(out_copies)
        sums[...] = jnp.zeros_like(sums)
        wait_all(up_copies)
        wait_all(out_copies)

    d_normed = d_sum_two[...] + matmul_right_t(d_up[...], w_up[...])
    value = normal[...]
    sums[:, :D] += column_sum(d_normed * value)
    sums[:, D : 2 * D] += column_sum(d_normed)
    d_one = normalize_back(
        d_normed * vectors[:, ATTN_GAIN : ATTN_GAIN + D], value, inverse[:, :1]
    )
    d_sum[...] = d_one
    low = rounded(d_one)
    d_attended[...] = low
    sums[:, 2 * D :] += column_sum(as_float(low))
    d_context[...] = rounded(matmul_right_t(low, w_out[...]))


def back_block(place, d_up, d_sum_two, normal, inverse, vectors, up_pieces, out_pieces):
    count = len(up_pieces)
    return call(
        back_body,
        "norm_back",
        (shape((LEN, D), F32), shape((LEN, D)), shape((LEN, D)), shape((1, 3 * D), F32)),
        (LEN // TOKEN_ROWS,),
        [tokens(FF), tokens(D), tokens(D), tokens(WIDE), constant((1, VECTORS))]
        + [ANYWHERE] * (2 * count),
        [tokens(D), tokens(D), tokens(D), constant((1, 3 * D))],
        [
            pltpu.VMEM((D, FF), LOW),
            pltpu.VMEM((D, D), LOW),
            pltpu.SemaphoreType.DMA((count,)),
            pltpu.SemaphoreType.DMA((count,)),
        ],
        flops=2 * LEN * D * (FF + D),
    )(place, d_up, d_sum_two, normal, inverse, vectors, *up_pieces, *out_pieces)


def input_body(place, weight, d_sum, *refs, spans):
    output, pieces = refs[-1], refs[:-1]
    total = d_sum[...]
    for piece, (partner, first, count) in zip(pieces, spans):
        block = 1 - place[CORE] if partner else place[CORE]
        at = pl.multiple_of((block * HALF_PAIRS + first) * TRIPLE, WIDE)
        total += matmul_right_t(piece[...], weight[:, pl.ds(at, count * TRIPLE)])
    output[...] = rounded(total)


def input_gradient(place, weight, d_sum, pieces, spans):
    return call(
        functools.partial(input_body, spans=spans),
        "input_gradient",
        shape((LEN, D)),
        (LEN // TOKEN_ROWS,),
        [constant((D, 3 * D)), tokens(D)] + [tokens(piece.shape[1]) for piece in pieces],
        tokens(D),
        flops=6 * LEN * D * D,
    )(place, weight, d_sum, *pieces)


def shard_row(place, d, rows):
    return pl.multiple_of(jnp.bitwise_xor(place[Y], d) * rows, rows)


def gradient_specs(shards, rows, block, got, index):
    if got is None:
        return shape((shards, rows, CHUNK)), pl.BlockSpec((shards, block, CHUNK), index), []
    one = pl.BlockSpec((block, CHUNK), lambda *at: index(*at)[1:])
    return (
        (shape((rows, CHUNK)),) * shards,
        [one] * shards,
        [pl.BlockSpec((shards, block, CHUNK), index)],
    )


def down_gradient_body(place, left, right, *refs, shards, adds):
    value = matmul_left_t(left[...], right[...])
    if not adds:
        refs[0][0] = rounded(value)
        return
    got, outs = refs[0], refs[1:]
    value = rounded(value + as_float(got[0]))
    for at in range(shards):

        @pl.when(pl.program_id(0) == shards - 1 - at)
        def _(at=at):
            outs[at][...] = value


def down_gradient(place, activated, d_down, partner, shards, got=None):
    rows = FF // shards
    order = lambda i: shards - 1 - i
    pick_column = lambda i, p: (0, 1 - p[CORE] if partner else p[CORE])
    one = pl.BlockSpec((1, rows, CHUNK), lambda i, p: (order(i), 0, 0))
    operands, specs = [activated, d_down], []
    if got is None:
        outs, out_specs = shape((shards, rows, CHUNK)), one
    else:
        operands.append(got)
        specs.append(one)
        outs, out_specs = (shape((rows, CHUNK)),) * shards, [constant((rows, CHUNK))] * shards
    return call(
        functools.partial(down_gradient_body, shards=shards, adds=got is not None),
        "down_gradient",
        outs,
        (shards,),
        [
            pl.BlockSpec((LEN, rows), lambda i, p: (0, jnp.bitwise_xor(p[Y], order(i)))),
            pl.BlockSpec((LEN, CHUNK), pick_column),
        ]
        + specs,
        out_specs,
        flops=LEN * D * FF,
    )(place, *operands)


def row_gradient_body(place, *refs, terms, shards, adds):
    rows = D // shards
    operands, rest = refs[: 2 * terms], refs[2 * terms :]
    got, outs, total = (rest[0], rest[1:-1], rest[-1]) if adds else (None, rest[:-1], rest[-1])
    block = 0
    for term in range(terms):
        left, right = operands[2 * term : 2 * term + 2]
        width = right.shape[1]
        total[:, :width] = matmul_left_t(left[...], right[...])
        for j in range(width // CHUNK):
            here = slice(block * rows, (block + 1) * rows)
            block += 1
            for d in range(shards):
                value = total[pl.ds(shard_row(place, d, rows), rows), j * CHUNK : (j + 1) * CHUNK]
                if adds:
                    outs[d][here, :] = rounded(value + as_float(got[d, here, :]))
                else:
                    outs[0][d, here, :] = rounded(value)


def row_gradient(place, terms, shards, steps=1, got=None):
    rows = D // shards
    widths = [right_width for _, _, right_width, _ in terms]
    count = sum(widths) // CHUNK
    block = count * rows
    specs, operands = [], []
    for left, right, width, first in terms:
        specs.append(constant((LEN, D)))
        specs.append(pl.BlockSpec((LEN, width), lambda i, p, first=first: (0, first(p) + i)))
        operands += [left, right]
    all_rows = pl.BlockSpec((shards, block, CHUNK), lambda i, p: (0, i, 0))
    one = pl.BlockSpec((block, CHUNK), lambda i, p: (i, 0))
    if got is None:
        outs, out_specs = shape((shards, steps * block, CHUNK)), all_rows
    else:
        specs.append(all_rows)
        operands.append(got)
        outs, out_specs = (shape((steps * block, CHUNK)),) * shards, [one] * shards
    return call(
        functools.partial(
            row_gradient_body, terms=len(terms), shards=shards, adds=got is not None
        ),
        "row_gradient",
        outs,
        (steps,),
        specs,
        out_specs,
        [pltpu.VMEM((D, max(widths)), F32)],
        flops=2 * LEN * D * sum(widths) * steps,
    )(place, *operands)


class Place:
    def __init__(self, replicas, shards):
        self.replicas, self.shards, self.depth = replicas, shards, replicas // 4
        replica = lax.axis_index("replica")
        self.index = [replica % 2, replica // 2 % 2, replica // 4, lax.axis_index("shard")]
        self.core, self.x, self.z, self.y = self.index
        self.vector = jnp.stack(self.index).astype(jnp.int32)

    def shard(self, value, mask):
        return lax.ppermute(value, "shard", [(i, i ^ mask) for i in range(self.shards)])

    def replica(self, value, mask):
        return lax.ppermute(value, "replica", [(i, i ^ mask) for i in range(self.replicas)])


def tie(value, *first):
    return lax.optimization_barrier((value,) + first)[0]


def pick(options, index):
    chosen = options[-1]
    for at in range(len(options) - 2, -1, -1):
        chosen = jnp.where(index == at, options[at], chosen)
    return chosen


def gather_shards(value, at):
    found = {0: value}
    mask = 1
    while mask < at.shards:
        for d in range(mask):
            found[d | mask] = at.shard(found[d], mask)
        mask *= 2
    return [found[d] for d in range(at.shards)]


def half_rows(weight, at):
    half = weight.shape[0] // 2
    return lax.dynamic_slice_in_dim(weight, at.core * half, half, 0)


def weight_pieces(weight, near, at):
    pieces = [weight]
    for block in near[1:]:
        pieces += [block, at.replica(block, 1)]
    return pieces


def exchange_shards(parts, at):
    mask = at.shards // 2
    while mask > 1:
        parts = [
            rounded(as_float(parts[d]) + as_float(at.shard(parts[d | mask], mask)))
            for d in range(mask)
        ]
        mask //= 2
    return parts[0], at.shard(parts[1], 1)


def split_body(place, *refs, count, parts):
    outs = refs[2 * count * parts :]
    for d in range(parts):
        row = 0
        for at in range(count):
            keep, got = refs[2 * (d * count + at) : 2 * (d * count + at) + 2]
            height = keep.shape[0]
            outs[d][row : row + height, :] = rounded(as_float(keep[...]) + as_float(got[...]))
            row += height


def split_add(at, which, groups, parts):
    heights = [keep.shape[0] // parts for keep, _ in groups]
    index = at.index[which]
    if any(height % 16 for height in heights):
        found = []
        for d in range(parts):
            blocks = []
            for (keep, got), height in zip(groups, heights):
                cut = lambda v: lax.dynamic_slice_in_dim(v, (index ^ d) * height, height, 0)
                blocks.append(rounded(as_float(cut(keep)) + as_float(cut(got))))
            found.append(jnp.concatenate(blocks) if len(blocks) > 1 else blocks[0])
        return found
    specs, operands = [], []
    for d in range(parts):
        for (keep, got), height in zip(groups, heights):
            spec = pl.BlockSpec(
                (height, CHUNK), lambda i, p, d=d: (jnp.bitwise_xor(p[which], d), 0)
            )
            specs += [spec, spec]
            operands += [keep, got]
    total = sum(heights)
    return call(
        functools.partial(split_body, count=len(groups), parts=parts),
        "split_add",
        (shape((total, CHUNK)),) * parts,
        (1,),
        specs,
        [constant((total, CHUNK))] * parts,
    )(at.vector, *operands)


def join_body(place, *refs, which):
    output = refs[-1]
    for d, piece in enumerate(refs[:-1]):
        height = piece.shape[0]
        start = pl.multiple_of(jnp.bitwise_xor(place[which], d) * height, 16)
        output[pl.ds(start, height), :] = piece[...]


def join_rows(at, which, pieces):
    height, parts = pieces[0].shape[0], len(pieces)
    index = at.index[which]
    if height % 16:
        return jnp.concatenate([pick(pieces, index ^ j) for j in range(parts)])
    return call(
        functools.partial(join_body, which=which),
        "join_rows",
        shape((parts * height, CHUNK)),
        (1,),
        [constant((height, CHUNK))] * parts,
        constant((parts * height, CHUNK)),
    )(at.vector, *pieces)


def sum_replicas(groups, at):
    keep, send = split_add(at, X, groups, 2)
    return finish_sum(keep, at.replica(send, 2), at)


def finish_sum(keep, got, at):
    blocks = split_add(at, Z, [(keep, got)], at.depth)
    total = as_float(blocks[0])
    for d in range(1, at.depth):
        total += as_float(at.replica(blocks[d], 4 * d))
    total = rounded(total)
    found = [total] + [at.replica(total, 4 * d) for d in range(1, at.depth)]
    mine = join_rows(at, Z, found)
    other = at.replica(mine, 2)
    return [mine, other, at.replica(mine, 1), at.replica(other, 1)]


def finish_feed_body(place, *refs, rows, blocks):
    sources, (down, up) = refs[:4], refs[4:]
    at = pl.program_id(0)
    half = blocks * rows
    for index in range(4):

        @pl.when(at == index)
        def _(index=index):
            source = sources[index]
            down[...] = as_float(source[: down.shape[0], :])
            for j in range(blocks):
                start = down.shape[0] + j * rows
                up[:, j * CHUNK : (j + 1) * CHUNK] = as_float(source[start : start + rows, :])


def finish_feed(at, sources):
    rows, down_rows = D // at.shards, FF // at.shards
    blocks = FF // (4 * CHUNK)
    half = lambda i, p: jnp.bitwise_xor(p[X], i % 2)
    core = lambda i, p: jnp.bitwise_xor(p[CORE], i // 2)
    return call(
        functools.partial(finish_feed_body, rows=rows, blocks=blocks),
        "finish_feed",
        (shape((down_rows, D), F32), shape((rows, FF), F32)),
        (4,),
        [constant(source.shape) for source in sources],
        [
            pl.BlockSpec((down_rows // 2, CHUNK), lambda i, p: (half(i, p), core(i, p))),
            pl.BlockSpec((rows, blocks * CHUNK), lambda i, p: (0, core(i, p) * 2 + half(i, p))),
        ],
    )(at.vector, *sources)


def finish_attention_body(place, *refs, layouts, rows):
    groups = len(layouts)
    sources, (qkv, out), holds = refs[: 4 * groups], refs[4 * groups : 4 * groups + 2], refs[4 * groups + 2 :]
    for group, layout in enumerate(layouts):
        hold = holds[group]
        for index in range(4):
            source = sources[4 * group + index]
            height = source.shape[0]
            start = pl.multiple_of(jnp.bitwise_xor(place[X], index % 2) * height, 16)
            hold[index // 2, pl.ds(start, height), :] = source[...]
        for side in range(2):
            core = jnp.bitwise_xor(place[CORE], side)
            for block, name in enumerate(layout):
                value = as_float(hold[side, block * rows : (block + 1) * rows, :])
                if name is None:
                    out[:, pl.ds(pl.multiple_of(core * CHUNK, WIDE), CHUNK)] = value
                    continue
                for part in range(3):
                    lane = part * D + (core * HALF_PAIRS + name) * WIDE
                    qkv[:, pl.ds(pl.multiple_of(lane, WIDE), WIDE)] = value[
                        :, part * WIDE : (part + 1) * WIDE
                    ]


def finish_attention(at, groups, layouts):
    rows = D // at.shards
    operands = [source for group in groups for source in group]
    return call(
        functools.partial(finish_attention_body, layouts=layouts, rows=rows),
        "finish_attention",
        (shape((rows, 3 * D), F32), shape((rows, D), F32)),
        (1,),
        [constant(source.shape) for source in operands],
        [constant((rows, 3 * D)), constant((rows, D))],
        [pltpu.VMEM((2, len(layout) * rows, CHUNK), LOW) for layout in layouts],
    )(at.vector, *operands)


def sum_small(values, at):
    parts = [lax.dynamic_index_in_dim(values, at.y ^ d, 0, False) for d in range(at.shards)]
    mask = at.shards // 2
    while mask:
        parts = [parts[d] + at.shard(parts[d | mask], mask) for d in range(mask)]
        mask //= 2
    total = parts[0]
    mask = 1
    while mask < at.replicas:
        total = total + at.replica(total, mask)
        mask *= 2
    return total


ATTENTION_GROUPS = ((0, 3),)


def local(
    replicas,
    shards,
    inputs,
    segments,
    w_qkv,
    b_qv,
    w_out,
    b_out,
    attn_gain,
    attn_shift,
    w_up,
    b_up,
    w_down,
    b_down,
    ffn_gain,
    ffn_shift,
    cotangent,
):
    at = Place(replicas, shards)
    place = at.vector
    segments = segments.reshape(LEN)

    near_qkv = gather_shards(half_rows(w_qkv, at), at)
    vectors = (b_qv, b_out, attn_gain, attn_shift, b_up, b_down, ffn_gain, ffn_shift)
    sizes = [vector.shape[0] for vector in vectors]
    small = gather_shards(jnp.concatenate(vectors), at)
    small = as_float(jnp.stack([pick(small, at.y ^ j) for j in range(shards)]))
    full, offset = [], 0
    for size in sizes:
        full.append(small[:, offset : offset + size].reshape(-1))
        offset += size
    full = jnp.concatenate(full).reshape(1, VECTORS)
    feature_q, feature_k = document_features(segments)
    forward_ranges = key_ranges(segments, FORWARD_ROWS)
    backward_ranges = key_ranges(segments, BACKWARD_ROWS)

    pieces_qkv = weight_pieces(w_qkv, near_qkv, at)
    half_out, half_up = (half_rows(w, at) for w in (w_out, w_up))
    half_out, half_up, *_ = lax.optimization_barrier((half_out, half_up, near_qkv[-1]))
    near_out, near_up = gather_shards(half_out, at), gather_shards(half_up, at)
    projected, weight_qkv = project(place, inputs, full, pieces_qkv)
    context, log_total = attn_fwd(
        forward_ranges, projected, feature_q, feature_k, 6
    )
    near_out, near_up, context = lax.optimization_barrier((near_out, near_up, context))
    half_down = tie(half_rows(w_down, at), near_up[-1])
    near_down = gather_shards(half_down, at)
    pieces_out = weight_pieces(w_out, near_out, at)
    pieces_up = weight_pieces(w_up, near_up, at)
    normal, inverse, low, activated, slope = up_block(
        place, context, inputs, full, pieces_out, pieces_up
    )
    near_down, activated = lax.optimization_barrier((near_down, activated))
    pieces_down = weight_pieces(w_down, near_down, at)
    layer_output, d_sum_two, d_down, d_up, sums_two = down_block(
        place, activated, slope, normal, cotangent, full, pieces_down
    )

    down_send = down_gradient(place, activated, d_down, True, shards)
    down_got = at.replica(down_send, 1)
    up_width = FF // 4
    other_half, own_half = (lambda p: 2 * (1 - p[CORE])), (lambda p: 2 * p[CORE])
    up_send = row_gradient(place, [(low, d_up, up_width, other_half)], shards, 2)
    up_got = at.replica(up_send, 1)
    down_parts = down_gradient(place, activated, d_down, False, shards, down_got)
    down_pair = exchange_shards(down_parts, at)
    up_parts = row_gradient(place, [(low, d_up, up_width, own_half)], shards, 2, up_got)
    up_parts, d_up = lax.optimization_barrier((up_parts, d_up))
    d_sum_one, d_attended, d_context, sums_one = back_block(
        place, d_up, d_sum_two, normal, inverse, full, pieces_up, pieces_out
    )

    def attention_back(block, first, count, d_context):
        start = (block * HALF_PAIRS + first) // count
        return attn_bwd(
            jnp.concatenate([backward_ranges, start.reshape(1)]),
            projected,
            context,
            d_context,
            log_total,
            feature_q,
            feature_k,
            count,
            count,
        )

    d_other, bias_other = attention_back(1 - at.core, 0, 3, d_context)
    down_pair, d_other = lax.optimization_barrier((down_pair, d_other))
    up_parts = tie(up_parts, down_pair[1])
    up_pair = exchange_shards(up_parts, at)
    other_out, own_out = (lambda p: 1 - p[CORE]), (lambda p: p[CORE])
    zero = lambda p: 0
    send = row_gradient(
        place,
        [(inputs, d_other, 3 * TRIPLE, zero), (context, d_attended, CHUNK, other_out)],
        shards,
    )
    got = at.replica(send, 1)
    d_context, got = lax.optimization_barrier((d_context, got))
    d_own, bias_own = attention_back(at.core, 0, 3, d_context)
    up_pair, d_own = lax.optimization_barrier((up_pair, d_own))
    parts = row_gradient(
        place,
        [(inputs, d_own, 3 * TRIPLE, zero), (context, d_attended, CHUNK, own_out)],
        shards,
        1,
        got,
    )
    attention_pair = exchange_shards(parts, at)
    feed = sum_replicas([down_pair, up_pair], at)
    attention_sum = sum_replicas([attention_pair], at)
    input_grad = input_gradient(
        place, weight_qkv, d_sum_one, [d_other, d_own], ((True, 0, 3), (False, 0, 3))
    )
    grad_w_down, grad_w_up = finish_feed(at, feed)
    grad_w_qkv, grad_w_out = finish_attention(at, [attention_sum], ((0, 1, 2, None),))

    bias = jnp.concatenate(
        [pick([bias_own, bias_other], at.core), pick([bias_other, bias_own], at.core)], axis=1
    )
    sums_one, sums_two = sums_one[0], sums_two[0]
    grads = (
        bias.reshape(-1),
        sums_one[2 * D :],
        sums_one[:D],
        sums_one[D : 2 * D],
        sums_two[3 * D :],
        sums_two[2 * D : 3 * D],
        sums_two[:D],
        sums_two[D : 2 * D],
    )
    packed = jnp.concatenate([grad.reshape(shards, -1) for grad in grads], axis=1)
    packed = sum_small(packed.reshape(shards, -1, 128), at).reshape(-1)
    owned, offset = [], 0
    for size in sizes:
        owned.append(packed[offset : offset + size])
        offset += size
    return (
        layer_output,
        input_grad,
        grad_w_qkv,
        owned[0],
        grad_w_out,
        owned[1],
        owned[2],
        owned[3],
        grad_w_up,
        owned[4],
        grad_w_down,
        owned[5],
        owned[6],
        owned[7],
    )


def solution(mesh):
    token, matrix, vector = P(("replica", "shard"), None), P("shard", None), P("shard")
    weights = (matrix, vector, matrix, vector, vector, vector)
    weights += (matrix, vector, matrix, vector, vector, vector)
    return jax.shard_map(
        functools.partial(local, mesh.shape["replica"], mesh.shape["shard"]),
        mesh=mesh,
        in_specs=(token, token) + weights + (token,),
        out_specs=(token, token) + weights,
        check_vma=False,
    )
```

```python
import functools

import jax
import jax.numpy as jnp
from jax import lax
from jax.experimental import pallas as pl
from jax.experimental.pallas import tpu as pltpu
from jax.sharding import PartitionSpec as P

D = 768
FF = 3072
HEADS = 12
HEAD_DIM = 64
LEN = 1024
PAIRS = HEADS // 2
HALF_PAIRS = PAIRS // 2
WIDE = 2 * HEAD_DIM
TRIPLE = 3 * WIDE
KEY_TILE = 128
FORWARD_ROWS = 128
BACKWARD_ROWS = 256
TOKEN_ROWS = 256
CHUNK = 384
BIG = float(2**30)
EPSILON = 1e-12
F32 = jnp.float32
LOW = jnp.bfloat16
B_QV, B_OUT, ATTN_GAIN, ATTN_SHIFT = 0, 2 * D, 3 * D, 4 * D
B_UP, B_DOWN, FFN_GAIN, FFN_SHIFT = 5 * D, 5 * D + FF, 6 * D + FF, 7 * D + FF
VECTORS = 8 * D + FF
CORE, X, Z, Y, Z_BITS = 0, 1, 2, 3, 4


def matmul(left, right):
    return jnp.dot(left, right, preferred_element_type=F32)


def matmul_right_t(left, right):
    return lax.dot_general(left, right, (((1,), (1,)), ((), ())), preferred_element_type=F32)


def matmul_left_t(left, right):
    return lax.dot_general(left, right, (((0,), (0,)), ((), ())), preferred_element_type=F32)


def as_float(value):
    return value.astype(F32)


def rounded(value):
    return value.astype(LOW)


def shape(dims, kind=LOW):
    return jax.ShapeDtypeStruct(dims, kind)


def constant(dims):
    return pl.BlockSpec(dims, lambda *at: (0,) * len(dims))


def tokens(width):
    return pl.BlockSpec((TOKEN_ROWS, width), lambda i, *place: (i, 0))


ANYWHERE = pl.BlockSpec(memory_space=pl.ANY)


def call(
    body, name, out_shape, grid, in_specs, out_specs, scratch=(), flops=0, exps=0, aliases=None
):
    return pl.pallas_call(
        body,
        out_shape=out_shape,
        grid_spec=pltpu.PrefetchScalarGridSpec(
            num_scalar_prefetch=1,
            grid=grid,
            in_specs=in_specs,
            out_specs=out_specs,
            scratch_shapes=list(scratch),
        ),
        cost_estimate=pl.CostEstimate(flops=flops, transcendentals=exps, bytes_accessed=1 << 20),
        input_output_aliases=aliases or {},
        name=name,
    )


def piece_rows(place, count, own_rows):
    half = own_rows // 2
    core, y = place[CORE], place[Y]
    found = [pl.multiple_of(y * own_rows, half)]
    for d in range(1, (count + 1) // 2):
        base = jnp.bitwise_xor(y, d) * own_rows
        found.append(pl.multiple_of(base + core * half, half))
        found.append(pl.multiple_of(base + (1 - core) * half, half))
    return found


def assemble(place, pieces, buffer, semaphores):
    starts = piece_rows(place, len(pieces), pieces[0].shape[0])
    return [
        pltpu.make_async_copy(
            piece, buffer.at[pl.ds(start, piece.shape[0]), :], semaphores.at[at]
        )
        for at, (piece, start) in enumerate(zip(pieces, starts))
    ]


def start_all(copies):
    for copy in copies:
        copy.start()


def wait_all(copies):
    for copy in copies:
        copy.wait()


def project_body(place, inputs, vectors, *refs):
    pieces, (projected, weight) = refs[:-2], refs[-2:]
    count = len(pieces) // 3
    starts = piece_rows(place, count, pieces[0].shape[0])
    for part in range(3):
        for at in range(count):
            block = pieces[part * count + at]
            rows = pl.ds(starts[at], block.shape[0])
            for j in range(2):
                lanes = slice(j * TRIPLE + part * WIDE, j * TRIPLE + (part + 1) * WIDE)
                weight[rows, lanes] = block[:, j * WIDE : (j + 1) * WIDE]
    first = pl.program_id(0) * 2 * WIDE
    bias = []
    for j in range(2):
        at = pl.multiple_of(first + j * WIDE, WIDE)
        bias.append(vectors[:, pl.ds(B_QV + at, WIDE)])
        bias.append(jnp.zeros((1, WIDE), F32))
        bias.append(vectors[:, pl.ds(B_QV + D + at, WIDE)])
    bias = jnp.concatenate(bias, axis=1)
    projected[...] = rounded(matmul(inputs[...], weight[...]) + bias)


def project(place, inputs, vectors, pieces):
    steps = PAIRS // 2
    column = pl.BlockSpec((LEN, 2 * TRIPLE), lambda i, p: (0, i))
    specs, operands = [], []
    for part in range(3):
        for piece in pieces:
            specs.append(
                pl.BlockSpec(
                    (piece.shape[0], 2 * WIDE), lambda i, p, part=part: (0, part * steps + i)
                )
            )
            operands.append(piece)
    return call(
        project_body,
        "project",
        (shape((LEN, 3 * D)), shape((D, 3 * D))),
        (steps,),
        [constant((LEN, D)), constant((1, VECTORS))] + specs,
        [column, pl.BlockSpec((D, 2 * TRIPLE), lambda i, p: (0, i))],
        flops=2 * LEN * D * 3 * D,
    )(place, inputs, vectors, *operands)


def key_ranges(segments, rows):
    tiles = segments.reshape(LEN // rows, rows)
    below = jnp.sum(segments[None, :] < tiles[:, :1], axis=1, dtype=jnp.int32)
    upto = jnp.sum(segments[None, :] <= tiles[:, -1:], axis=1, dtype=jnp.int32)
    start = below // KEY_TILE
    count = (upto + KEY_TILE - 1) // KEY_TILE - start
    return jnp.concatenate([start, count])
def document_features(segments):
    lane = jnp.arange(WIDE, dtype=jnp.int32) % HEAD_DIM
    hot = segments[:, None] == lane[None, :]
    q = jnp.where((lane < 16) & hot, 1.0, 0.0).astype(LOW)
    k = jnp.where(lane < 16, jnp.where(hot, 0.0, -BIG), jnp.where(lane < 19, 1.0, 0.0)).astype(LOW)
    return q,k
def stack_heads(pair, side_a, side_b, left):
    zero=jnp.zeros_like(pair)
    a=jnp.concatenate([jnp.where(left,pair,zero),side_a],axis=1)
    b=jnp.concatenate([jnp.where(left,zero,pair),side_b],axis=1)
    return jnp.concatenate([a,b],axis=0)


def fwd_body(ranges, packed, feature_q, feature_k, context, log_total, key_side, value_t, *, group):
    tiles=LEN//FORWARD_ROWS
    for g in range(group):
        at=3*WIDE*g
        key_side[g,:,:WIDE]=packed[:,at+WIDE:at+2*WIDE]
        key_side[g,:,WIDE:]=feature_k[...]
        value_t[g,:WIDE,:]=packed[:,at+2*WIDE:at+3*WIDE].T
        value_t[g,WIDE:,:]=jnp.ones((16,LEN),LOW)
    left=lax.broadcasted_iota(jnp.int32,(FORWARD_ROWS,WIDE),1)<HEAD_DIM
    def tile(index,carry):
        here=pl.ds(pl.multiple_of(index*FORWARD_ROWS,FORWARD_ROWS),FORWARD_ROWS)
        side=feature_q[here,:]
        zero=jnp.zeros_like(side)
        sa=jnp.where(left,side,zero); sb=jnp.where(left,zero,side)
        stats=[stack_heads(packed[here,3*WIDE*g:3*WIDE*g+WIDE]*jnp.asarray(HEAD_DIM**-0.5,LOW),sa,sb,left) for g in range(group)]
        start=pl.multiple_of(ranges[index]*KEY_TILE,KEY_TILE)
        def over(width):
            def run():
                span=pl.ds(start,width)
                ss=[matmul_right_t(key_side[g,span,:],stats[g]) for g in range(group)]
                for g in range(group):
                    s=ss[g]
                    m=jnp.max(s,axis=0,keepdims=True)
                    p=jnp.exp(s-m).astype(LOW)
                    o=matmul(value_t[g,:,span],p)
                    total=o[WIDE:WIDE+1,:]
                    inv=1.0/total
                    lse=m+jnp.log(total)
                    log_total[g,0:1,here]=lse[:,:FORWARD_ROWS]
                    log_total[g,1:2,here]=lse[:,FORWARD_ROWS:]
                    both=jnp.concatenate([o[:HEAD_DIM,:FORWARD_ROWS]*inv[:,:FORWARD_ROWS],o[HEAD_DIM:WIDE,FORWARD_ROWS:]*inv[:,FORWARD_ROWS:]],axis=0)
                    context[here,g*WIDE:(g+1)*WIDE]=both.T.astype(LOW)
            return run
        lax.switch(ranges[tiles+index]-1,[over(KEY_TILE*(n+1)) for n in range(LEN//KEY_TILE)])
        return carry
    lax.fori_loop(0,tiles,tile,0)

def attn_fwd(r,packed,fq,fk,group=2):
    whole=pl.BlockSpec((LEN,WIDE),lambda h,r:(0,0))
    return pl.pallas_call(lambda *a: fwd_body(*a,group=group),
        out_shape=(jax.ShapeDtypeStruct((LEN,D),LOW),jax.ShapeDtypeStruct((PAIRS,2,LEN),F32)),
        grid_spec=pltpu.PrefetchScalarGridSpec(num_scalar_prefetch=1,grid=(PAIRS//group,),
          in_specs=[pl.BlockSpec((LEN,3*WIDE*group),lambda h,r:(0,h)),whole,whole],
          out_specs=[pl.BlockSpec((LEN,WIDE*group),lambda h,r:(0,h)),pl.BlockSpec((group,2,LEN),lambda h,r:(h,0,0))],
          scratch_shapes=[pltpu.VMEM((group,LEN,2*WIDE),LOW),pltpu.VMEM((group,WIDE+16,LEN),LOW)]),
        name="attention_forward")(r,packed,fq,fk)

def bwd_body(ranges,packed,context,d_context,log_total,feature_q,feature_k,d_packed,bias_sums,key_side,value_side,key_t,d_key,d_value,*,group):
    tiles=LEN//BACKWARD_ROWS
    lane=lax.broadcasted_iota(jnp.int32,(LEN,WIDE),1)
    ones=jnp.where(lane%HEAD_DIM<3,1.0,0.0).astype(LOW)
    for g in range(group):
        at=3*WIDE*g
        keys=packed[:,at+WIDE:at+2*WIDE]
        key_side[g,:,:WIDE]=keys
        key_side[g,:,WIDE:]=feature_k[...]
        value_side[g,:,:WIDE]=packed[:,at+2*WIDE:at+3*WIDE]
        value_side[g,:,WIDE:]=ones
        key_t[g]=keys.T
    d_key[...]=jnp.zeros_like(d_key); d_value[...]=jnp.zeros_like(d_value)
    lane_q=lax.broadcasted_iota(jnp.int32,(BACKWARD_ROWS,WIDE),1)
    left=lane_q<HEAD_DIM; inner=lane_q%HEAD_DIM
    zero=jnp.zeros((BACKWARD_ROWS,WIDE),LOW)
    def spread(value,base):
        high=as_float(value.astype(LOW)); rest=value-high
        middle=as_float(rest.astype(LOW)); tail=rest-middle
        return jnp.where(inner==base,high,jnp.where(inner==base+1,middle,jnp.where(inner==base+2,tail,0.0))).astype(LOW)
    def tile(index,sums):
        here=pl.ds(pl.multiple_of(index*BACKWARD_ROWS,BACKWARD_ROWS),BACKWARD_ROWS)
        hot=feature_q[here,:]
        qs=[];gs=[]
        for g in range(group):
            queries=packed[here,3*WIDE*g:3*WIDE*g+WIDE]*jnp.asarray(HEAD_DIM**-0.5,LOW)
            logs=log_total[g,:,here]
            cols=jnp.concatenate([logs,jnp.zeros((6,BACKWARD_ROWS),F32)],axis=0).T
            lse=jnp.where(left,cols[:,0:1],cols[:,1:2])
            side=hot+spread(-lse,16)
            qs.append(stack_heads(queries,jnp.where(left,side,zero),jnp.where(left,zero,side),left))
            grad=d_context[here,g*WIDE:(g+1)*WIDE]
            product=as_float(grad)*as_float(context[here,g*WIDE:(g+1)*WIDE])
            dot_a=jnp.sum(jnp.where(left,product,0.0),axis=1,keepdims=True)
            dot_b=jnp.sum(jnp.where(left,0.0,product),axis=1,keepdims=True)
            side_g=spread(-jnp.where(left,dot_a,dot_b),0)
            gs.append(stack_heads(grad,jnp.where(left,side_g,zero),jnp.where(left,zero,side_g),left))
        start=pl.multiple_of(ranges[index]*KEY_TILE,KEY_TILE)
        def over(width):
            def run():
                span=pl.ds(start,width)
                for g in range(group):
                    p=jnp.exp(matmul_right_t(key_side[g,span,:],qs[g]))
                    dp=matmul_right_t(value_side[g,span,:],gs[g])
                    pb=p.astype(LOW); ds=(p*dp).astype(LOW)
                    d_value[g,span,:]+=matmul(pb,gs[g][:,:WIDE])
                    d_key[g,span,:]+=matmul(ds,qs[g][:,:WIDE])
                    dq=matmul(key_t[g,:,span],ds)
                    dq=jnp.concatenate([dq[:HEAD_DIM,:BACKWARD_ROWS],dq[HEAD_DIM:,BACKWARD_ROWS:]],axis=0)
                    d_packed[here,3*WIDE*g:3*WIDE*g+WIDE]=(dq.T*HEAD_DIM**-0.5).astype(LOW)
            return run
        lax.switch(ranges[tiles+index]-1,[over(KEY_TILE*(n+1)) for n in range(LEN//KEY_TILE)])
        return tuple(sums[g]+jnp.sum(as_float(d_packed[here,3*WIDE*g:3*WIDE*g+WIDE]),axis=0,keepdims=True) for g in range(group))
    sums=lax.fori_loop(0,tiles,tile,(jnp.zeros((1,WIDE),F32),)*group)
    for g in range(group):
        at=3*WIDE*g
        low=d_value[g].astype(LOW)
        d_packed[:,at+WIDE:at+2*WIDE]=d_key[g].astype(LOW)
        d_packed[:,at+2*WIDE:at+3*WIDE]=low
        bias_sums[0:1,g*WIDE:(g+1)*WIDE]=sums[g]
        bias_sums[1:2,g*WIDE:(g+1)*WIDE]=jnp.sum(as_float(low),axis=0,keepdims=True)

def attn_bwd(r,packed,ctx,dctx,lse,fq,fk,pairs,group=2):
    whole=pl.BlockSpec((LEN,WIDE),lambda h,r:(0,0))
    last=r.shape[0]-1
    col=lambda w: pl.BlockSpec((LEN,w*group),lambda h,r:(0,r[last]+h))
    return pl.pallas_call(lambda *a: bwd_body(*a,group=group),
        out_shape=(jax.ShapeDtypeStruct((LEN,pairs*3*WIDE),LOW),jax.ShapeDtypeStruct((2,pairs*WIDE),F32)),
        grid_spec=pltpu.PrefetchScalarGridSpec(num_scalar_prefetch=1,grid=(pairs//group,),
          in_specs=[col(3*WIDE),col(WIDE),col(WIDE),pl.BlockSpec((group,2,LEN),lambda h,r:(r[last]+h,0,0)),whole,whole],
          out_specs=[pl.BlockSpec((LEN,3*WIDE*group),lambda h,r:(0,h)),pl.BlockSpec((2,WIDE*group),lambda h,r:(0,h))],
          scratch_shapes=[pltpu.VMEM((group,LEN,2*WIDE),LOW)]*2+[pltpu.VMEM((group,WIDE,LEN),LOW)]+[pltpu.VMEM((group,LEN,WIDE),F32)]*2),
        name="attention_backward")(r,packed,ctx,dctx,lse,fq,fk)


def normalize(hidden):
    average = jnp.mean(hidden, axis=-1, keepdims=True)
    centered = hidden - average
    variance = jnp.mean(centered * centered, axis=-1, keepdims=True)
    inverse = lax.rsqrt(variance + EPSILON)
    return centered * inverse, inverse


def normalize_back(grad, normal, inverse):
    first = jnp.mean(grad, axis=-1, keepdims=True)
    second = jnp.mean(grad * normal, axis=-1, keepdims=True)
    return (grad - first - normal * second) * inverse


def column_sum(value):
    return jnp.sum(value, axis=0, keepdims=True)


def up_body(place, context, inputs, vectors, *refs):
    count = (len(refs) - 9) // 2
    out_pieces, up_pieces = refs[:count], refs[count : 2 * count]
    normal, inverse, low, activated, slope, w_out, w_up, out_sem, up_sem = refs[2 * count :]
    out_copies = assemble(place, out_pieces, w_out, out_sem)
    up_copies = assemble(place, up_pieces, w_up, up_sem)
    step = pl.program_id(0)

    @pl.when(step == 0)
    def _():
        start_all(out_copies)
        start_all(up_copies)
        wait_all(out_copies)

    attended = matmul(context[...], w_out[...]) + vectors[:, B_OUT : B_OUT + D]
    value, scale = normalize(as_float(inputs[...]) + attended)
    normal[...] = value
    inverse[...] = jnp.broadcast_to(scale, inverse.shape)
    normed = rounded(
        value * vectors[:, ATTN_GAIN : ATTN_GAIN + D] + vectors[:, ATTN_SHIFT : ATTN_SHIFT + D]
    )
    low[...] = normed

    @pl.when(step == 0)
    def _():
        wait_all(up_copies)

    for at in range(0, FF, D):
        up = matmul(normed, w_up[:, at : at + D]) + vectors[:, B_UP + at : B_UP + at + D]
        below = 0.5 + 0.5 * lax.erf(up * (0.5**0.5))
        density = jnp.exp(-0.5 * up * up) * 0.3989422804014327
        activated[:, at : at + D] = rounded(up * below)
        slope[:, at : at + D] = rounded(below + up * density)


def up_block(place, context, inputs, vectors, out_pieces, up_pieces):
    count = len(out_pieces)
    return call(
        up_body,
        "out_norm_up",
        (
            shape((LEN, D), F32),
            shape((LEN, WIDE), F32),
            shape((LEN, D)),
            shape((LEN, FF)),
            shape((LEN, FF)),
        ),
        (LEN // TOKEN_ROWS,),
        [tokens(D), tokens(D), constant((1, VECTORS))] + [ANYWHERE] * (2 * count),
        [tokens(D), tokens(WIDE), tokens(D), tokens(FF), tokens(FF)],
        [
            pltpu.VMEM((D, D), LOW),
            pltpu.VMEM((D, FF), LOW),
            pltpu.SemaphoreType.DMA((count,)),
            pltpu.SemaphoreType.DMA((count,)),
        ],
        flops=2 * LEN * D * (D + FF),
        exps=2 * LEN * FF,
    )(place, context, inputs, vectors, *out_pieces, *up_pieces)


def down_body(place, activated, slope, normal, cotangent, vectors, *refs):
    count = len(refs) - 7
    pieces = refs[:count]
    output, d_sum, d_down, d_up, sums, w_down, sem = refs[count:]
    copies = assemble(place, pieces, w_down, sem)
    step = pl.program_id(0)

    @pl.when(step == 0)
    def _():
        start_all(copies)
        sums[...] = jnp.zeros_like(sums)
        wait_all(copies)

    down = matmul(activated[...], w_down[...]) + vectors[:, B_DOWN : B_DOWN + D]
    gain = vectors[:, ATTN_GAIN : ATTN_GAIN + D]
    normed = normal[...] * gain + vectors[:, ATTN_SHIFT : ATTN_SHIFT + D]
    value, scale = normalize(normed + down)
    gain = vectors[:, FFN_GAIN : FFN_GAIN + D]
    output[...] = rounded(value * gain + vectors[:, FFN_SHIFT : FFN_SHIFT + D])
    grad = as_float(cotangent[...])
    sums[:, :D] += column_sum(grad * value)
    sums[:, D : 2 * D] += column_sum(grad)
    d_two = normalize_back(grad * gain, value, scale)
    d_sum[...] = d_two
    d_low = rounded(d_two)
    d_down[...] = d_low
    sums[:, 2 * D : 3 * D] += column_sum(as_float(d_low))
    for at in range(0, FF, D):
        d_activated = matmul_right_t(d_low, w_down[at : at + D, :])
        part = rounded(d_activated * as_float(slope[:, at : at + D]))
        d_up[:, at : at + D] = part
        sums[:, 3 * D + at : 4 * D + at] += column_sum(as_float(part))


def down_block(place, activated, slope, normal, cotangent, vectors, pieces):
    count = len(pieces)
    return call(
        down_body,
        "down_norm_back",
        (
            shape((LEN, D)),
            shape((LEN, D), F32),
            shape((LEN, D)),
            shape((LEN, FF)),
            shape((1, 3 * D + FF), F32),
        ),
        (LEN // TOKEN_ROWS,),
        [tokens(FF), tokens(FF), tokens(D), tokens(D), constant((1, VECTORS))]
        + [ANYWHERE] * count,
        [tokens(D), tokens(D), tokens(D), tokens(FF), constant((1, 3 * D + FF))],
        [pltpu.VMEM((FF, D), LOW), pltpu.SemaphoreType.DMA((count,))],
        flops=4 * LEN * D * FF,
    )(place, activated, slope, normal, cotangent, vectors, *pieces)


def back_body(place, d_up, d_sum_two, normal, inverse, vectors, *refs):
    count = (len(refs) - 8) // 2
    up_pieces, out_pieces = refs[:count], refs[count : 2 * count]
    d_sum, d_attended, d_context, sums, w_up, w_out, up_sem, out_sem = refs[2 * count :]
    up_copies = assemble(place, up_pieces, w_up, up_sem)
    out_copies = assemble(place, out_pieces, w_out, out_sem)
    step = pl.program_id(0)

    @pl.when(step == 0)
    def _():
        start_all(up_copies)
        start_all(out_copies)
        sums[...] = jnp.zeros_like(sums)
        wait_all(up_copies)
        wait_all(out_copies)

    d_normed = d_sum_two[...] + matmul_right_t(d_up[...], w_up[...])
    value = normal[...]
    sums[:, :D] += column_sum(d_normed * value)
    sums[:, D : 2 * D] += column_sum(d_normed)
    d_one = normalize_back(
        d_normed * vectors[:, ATTN_GAIN : ATTN_GAIN + D], value, inverse[:, :1]
    )
    d_sum[...] = d_one
    low = rounded(d_one)
    d_attended[...] = low
    sums[:, 2 * D :] += column_sum(as_float(low))
    d_context[...] = rounded(matmul_right_t(low, w_out[...]))


def back_block(place, d_up, d_sum_two, normal, inverse, vectors, up_pieces, out_pieces):
    count = len(up_pieces)
    return call(
        back_body,
        "norm_back",
        (shape((LEN, D), F32), shape((LEN, D)), shape((LEN, D)), shape((1, 3 * D), F32)),
        (LEN // TOKEN_ROWS,),
        [tokens(FF), tokens(D), tokens(D), tokens(WIDE), constant((1, VECTORS))]
        + [ANYWHERE] * (2 * count),
        [tokens(D), tokens(D), tokens(D), constant((1, 3 * D))],
        [
            pltpu.VMEM((D, FF), LOW),
            pltpu.VMEM((D, D), LOW),
            pltpu.SemaphoreType.DMA((count,)),
            pltpu.SemaphoreType.DMA((count,)),
        ],
        flops=2 * LEN * D * (FF + D),
    )(place, d_up, d_sum_two, normal, inverse, vectors, *up_pieces, *out_pieces)


def input_body(place, weight, d_sum, *refs, spans):
    output, pieces = refs[-1], refs[:-1]
    total = d_sum[...]
    for piece, (partner, first, count) in zip(pieces, spans):
        block = 1 - place[CORE] if partner else place[CORE]
        at = pl.multiple_of((first + block * count) * TRIPLE, WIDE)
        total += matmul_right_t(piece[...], weight[:, pl.ds(at, count * TRIPLE)])
    output[...] = rounded(total)


def input_gradient(place, weight, d_sum, pieces, spans):
    return call(
        functools.partial(input_body, spans=spans),
        "input_gradient",
        shape((LEN, D)),
        (LEN // TOKEN_ROWS,),
        [constant((D, 3 * D)), tokens(D)] + [tokens(piece.shape[1]) for piece in pieces],
        tokens(D),
        flops=6 * LEN * D * D,
    )(place, weight, d_sum, *pieces)


def piece_row(place, piece, rows, cuts):
    dy, dx = divmod(piece, cuts)
    start = jnp.bitwise_xor(place[Y], dy) * (cuts * rows)
    if cuts == 2:
        start += jnp.bitwise_xor(place[X], dx) * rows
    return pl.multiple_of(start, 16)


def down_gradient_body(place, left, right, *refs, shards, adds):
    value = matmul_left_t(left[...], right[...])
    if not adds:
        refs[0][0] = rounded(value)
        return
    value = rounded(value + as_float(refs[0][0]))
    for at in range(shards):

        @pl.when(pl.program_id(0) == at)
        def _(at=at):
            refs[1 + at][...] = value


def down_gradient(place, activated, d_down, partner, shards, got=None):
    rows = FF // shards
    pick_column = lambda i, p: (0, 1 - p[CORE] if partner else p[CORE])
    one = pl.BlockSpec((1, rows, CHUNK), lambda i, p: (i, 0, 0))
    operands, specs = [activated, d_down], []
    if got is None:
        outs, out_specs = shape((shards, rows, CHUNK)), one
    else:
        operands.append(got)
        specs.append(one)
        outs, out_specs = (shape((rows, CHUNK)),) * shards, [constant((rows, CHUNK))] * shards
    return call(
        functools.partial(down_gradient_body, shards=shards, adds=got is not None),
        "down_gradient",
        outs,
        (shards,),
        [
            pl.BlockSpec((LEN, rows), lambda i, p: (0, jnp.bitwise_xor(p[Y], i))),
            pl.BlockSpec((LEN, CHUNK), pick_column),
        ]
        + specs,
        out_specs,
        flops=LEN * D * FF,
    )(place, *operands)


def row_gradient_body(place, left, right, *refs, pieces, cuts, adds, extends):
    got, refs = (refs[0], refs[1:]) if adds else (None, refs)
    outs, total = refs[pieces if extends else 0 : -1], refs[-1]
    rows = D // pieces
    total[...] = matmul_left_t(left[...], right[...])
    for j in range(right.shape[1] // CHUNK):
        here = slice(j * rows, (j + 1) * rows)
        for piece in range(pieces):
            start = piece_row(place, piece, rows, cuts)
            value = total[pl.ds(start, rows), j * CHUNK : (j + 1) * CHUNK]
            if adds:
                outs[piece][here, :] = rounded(value + as_float(got[piece, here, :]))
            else:
                outs[0][piece, here, :] = rounded(value)


def row_gradient(
    place, left, right, width, first, steps, pieces, cuts, got=None, spare=0, into=None
):
    rows = D // pieces
    block = width // CHUNK * rows
    specs = [
        constant((LEN, D)),
        pl.BlockSpec((LEN, width), lambda i, p: (0, first(p) + i)),
    ]
    operands, aliases, at = [left, right], {}, 0
    if got is None:
        outs = shape((pieces, steps * block, CHUNK))
        out_specs = pl.BlockSpec((pieces, block, CHUNK), lambda i, p: (0, i, 0))
    else:
        specs.append(pl.BlockSpec((pieces, block, CHUNK), lambda i, p: (0, i, 0)))
        operands.append(got)
        height = steps * block + spare * rows
        if into is not None:
            height = into[0].shape[0]
            at = height // block - steps
            aliases = {len(operands) + 1 + n: n for n in range(pieces)}
            operands += into
            specs += [ANYWHERE] * pieces
        outs = (shape((height, CHUNK)),) * pieces
        out_specs = [pl.BlockSpec((block, CHUNK), lambda i, p: (at + i, 0))] * pieces
    return call(
        functools.partial(
            row_gradient_body,
            pieces=pieces,
            cuts=cuts,
            adds=got is not None,
            extends=into is not None,
        ),
        "row_gradient",
        outs,
        (steps,),
        specs,
        out_specs,
        [pltpu.VMEM((D, width), F32)],
        flops=2 * LEN * D * width * steps,
        aliases=aliases,
    )(place, *operands)


class Place:
    def __init__(self, replicas, shards):
        self.replicas, self.shards, self.depth = replicas, shards, replicas // 4
        replica = lax.axis_index("replica")
        self.index = [replica % 2, replica // 2 % 2, replica // 4, lax.axis_index("shard")]
        self.core, self.x, self.z, self.y = self.index
        self.z_bits = self.depth.bit_length() - 1
        self.index += [self.z >> bit & 1 for bit in range(self.z_bits)]
        self.vector = jnp.stack(self.index).astype(jnp.int32)

    def shard(self, value, mask):
        return lax.ppermute(value, "shard", [(i, i ^ mask) for i in range(self.shards)])

    def cross(self, value, dy, dx):
        def partner(i):
            replica, shard = divmod(i, self.shards)
            return (replica ^ (2 * dx)) * self.shards + (shard ^ dy)

        pairs = [(i, partner(i)) for i in range(self.replicas * self.shards)]
        return lax.ppermute(value, ("replica", "shard"), pairs)

    def replica(self, value, mask):
        return lax.ppermute(value, "replica", [(i, i ^ mask) for i in range(self.replicas)])


def tie(value, *first):
    return lax.optimization_barrier((value,) + first)[0]


def pick(options, index):
    chosen = options[-1]
    for at in range(len(options) - 2, -1, -1):
        chosen = jnp.where(index == at, options[at], chosen)
    return chosen


def gather_shards(value, at):
    found = {0: value}
    mask = 1
    while mask < at.shards:
        for d in range(mask):
            found[d | mask] = at.shard(found[d], mask)
        mask *= 2
    return [found[d] for d in range(at.shards)]


def half_rows(weight, at):
    half = weight.shape[0] // 2
    return lax.dynamic_slice_in_dim(weight, at.core * half, half, 0)


def weight_pieces(weight, near, at):
    pieces = [weight]
    for block in near[1:]:
        pieces += [block, at.replica(block, 1)]
    return pieces


def exchange_pieces(parts, at):
    return [parts[0]] + [at.cross(parts[n], *divmod(n, 2)) for n in range(1, len(parts))]


def exchange_shards(parts, at):
    mask = at.shards // 2
    while mask > 1:
        parts = [
            rounded(as_float(parts[d]) + as_float(at.shard(parts[d | mask], mask)))
            for d in range(mask)
        ]
        mask //= 2
    return parts[0], at.shard(parts[1], 1)


def row_block(rows, block):
    return pl.BlockSpec((rows, CHUNK), lambda i, p: (block(p), 0))


def add_job(at, groups, parts, block, plain_block):
    heights = [rows // parts for _, rows, _ in groups]
    if any(h % 16 or first % h for h, (_, _, first) in zip(heights, groups)):
        found = []
        for n in range(parts):
            cuts = []
            for (terms, _, first), h in zip(groups, heights):
                start = first + plain_block(n) * h
                cut = [as_float(lax.dynamic_slice_in_dim(t, start, h, 0)) for t in terms]
                cuts.append(rounded(sum(cut)))
            found.append(jnp.concatenate(cuts) if len(cuts) > 1 else cuts[0])
        return found
    count = sum(len(terms) for terms, _, _ in groups)

    def body(place, ins, outs):
        for n in range(parts):
            at_term, row = n * count, 0
            for (terms, _, _), h in zip(groups, heights):
                total = as_float(ins[at_term][...])
                for term in range(1, len(terms)):
                    total += as_float(ins[at_term + term][...])
                outs[n][row : row + h, :] = rounded(total)
                at_term, row = at_term + len(terms), row + h

    specs, operands = [], []
    for n in range(parts):
        for (terms, _, first), h in zip(groups, heights):
            where = lambda p, n=n, base=first // h: base + block(n, p)
            specs += [row_block(h, where)] * len(terms)
            operands += terms
    results = [jax.ShapeDtypeStruct((sum(heights), CHUNK), LOW)] * parts
    return body, operands, specs, results


def all_rows(terms):
    return terms, terms[0].shape[0], 0


def halve(at, which, *groups):
    return add_job(
        at,
        groups,
        2,
        lambda n, p: jnp.bitwise_xor(p[which], n),
        lambda n: at.index[which] ^ n,
    )


def add_small(value, got):
    def body(place, ins, outs):
        outs[0][...] = ins[0][...] + ins[1][...]

    spec = constant(value.shape)
    return body, [value, got], [spec, spec], [jax.ShapeDtypeStruct(value.shape, F32)]


def split_z(at, terms):
    return add_job(
        at, [all_rows(terms)], at.depth, lambda n, p: jnp.bitwise_xor(p[Z], n), lambda n: at.z ^ n
    )


def total(at, terms):
    return add_job(at, [all_rows(terms)], 1, lambda n, p: 0, lambda n: 0)


def join(at, pieces, block, plain_block):
    rows = pieces[0].shape[0]
    count = len(pieces)
    if rows % 16:
        where = [plain_block(n) for n in range(count)]
        joined = []
        for j in range(count):
            chosen = pieces[0]
            for n in range(1, count):
                chosen = jnp.where(where[n] == j, pieces[n], chosen)
            joined.append(chosen)
        return [jnp.concatenate(joined)]

    def body(place, ins, outs):
        for n in range(count):
            start = pl.multiple_of(block(n, place) * rows, 16)
            outs[0][pl.ds(start, rows), :] = ins[n][...]

    result = jax.ShapeDtypeStruct((rows * count, CHUNK), LOW)
    return body, list(pieces), [constant((rows, CHUNK))] * count, [result]


def join_z(at, pieces):
    return join(at, pieces, lambda n, p: jnp.bitwise_xor(p[Z], n), lambda n: at.z ^ n)


def bit_order(at):
    order = [0]
    for bit in reversed(range(at.z_bits)):
        order += [d | 1 << bit for d in order]
    return order


def join_bits(at, pieces):
    order, top = bit_order(at), at.z_bits - 1

    def place_of(n, bits):
        return sum((bits[bit] ^ (order[n] >> bit & 1)) << (top - bit) for bit in range(at.z_bits))

    return join(
        at,
        pieces,
        lambda n, p: place_of(n, [p[Z_BITS + bit] for bit in range(at.z_bits)]),
        lambda n: place_of(n, at.index[Z_BITS:]),
    )


def join_split(at, pieces):
    order = bit_order(at)
    return join(
        at, pieces, lambda n, p: jnp.bitwise_xor(p[Z], order[n]), lambda n: at.z ^ order[n]
    )


def run_jobs(at, *jobs):
    results = [job if isinstance(job, list) else None for job in jobs]
    todo = [n for n, job in enumerate(jobs) if not isinstance(job, list)]
    if todo:
        operands, specs, outs = [], [], []
        for n in todo:
            operands += jobs[n][1]
            specs += jobs[n][2]
            outs += jobs[n][3]

        def body(place, *refs):
            ins, outs = refs[: len(operands)], refs[len(operands) :]
            for n in todo:
                job_body, job_ins, _, job_outs = jobs[n]
                job_body(place, ins[: len(job_ins)], outs[: len(job_outs)])
                ins, outs = ins[len(job_ins) :], outs[len(job_outs) :]

        found = call(
            body,
            "exchange_step",
            outs,
            (1,),
            specs,
            [constant(out.shape) for out in outs],
        )(at.vector, *operands)
        for n in todo:
            count = len(jobs[n][3])
            results[n], found = list(found[:count]), found[count:]
    return results


def send_x(halves, at):
    return halves[0], at.replica(halves[1], 2)


def send_bit(halves, bit, at):
    return halves[0], at.replica(halves[1], 4 << bit)


def send_z(blocks, at):
    return [blocks[0]] + [at.replica(blocks[d], 4 * d) for d in range(1, at.depth)]


def spread_z(whole, at):
    return [whole] + [at.replica(whole, 4 * d) for d in range(1, at.depth)]


def spread_bit(found, bit, at):
    return found + [at.replica(piece, 4 << bit) for piece in found]


def spread_x(mine, at):
    return mine, at.replica(mine, 2)


def spread_core(mine, other, at):
    return [mine, other, at.replica(mine, 1), at.replica(other, 1)]


def finish_down_body(place, *refs):
    for index in range(4):

        @pl.when(pl.program_id(0) == index)
        def _(index=index):
            refs[4][...] = as_float(refs[index][...])


def finish_up_body(place, *refs, rows, blocks):
    sources, (up, out) = refs[:4], refs[4:]
    for index in range(4):

        @pl.when(pl.program_id(0) == index)
        def _(index=index):
            source = sources[index]
            for j in range(blocks):
                up[:, j * CHUNK : (j + 1) * CHUNK] = as_float(source[j * rows : (j + 1) * rows, :])
            out[...] = as_float(source[blocks * rows :, :])


def finish_down(at, sources):
    rows = FF // at.shards
    half = lambda i, p: jnp.bitwise_xor(p[X], i % 2)
    core = lambda i, p: jnp.bitwise_xor(p[CORE], i // 2)
    return call(
        finish_down_body,
        "finish_down",
        shape((rows, D), F32),
        (4,),
        [constant(source.shape) for source in sources],
        pl.BlockSpec((rows // 2, CHUNK), lambda i, p: (half(i, p), core(i, p))),
    )(at.vector, *sources)


def finish_up(at, sources):
    rows = D // at.shards
    blocks = FF // (4 * CHUNK)
    half = lambda i, p: jnp.bitwise_xor(p[X], i % 2)
    core = lambda i, p: jnp.bitwise_xor(p[CORE], i // 2)
    return call(
        functools.partial(finish_up_body, rows=rows, blocks=blocks),
        "finish_up",
        (shape((rows, FF), F32), shape((rows, D), F32)),
        (4,),
        [constant(source.shape) for source in sources],
        [
            pl.BlockSpec((rows, blocks * CHUNK), lambda i, p: (0, core(i, p) * 2 + half(i, p))),
            pl.BlockSpec((rows // 2, CHUNK), lambda i, p: (half(i, p), core(i, p))),
        ],
    )(at.vector, *sources)


def finish_attention_body(place, *refs, rows):
    sources, qkv = refs[:4], refs[4]
    half = rows // 2
    for index in range(4):
        source = sources[index]
        core = jnp.bitwise_xor(place[CORE], index // 2)
        start = pl.multiple_of(jnp.bitwise_xor(place[X], index % 2) * half, 16)
        for pair in range(HALF_PAIRS):
            value = as_float(source[pair * half : (pair + 1) * half, :])
            for part in range(3):
                lane = pl.multiple_of(part * D + (core * HALF_PAIRS + pair) * WIDE, WIDE)
                qkv[pl.ds(start, half), pl.ds(lane, WIDE)] = value[
                    :, part * WIDE : (part + 1) * WIDE
                ]


def finish_attention(at, sources):
    rows = D // at.shards
    return call(
        functools.partial(finish_attention_body, rows=rows),
        "finish_attention",
        shape((rows, 3 * D), F32),
        (1,),
        [constant(source.shape) for source in sources],
        constant((rows, 3 * D)),
    )(at.vector, *sources)


def local(
    replicas,
    shards,
    inputs,
    segments,
    w_qkv,
    b_qv,
    w_out,
    b_out,
    attn_gain,
    attn_shift,
    w_up,
    b_up,
    w_down,
    b_down,
    ffn_gain,
    ffn_shift,
    cotangent,
):
    at = Place(replicas, shards)
    place = at.vector
    segments = segments.reshape(LEN)

    near_qkv = gather_shards(half_rows(w_qkv, at), at)
    vectors = (b_qv, b_out, attn_gain, attn_shift, b_up, b_down, ffn_gain, ffn_shift)
    sizes = [vector.shape[0] for vector in vectors]
    small = gather_shards(jnp.concatenate(vectors), at)
    small = as_float(jnp.stack([pick(small, at.y ^ j) for j in range(shards)]))
    full, offset = [], 0
    for size in sizes:
        full.append(small[:, offset : offset + size].reshape(-1))
        offset += size
    full = jnp.concatenate(full).reshape(1, VECTORS)
    feature_q, feature_k = document_features(segments)
    forward_ranges = key_ranges(segments, FORWARD_ROWS)
    backward_ranges = key_ranges(segments, BACKWARD_ROWS)

    pieces_qkv = weight_pieces(w_qkv, near_qkv, at)
    half_out, half_up = (half_rows(w, at) for w in (w_out, w_up))
    half_out, half_up, *_ = lax.optimization_barrier((half_out, half_up, near_qkv[-1]))
    near_out, near_up = gather_shards(half_out, at), gather_shards(half_up, at)
    projected, weight_qkv = project(place, inputs, full, pieces_qkv)
    context, log_total = attn_fwd(
        forward_ranges, projected, feature_q, feature_k, 6
    )
    near_out, near_up, context = lax.optimization_barrier((near_out, near_up, context))
    half_down = tie(half_rows(w_down, at), near_up[-1])
    near_down = gather_shards(half_down, at)
    pieces_out = weight_pieces(w_out, near_out, at)
    pieces_up = weight_pieces(w_up, near_up, at)
    normal, inverse, low, activated, slope = up_block(
        place, context, inputs, full, pieces_out, pieces_up
    )
    near_down, activated = lax.optimization_barrier((near_down, activated))
    pieces_down = weight_pieces(w_down, near_down, at)
    layer_output, d_sum_two, d_down, d_up, sums_two = down_block(
        place, activated, slope, normal, cotangent, full, pieces_down
    )

    barrier = lax.optimization_barrier
    zero = lambda p: 0
    other_core, own_core = (lambda p: 1 - p[CORE]), (lambda p: p[CORE])
    other_half, own_half = (lambda p: 2 * (1 - p[CORE])), (lambda p: 2 * p[CORE])
    wide, packed_width = FF // 4, HALF_PAIRS * TRIPLE

    down_send = down_gradient(place, activated, d_down, True, shards)
    down_got = at.replica(down_send, 1)
    up_send = row_gradient(place, low, d_up, wide, other_half, 2, shards, 1)
    up_got = at.replica(up_send, 1)
    down_parts = down_gradient(place, activated, d_down, False, shards, down_got)
    down = exchange_shards(down_parts, at)
    up_parts = row_gradient(place, low, d_up, wide, own_half, 2, shards, 1, up_got, 1)
    up_parts, d_up = barrier((up_parts, d_up))
    d_sum_one, d_attended, d_context, sums_one = back_block(
        place, d_up, d_sum_two, normal, inverse, full, pieces_up, pieces_out
    )

    def attention_back(index, d_context):
        return attn_bwd(
            jnp.concatenate([backward_ranges, index.reshape(1)]),
            projected,
            context,
            d_context,
            log_total,
            feature_q,
            feature_k,
            HALF_PAIRS,
            HALF_PAIRS,
        )

    bits = at.z_bits
    pieces = 2 * shards
    out_send = row_gradient(place, context, d_attended, CHUNK, other_core, 1, shards, 1)
    out_got = at.replica(out_send, 1)
    down, out_send = barrier((down, out_send))
    (down,) = run_jobs(at, halve(at, X, all_rows(down)))
    up_parts = row_gradient(
        place,
        context,
        d_attended,
        CHUNK,
        own_core,
        1,
        shards,
        1,
        tie(out_got, down[0]),
        0,
        up_parts,
    )
    down = send_x(down, at)
    up = exchange_shards(up_parts, at)
    up_parts, d_context = barrier((up_parts, d_context))
    d_other, bias_other = attention_back(1 - at.core, d_context)
    down, d_other, d_context = barrier((down, d_other, d_context))
    (down,) = run_jobs(at, split_z(at, down))
    send = row_gradient(
        place, inputs, tie(d_other, down[0]), packed_width, zero, 1, pieces, 2
    )
    down = send_z(down, at)
    got = at.replica(send, 1)
    up, send, d_context = barrier((up, send, d_context))
    up_rows = FF // (2 * CHUNK) * (D // shards)
    (up,) = run_jobs(
        at, halve(at, X, (up, up_rows, 0), (up, D // shards, up_rows))
    )
    up = send_x(up, at)
    d_own, bias_own = attention_back(at.core, tie(d_context, up[0]))
    up, down, d_own, got = barrier((up, down, d_own, got))
    (up,) = run_jobs(at, halve(at, Z_BITS, all_rows(up)))
    parts = row_gradient(
        place, inputs, tie(d_own, up[0]), packed_width, zero, 1, pieces, 2, got
    )
    up = send_bit(up, 0, at)
    mine = exchange_pieces(parts, at)

    bias = jnp.concatenate(
        [pick([bias_own, bias_other], at.core), pick([bias_other, bias_own], at.core)], axis=1
    )
    sums_one, sums_two = sums_one[0], sums_two[0]
    grads = (
        bias.reshape(-1),
        sums_one[2 * D :],
        sums_one[:D],
        sums_one[D : 2 * D],
        sums_two[3 * D :],
        sums_two[2 * D : 3 * D],
        sums_two[:D],
        sums_two[D : 2 * D],
    )
    packed = jnp.concatenate([grad.reshape(shards, -1) for grad in grads], axis=1)
    packed = packed.reshape(shards, -1, 128)
    small = [lax.dynamic_index_in_dim(packed, at.y ^ d, 0, False) for d in range(shards)]
    mask = shards // 2
    while mask > 1:
        small = [small[d] + at.shard(small[d | mask], mask) for d in range(mask)]
        mask //= 2

    down, up, d_own, small, parts = barrier((down, up, d_own, small, parts))
    if bits > 1:
        down, up = run_jobs(at, total(at, down), halve(at, Z_BITS + 1, all_rows(up)))
        up = send_bit(up, 1, at)
        for bit in range(2, bits):
            (up,) = run_jobs(at, halve(at, Z_BITS + bit, all_rows(up)))
            up = send_bit(up, bit, at)
    else:
        (down,) = run_jobs(at, total(at, down))
    down, d_own = barrier((down, d_own))
    down = spread_bit(down, bits - 1, at)
    input_grad = input_gradient(
        place,
        weight_qkv,
        d_sum_one,
        [d_other, d_own],
        ((True, 0, HALF_PAIRS), (False, 0, HALF_PAIRS)),
    )
    down, up, input_grad = barrier((down, up, input_grad))
    (up,) = run_jobs(at, total(at, up))
    mine, up = barrier((mine, up))
    (mine,) = run_jobs(at, split_z(at, mine))
    mine = send_z(mine, at)
    for bit in reversed(range(bits - 1)):
        down = spread_bit(down, bit, at)
    up = spread_bit(up, bits - 1, at)
    small = (small[0], at.shard(small[1], 1))
    down, up, small, kept = barrier((down, up, small, mine[0]))
    down, small = run_jobs(at, join_split(at, down), add_small(*small))
    small = (small[0], at.replica(small[0], 1))
    mine, small, kept = barrier((mine, small, down))
    mine, small = run_jobs(at, total(at, mine), add_small(*small))
    down = spread_x(kept[0], at)
    mine = spread_z(mine[0], at)
    for bit in reversed(range(bits - 1)):
        up = spread_bit(up, bit, at)
    small = (small[0], at.replica(small[0], 2))
    up, small, kept = barrier((up, small, mine[0]))
    up, small = run_jobs(at, join_bits(at, up), add_small(*small))
    mine, up, small = barrier((mine, up, small))
    (mine,) = run_jobs(at, join_z(at, mine))
    mine = spread_x(mine[0], at)
    up = spread_x(up[0], at)
    small = (small[0], at.replica(small[0], 4))
    down, kept, small = barrier((down, mine[0], small))
    grad_w_down = finish_down(at, spread_core(*down, at))
    small = small[0] + small[1]
    for bit in range(1, bits):
        small = small + at.replica(small, 4 << bit)
    up, grad_w_down, small = barrier((up, grad_w_down, small))
    grad_w_up, grad_w_out = finish_up(at, spread_core(*up, at))
    mine, grad_w_up = barrier((mine, grad_w_up))
    grad_w_qkv = finish_attention(at, spread_core(*mine, at))

    packed = small.reshape(-1)
    owned, offset = [], 0
    for size in sizes:
        owned.append(packed[offset : offset + size])
        offset += size
    return (
        layer_output,
        input_grad,
        grad_w_qkv,
        owned[0],
        grad_w_out,
        owned[1],
        owned[2],
        owned[3],
        grad_w_up,
        owned[4],
        grad_w_down,
        owned[5],
        owned[6],
        owned[7],
    )


def solution(mesh):
    token, matrix, vector = P(("replica", "shard"), None), P("shard", None), P("shard")
    weights = (matrix, vector, matrix, vector, vector, vector)
    weights += (matrix, vector, matrix, vector, vector, vector)
    return jax.shard_map(
        functools.partial(local, mesh.shape["replica"], mesh.shape["shard"]),
        mesh=mesh,
        in_specs=(token, token) + weights + (token,),
        out_specs=(token, token) + weights,
        check_vma=False,
    )
```

```python
import functools

import jax
import jax.numpy as jnp
from jax import lax
from jax.experimental import pallas as pl
from jax.experimental.pallas import tpu as pltpu
from jax.sharding import PartitionSpec as P

D = 768
FF = 3072
HEADS = 12
HEAD_DIM = 64
LEN = 1024
PAIRS = HEADS // 2
HALF_PAIRS = PAIRS // 2
WIDE = 2 * HEAD_DIM
TRIPLE = 3 * WIDE
KEY_TILE = 128
FORWARD_ROWS = 128
BACKWARD_ROWS = 256
TOKEN_ROWS = 256
CHUNK = 384
BIG = float(2**30)
EPSILON = 1e-12
F32 = jnp.float32
LOW = jnp.bfloat16
B_QV, B_OUT, ATTN_GAIN, ATTN_SHIFT = 0, 2 * D, 3 * D, 4 * D
B_UP, B_DOWN, FFN_GAIN, FFN_SHIFT = 5 * D, 5 * D + FF, 6 * D + FF, 7 * D + FF
VECTORS = 8 * D + FF
CORE, X, Z, Y, Z_BITS = 0, 1, 2, 3, 4


def matmul(left, right):
    return jnp.dot(left, right, preferred_element_type=F32)


def matmul_right_t(left, right):
    return lax.dot_general(left, right, (((1,), (1,)), ((), ())), preferred_element_type=F32)


def matmul_left_t(left, right):
    return lax.dot_general(left, right, (((0,), (0,)), ((), ())), preferred_element_type=F32)


def as_float(value):
    return value.astype(F32)


def rounded(value):
    return value.astype(LOW)


def shape(dims, kind=LOW):
    return jax.ShapeDtypeStruct(dims, kind)


def constant(dims):
    return pl.BlockSpec(dims, lambda *at: (0,) * len(dims))


def tokens(width):
    return pl.BlockSpec((TOKEN_ROWS, width), lambda i, *place: (i, 0))


ANYWHERE = pl.BlockSpec(memory_space=pl.ANY)
LOCAL = pl.BlockSpec(memory_space=pltpu.VMEM)


def call(
    body, name, out_shape, grid, in_specs, out_specs, scratch=(), flops=0, exps=0, aliases=None
):
    return pl.pallas_call(
        body,
        out_shape=out_shape,
        grid_spec=pltpu.PrefetchScalarGridSpec(
            num_scalar_prefetch=1,
            grid=grid,
            in_specs=in_specs,
            out_specs=out_specs,
            scratch_shapes=list(scratch),
        ),
        cost_estimate=pl.CostEstimate(flops=flops, transcendentals=exps, bytes_accessed=1 << 20),
        input_output_aliases=aliases or {},
        name=name,
    )


def piece_rows(place, count, own_rows):
    half = own_rows // 2
    core, y = place[CORE], place[Y]
    found = [pl.multiple_of(y * own_rows, half)]
    for d in range(1, (count + 1) // 2):
        base = jnp.bitwise_xor(y, d) * own_rows
        found.append(pl.multiple_of(base + core * half, half))
        found.append(pl.multiple_of(base + (1 - core) * half, half))
    return found


def assemble(place, pieces, buffer, semaphores):
    starts = piece_rows(place, len(pieces), pieces[0].shape[0])
    return [
        pltpu.make_async_copy(
            piece, buffer.at[pl.ds(start, piece.shape[0]), :], semaphores.at[at]
        )
        for at, (piece, start) in enumerate(zip(pieces, starts))
    ]


def start_all(copies):
    for copy in copies:
        copy.start()


def wait_all(copies):
    for copy in copies:
        copy.wait()


def project_body(place, inputs, vectors, *refs):
    pieces, (projected, weight) = refs[:-2], refs[-2:]
    count = len(pieces) // 3
    starts = piece_rows(place, count, pieces[0].shape[0])
    for part in range(3):
        for at in range(count):
            block = pieces[part * count + at]
            rows = pl.ds(starts[at], block.shape[0])
            for j in range(2):
                lanes = slice(j * TRIPLE + part * WIDE, j * TRIPLE + (part + 1) * WIDE)
                weight[rows, lanes] = block[:, j * WIDE : (j + 1) * WIDE]
    first = pl.program_id(0) * 2 * WIDE
    bias = []
    for j in range(2):
        at = pl.multiple_of(first + j * WIDE, WIDE)
        bias.append(vectors[:, pl.ds(B_QV + at, WIDE)])
        bias.append(jnp.zeros((1, WIDE), F32))
        bias.append(vectors[:, pl.ds(B_QV + D + at, WIDE)])
    bias = jnp.concatenate(bias, axis=1)
    projected[...] = rounded(matmul(inputs[...], weight[...]) + bias)


def project(place, inputs, vectors, pieces):
    steps = PAIRS // 2
    column = pl.BlockSpec((LEN, 2 * TRIPLE), lambda i, p: (0, i))
    specs, operands = [], []
    for part in range(3):
        for piece in pieces:
            specs.append(
                pl.BlockSpec(
                    (piece.shape[0], 2 * WIDE), lambda i, p, part=part: (0, part * steps + i)
                )
            )
            operands.append(piece)
    return call(
        project_body,
        "project",
        (shape((LEN, 3 * D)), shape((D, 3 * D))),
        (steps,),
        [constant((LEN, D)), constant((1, VECTORS))] + specs,
        [column, pl.BlockSpec((D, 2 * TRIPLE), lambda i, p: (0, i))],
        flops=2 * LEN * D * 3 * D,
    )(place, inputs, vectors, *operands)


def key_ranges(segments, rows):
    tiles = segments.reshape(LEN // rows, rows)
    below = jnp.sum(segments[None, :] < tiles[:, :1], axis=1, dtype=jnp.int32)
    upto = jnp.sum(segments[None, :] <= tiles[:, -1:], axis=1, dtype=jnp.int32)
    start = below // KEY_TILE
    count = (upto + KEY_TILE - 1) // KEY_TILE - start
    return jnp.concatenate([start, count])
def document_features(segments):
    lane = jnp.arange(WIDE, dtype=jnp.int32) % HEAD_DIM
    hot = segments[:, None] == lane[None, :]
    q = jnp.where((lane < 16) & hot, 1.0, 0.0).astype(LOW)
    k = jnp.where(lane < 16, jnp.where(hot, 0.0, -BIG), jnp.where(lane < 19, 1.0, 0.0)).astype(LOW)
    return q,k
def stack_heads(pair, side_a, side_b, left):
    zero=jnp.zeros_like(pair)
    a=jnp.concatenate([jnp.where(left,pair,zero),side_a],axis=1)
    b=jnp.concatenate([jnp.where(left,zero,pair),side_b],axis=1)
    return jnp.concatenate([a,b],axis=0)


def fwd_body(ranges, packed, feature_q, feature_k, context, log_total, key_side, value_t, *, group):
    tiles=LEN//FORWARD_ROWS
    for g in range(group):
        at=3*WIDE*g
        key_side[g,:,:WIDE]=packed[:,at+WIDE:at+2*WIDE]
        key_side[g,:,WIDE:]=feature_k[...]
        value_t[g,:WIDE,:]=packed[:,at+2*WIDE:at+3*WIDE].T
        value_t[g,WIDE:,:]=jnp.ones((16,LEN),LOW)
    left=lax.broadcasted_iota(jnp.int32,(FORWARD_ROWS,WIDE),1)<HEAD_DIM
    def tile(index,carry):
        here=pl.ds(pl.multiple_of(index*FORWARD_ROWS,FORWARD_ROWS),FORWARD_ROWS)
        side=feature_q[here,:]
        zero=jnp.zeros_like(side)
        sa=jnp.where(left,side,zero); sb=jnp.where(left,zero,side)
        stats=[stack_heads(packed[here,3*WIDE*g:3*WIDE*g+WIDE]*jnp.asarray(HEAD_DIM**-0.5,LOW),sa,sb,left) for g in range(group)]
        start=pl.multiple_of(ranges[index]*KEY_TILE,KEY_TILE)
        def over(width):
            def run():
                span=pl.ds(start,width)
                ss=[matmul_right_t(key_side[g,span,:],stats[g]) for g in range(group)]
                for g in range(group):
                    s=ss[g]
                    m=jnp.max(s,axis=0,keepdims=True)
                    p=jnp.exp(s-m).astype(LOW)
                    o=matmul(value_t[g,:,span],p)
                    total=o[WIDE:WIDE+1,:]
                    inv=1.0/total
                    lse=m+jnp.log(total)
                    log_total[g,0:1,here]=lse[:,:FORWARD_ROWS]
                    log_total[g,1:2,here]=lse[:,FORWARD_ROWS:]
                    both=jnp.concatenate([o[:HEAD_DIM,:FORWARD_ROWS]*inv[:,:FORWARD_ROWS],o[HEAD_DIM:WIDE,FORWARD_ROWS:]*inv[:,FORWARD_ROWS:]],axis=0)
                    context[here,g*WIDE:(g+1)*WIDE]=both.T.astype(LOW)
            return run
        lax.switch(ranges[tiles+index]-1,[over(KEY_TILE*(n+1)) for n in range(LEN//KEY_TILE)])
        return carry
    lax.fori_loop(0,tiles,tile,0)

def attn_fwd(r,packed,fq,fk,group=2):
    whole=pl.BlockSpec((LEN,WIDE),lambda h,r:(0,0))
    return pl.pallas_call(lambda *a: fwd_body(*a,group=group),
        out_shape=(jax.ShapeDtypeStruct((LEN,D),LOW),jax.ShapeDtypeStruct((PAIRS,2,LEN),F32)),
        grid_spec=pltpu.PrefetchScalarGridSpec(num_scalar_prefetch=1,grid=(PAIRS//group,),
          in_specs=[pl.BlockSpec((LEN,3*WIDE*group),lambda h,r:(0,h)),whole,whole],
          out_specs=[pl.BlockSpec((LEN,WIDE*group),lambda h,r:(0,h)),pl.BlockSpec((group,2,LEN),lambda h,r:(h,0,0))],
          scratch_shapes=[pltpu.VMEM((group,LEN,2*WIDE),LOW),pltpu.VMEM((group,WIDE+16,LEN),LOW)]),
        name="attention_forward")(r,packed,fq,fk)

def bwd_body(ranges,packed,context,d_context,log_total,feature_q,feature_k,*refs,group,pieces):
    if pieces:
        inputs,refs=refs[0],refs[1:]
        out,total=refs[2],refs[-1]
    d_packed,bias_sums=refs[:2]
    key_side,value_side,key_t,d_key,d_value=refs[3:8] if pieces else refs[2:]
    tiles=LEN//BACKWARD_ROWS
    lane=lax.broadcasted_iota(jnp.int32,(LEN,WIDE),1)
    ones=jnp.where(lane%HEAD_DIM<3,1.0,0.0).astype(LOW)
    for g in range(group):
        at=3*WIDE*g
        keys=packed[:,at+WIDE:at+2*WIDE]
        key_side[g,:,:WIDE]=keys
        key_side[g,:,WIDE:]=feature_k[...]
        value_side[g,:,:WIDE]=packed[:,at+2*WIDE:at+3*WIDE]
        value_side[g,:,WIDE:]=ones
        key_t[g]=keys.T
    d_key[...]=jnp.zeros_like(d_key); d_value[...]=jnp.zeros_like(d_value)
    lane_q=lax.broadcasted_iota(jnp.int32,(BACKWARD_ROWS,WIDE),1)
    left=lane_q<HEAD_DIM; inner=lane_q%HEAD_DIM
    zero=jnp.zeros((BACKWARD_ROWS,WIDE),LOW)
    def spread(value,base):
        high=as_float(value.astype(LOW)); rest=value-high
        middle=as_float(rest.astype(LOW)); tail=rest-middle
        return jnp.where(inner==base,high,jnp.where(inner==base+1,middle,jnp.where(inner==base+2,tail,0.0))).astype(LOW)
    def tile(index,sums):
        here=pl.ds(pl.multiple_of(index*BACKWARD_ROWS,BACKWARD_ROWS),BACKWARD_ROWS)
        hot=feature_q[here,:]
        qs=[];gs=[]
        for g in range(group):
            queries=packed[here,3*WIDE*g:3*WIDE*g+WIDE]*jnp.asarray(HEAD_DIM**-0.5,LOW)
            logs=log_total[g,:,here]
            cols=jnp.concatenate([logs,jnp.zeros((6,BACKWARD_ROWS),F32)],axis=0).T
            lse=jnp.where(left,cols[:,0:1],cols[:,1:2])
            side=hot+spread(-lse,16)
            qs.append(stack_heads(queries,jnp.where(left,side,zero),jnp.where(left,zero,side),left))
            grad=d_context[here,g*WIDE:(g+1)*WIDE]
            product=as_float(grad)*as_float(context[here,g*WIDE:(g+1)*WIDE])
            dot_a=jnp.sum(jnp.where(left,product,0.0),axis=1,keepdims=True)
            dot_b=jnp.sum(jnp.where(left,0.0,product),axis=1,keepdims=True)
            side_g=spread(-jnp.where(left,dot_a,dot_b),0)
            gs.append(stack_heads(grad,jnp.where(left,side_g,zero),jnp.where(left,zero,side_g),left))
        start=pl.multiple_of(ranges[index]*KEY_TILE,KEY_TILE)
        def over(width):
            def run():
                span=pl.ds(start,width)
                for g in range(group):
                    p=jnp.exp(matmul_right_t(key_side[g,span,:],qs[g]))
                    dp=matmul_right_t(value_side[g,span,:],gs[g])
                    pb=p.astype(LOW); ds=(p*dp).astype(LOW)
                    d_value[g,span,:]+=matmul(pb,gs[g][:,:WIDE])
                    d_key[g,span,:]+=matmul(ds,qs[g][:,:WIDE])
                    dq=matmul(key_t[g,:,span],ds)
                    dq=jnp.concatenate([dq[:HEAD_DIM,:BACKWARD_ROWS],dq[HEAD_DIM:,BACKWARD_ROWS:]],axis=0)
                    d_packed[here,3*WIDE*g:3*WIDE*g+WIDE]=(dq.T*HEAD_DIM**-0.5).astype(LOW)
            return run
        lax.switch(ranges[tiles+index]-1,[over(KEY_TILE*(n+1)) for n in range(LEN//KEY_TILE)])
        return tuple(sums[g]+jnp.sum(as_float(d_packed[here,3*WIDE*g:3*WIDE*g+WIDE]),axis=0,keepdims=True) for g in range(group))
    sums=lax.fori_loop(0,tiles,tile,(jnp.zeros((1,WIDE),F32),)*group)
    for g in range(group):
        at=3*WIDE*g
        low=d_value[g].astype(LOW)
        d_packed[:,at+WIDE:at+2*WIDE]=d_key[g].astype(LOW)
        d_packed[:,at+2*WIDE:at+3*WIDE]=low
        bias_sums[0:1,g*WIDE:(g+1)*WIDE]=sums[g]
        bias_sums[1:2,g*WIDE:(g+1)*WIDE]=jnp.sum(as_float(low),axis=0,keepdims=True)
    if not pieces:
        return
    total[...]=matmul_left_t(inputs[...],d_packed[...])
    rows=D//pieces
    base=2*(LEN//BACKWARD_ROWS)+1
    x,y=ranges[base],ranges[base+1]
    for piece in range(pieces):
        dy,dx=divmod(piece,2)
        start=pl.multiple_of((jnp.bitwise_xor(y,dy)*2+jnp.bitwise_xor(x,dx))*rows,16)
        for j in range(group):
            here=slice(j*rows,(j+1)*rows)
            out[piece,here,:]=rounded(total[pl.ds(start,rows),j*CHUNK:(j+1)*CHUNK])


def attn_bwd(ranges,packed,ctx,dctx,lse,fq,fk,inputs,pieces):
    group=HALF_PAIRS
    whole=pl.BlockSpec((LEN,WIDE),lambda h,r:(0,0))
    half=2*(LEN//BACKWARD_ROWS)
    col=lambda w: pl.BlockSpec((LEN,w*group),lambda h,r:(0,r[half]+h))
    specs=[col(3*WIDE),col(WIDE),col(WIDE),pl.BlockSpec((group,2,LEN),lambda h,r:(r[half]+h,0,0)),whole,whole]
    operands=[packed,ctx,dctx,lse,fq,fk]
    outs=[shape((LEN,group*3*WIDE)),shape((2,group*WIDE),F32)]
    scratch=[pltpu.VMEM((group,LEN,2*WIDE),LOW)]*2+[pltpu.VMEM((group,WIDE,LEN),LOW)]+[pltpu.VMEM((group,LEN,WIDE),F32)]*2
    if pieces:
        specs.append(constant((LEN,D)))
        operands.append(inputs)
        outs.append(shape((pieces,group*(D//pieces),CHUNK)))
        scratch.append(pltpu.VMEM((D,group*CHUNK),F32))
    return pl.pallas_call(functools.partial(bwd_body,group=group,pieces=pieces),
        out_shape=outs,
        grid_spec=pltpu.PrefetchScalarGridSpec(num_scalar_prefetch=1,grid=(1,),
          in_specs=specs,
          out_specs=[constant(out.shape) for out in outs],
          scratch_shapes=scratch),
        name="attention_backward")(ranges,*operands)


def normalize(hidden):
    average = jnp.mean(hidden, axis=-1, keepdims=True)
    centered = hidden - average
    variance = jnp.mean(centered * centered, axis=-1, keepdims=True)
    inverse = lax.rsqrt(variance + EPSILON)
    return centered * inverse, inverse


def normalize_back(grad, normal, inverse):
    first = jnp.mean(grad, axis=-1, keepdims=True)
    second = jnp.mean(grad * normal, axis=-1, keepdims=True)
    return (grad - first - normal * second) * inverse


def column_sum(value):
    return jnp.sum(value, axis=0, keepdims=True)


def up_body(place, context, inputs, vectors, *refs):
    count = (len(refs) - 9) // 2
    out_pieces, up_pieces = refs[:count], refs[count : 2 * count]
    normal, inverse, low, activated, slope, w_out, w_up, out_sem, up_sem = refs[2 * count :]
    out_copies = assemble(place, out_pieces, w_out, out_sem)
    up_copies = assemble(place, up_pieces, w_up, up_sem)
    step = pl.program_id(0)

    @pl.when(step == 0)
    def _():
        start_all(out_copies)
        start_all(up_copies)
        wait_all(out_copies)

    attended = matmul(context[...], w_out[...]) + vectors[:, B_OUT : B_OUT + D]
    value, scale = normalize(as_float(inputs[...]) + attended)
    normal[...] = value
    inverse[...] = jnp.broadcast_to(scale, inverse.shape)
    normed = rounded(
        value * vectors[:, ATTN_GAIN : ATTN_GAIN + D] + vectors[:, ATTN_SHIFT : ATTN_SHIFT + D]
    )
    low[...] = normed

    @pl.when(step == 0)
    def _():
        wait_all(up_copies)

    for at in range(0, FF, D):
        up = matmul(normed, w_up[:, at : at + D]) + vectors[:, B_UP + at : B_UP + at + D]
        below = 0.5 + 0.5 * lax.erf(up * (0.5**0.5))
        density = jnp.exp(-0.5 * up * up) * 0.3989422804014327
        activated[:, at : at + D] = rounded(up * below)
        slope[:, at : at + D] = rounded(below + up * density)


def up_block(place, context, inputs, vectors, out_pieces, up_pieces):
    count = len(out_pieces)
    return call(
        up_body,
        "out_norm_up",
        (
            shape((LEN, D), F32),
            shape((LEN, WIDE), F32),
            shape((LEN, D)),
            shape((LEN, FF)),
            shape((LEN, FF)),
        ),
        (LEN // TOKEN_ROWS,),
        [tokens(D), tokens(D), constant((1, VECTORS))] + [ANYWHERE] * (2 * count),
        [tokens(D), tokens(WIDE), tokens(D), tokens(FF), tokens(FF)],
        [
            pltpu.VMEM((D, D), LOW),
            pltpu.VMEM((D, FF), LOW),
            pltpu.SemaphoreType.DMA((count,)),
            pltpu.SemaphoreType.DMA((count,)),
        ],
        flops=2 * LEN * D * (D + FF),
        exps=2 * LEN * FF,
    )(place, context, inputs, vectors, *out_pieces, *up_pieces)


def down_body(place, activated, slope, normal, cotangent, vectors, *refs):
    count = len(refs) - 7
    pieces = refs[:count]
    output, d_sum, d_down, d_up, sums, w_down, sem = refs[count:]
    copies = assemble(place, pieces, w_down, sem)
    step = pl.program_id(0)

    @pl.when(step == 0)
    def _():
        start_all(copies)
        sums[...] = jnp.zeros_like(sums)
        wait_all(copies)

    down = matmul(activated[...], w_down[...]) + vectors[:, B_DOWN : B_DOWN + D]
    gain = vectors[:, ATTN_GAIN : ATTN_GAIN + D]
    normed = normal[...] * gain + vectors[:, ATTN_SHIFT : ATTN_SHIFT + D]
    value, scale = normalize(normed + down)
    gain = vectors[:, FFN_GAIN : FFN_GAIN + D]
    output[...] = rounded(value * gain + vectors[:, FFN_SHIFT : FFN_SHIFT + D])
    grad = as_float(cotangent[...])
    sums[:, :D] += column_sum(grad * value)
    sums[:, D : 2 * D] += column_sum(grad)
    d_two = normalize_back(grad * gain, value, scale)
    d_sum[...] = d_two
    d_low = rounded(d_two)
    d_down[...] = d_low
    sums[:, 2 * D : 3 * D] += column_sum(as_float(d_low))
    for at in range(0, FF, D):
        d_activated = matmul_right_t(d_low, w_down[at : at + D, :])
        part = rounded(d_activated * as_float(slope[:, at : at + D]))
        d_up[:, at : at + D] = part
        sums[:, 3 * D + at : 4 * D + at] += column_sum(as_float(part))


def down_block(place, activated, slope, normal, cotangent, vectors, pieces):
    count = len(pieces)
    return call(
        down_body,
        "down_norm_back",
        (
            shape((LEN, D)),
            shape((LEN, D), F32),
            shape((LEN, D)),
            shape((LEN, FF)),
            shape((1, 3 * D + FF), F32),
        ),
        (LEN // TOKEN_ROWS,),
        [tokens(FF), tokens(FF), tokens(D), tokens(D), constant((1, VECTORS))]
        + [ANYWHERE] * count,
        [tokens(D), tokens(D), tokens(D), tokens(FF), constant((1, 3 * D + FF))],
        [pltpu.VMEM((FF, D), LOW), pltpu.SemaphoreType.DMA((count,))],
        flops=4 * LEN * D * FF,
    )(place, activated, slope, normal, cotangent, vectors, *pieces)


def back_body(place, d_up, d_sum_two, normal, inverse, vectors, *refs, shards):
    context, refs = refs[0], refs[1:]
    count = (len(refs) - 8 - 2 * shards) // 2
    up_pieces, out_pieces = refs[:count], refs[count : 2 * count]
    refs = refs[2 * count :]
    d_sum, d_context, sums = refs[:3]
    sends, keeps = refs[3 : 3 + shards], refs[3 + shards : 3 + 2 * shards]
    w_up, w_out, total, up_sem, out_sem = refs[-5:]
    up_copies = assemble(place, up_pieces, w_up, up_sem)
    out_copies = assemble(place, out_pieces, w_out, out_sem)
    step = pl.program_id(0)

    @pl.when(step == 0)
    def _():
        start_all(up_copies)
        start_all(out_copies)
        sums[...] = jnp.zeros_like(sums)
        wait_all(up_copies)
        wait_all(out_copies)

    d_normed = d_sum_two[...] + matmul_right_t(d_up[...], w_up[...])
    value = normal[...]
    sums[:, :D] += column_sum(d_normed * value)
    sums[:, D : 2 * D] += column_sum(d_normed)
    d_one = normalize_back(
        d_normed * vectors[:, ATTN_GAIN : ATTN_GAIN + D], value, inverse[:, :1]
    )
    d_sum[...] = d_one
    low = rounded(d_one)
    sums[:, 2 * D :] += column_sum(as_float(low))
    d_context[...] = rounded(matmul_right_t(low, w_out[...]))
    product = matmul_left_t(context[...], low)

    @pl.when(step == 0)
    def _():
        total[...] = product

    @pl.when(step > 0)
    def _():
        total[...] += product

    @pl.when(step == pl.num_programs(0) - 1)
    def _():
        rows = D // shards
        for d in range(shards):
            start = pl.multiple_of(jnp.bitwise_xor(place[Y], d) * rows, 16)
            for out, core in ((sends[d], 1 - place[CORE]), (keeps[d], place[CORE])):
                lane = pl.multiple_of(core * CHUNK, WIDE)
                out[...] = rounded(total[pl.ds(start, rows), pl.ds(lane, CHUNK)])


def back_block(
    place, d_up, d_sum_two, normal, inverse, vectors, context, up_pieces, out_pieces, shards
):
    count = len(up_pieces)
    half = (D // shards, CHUNK)
    found = call(
        functools.partial(back_body, shards=shards),
        "norm_back",
        [shape((LEN, D), F32), shape((LEN, D)), shape((1, 3 * D), F32)]
        + [shape(half)] * (2 * shards),
        (LEN // TOKEN_ROWS,),
        [tokens(FF), tokens(D), tokens(D), tokens(WIDE), constant((1, VECTORS)), tokens(D)]
        + [ANYWHERE] * (2 * count),
        [tokens(D), tokens(D), constant((1, 3 * D))] + [constant(half)] * (2 * shards),
        [
            pltpu.VMEM((D, FF), LOW),
            pltpu.VMEM((D, D), LOW),
            pltpu.VMEM((D, D), F32),
            pltpu.SemaphoreType.DMA((count,)),
            pltpu.SemaphoreType.DMA((count,)),
        ],
        flops=2 * LEN * D * (FF + 2 * D),
    )(place, d_up, d_sum_two, normal, inverse, vectors, context, *up_pieces, *out_pieces)
    return found[0], found[1], found[2], found[3 : 3 + shards], found[3 + shards :]


def input_body(place, weight, d_sum, *refs, spans):
    output, pieces = refs[-1], refs[:-1]
    total = d_sum[...]
    for piece, (partner, first, count) in zip(pieces, spans):
        block = 1 - place[CORE] if partner else place[CORE]
        at = pl.multiple_of((first + block * count) * TRIPLE, WIDE)
        total += matmul_right_t(piece[...], weight[:, pl.ds(at, count * TRIPLE)])
    output[...] = rounded(total)


def input_gradient(place, weight, d_sum, pieces, spans):
    return call(
        functools.partial(input_body, spans=spans),
        "input_gradient",
        shape((LEN, D)),
        (LEN // TOKEN_ROWS,),
        [constant((D, 3 * D)), tokens(D)] + [tokens(piece.shape[1]) for piece in pieces],
        tokens(D),
        flops=6 * LEN * D * D,
    )(place, weight, d_sum, *pieces)


def piece_row(place, piece, rows, cuts):
    dy, dx = divmod(piece, cuts)
    start = jnp.bitwise_xor(place[Y], dy) * (cuts * rows)
    if cuts == 2:
        start += jnp.bitwise_xor(place[X], dx) * rows
    return pl.multiple_of(start, 16)


def down_gradient_body(place, left, right, *refs, shards, adds):
    value = matmul_left_t(left[...], right[...])
    if not adds:
        refs[0][0] = rounded(value)
        return
    value = rounded(value + as_float(refs[0][0]))
    for at in range(shards):

        @pl.when(pl.program_id(0) == at)
        def _(at=at):
            refs[1 + at][...] = value


def down_gradient(place, activated, d_down, partner, shards, got=None):
    rows = FF // shards
    pick_column = lambda i, p: (0, 1 - p[CORE] if partner else p[CORE])
    one = pl.BlockSpec((1, rows, CHUNK), lambda i, p: (i, 0, 0))
    operands, specs = [activated, d_down], []
    if got is None:
        outs, out_specs = shape((shards, rows, CHUNK)), one
    else:
        operands.append(got)
        specs.append(one)
        outs, out_specs = (shape((rows, CHUNK)),) * shards, [constant((rows, CHUNK))] * shards
    return call(
        functools.partial(down_gradient_body, shards=shards, adds=got is not None),
        "down_gradient",
        outs,
        (shards,),
        [
            pl.BlockSpec((LEN, rows), lambda i, p: (0, jnp.bitwise_xor(p[Y], i))),
            pl.BlockSpec((LEN, CHUNK), pick_column),
        ]
        + specs,
        out_specs,
        flops=LEN * D * FF,
    )(place, *operands)


def row_gradient_body(place, left, right, *refs, pieces, cuts, adds, extends):
    got, refs = (refs[0], refs[1:]) if adds else (None, refs)
    outs, total = refs[pieces if extends else 0 : -1], refs[-1]
    rows = D // pieces
    total[...] = matmul_left_t(left[...], right[...])
    for j in range(right.shape[1] // CHUNK):
        here = slice(j * rows, (j + 1) * rows)
        for piece in range(pieces):
            start = piece_row(place, piece, rows, cuts)
            value = total[pl.ds(start, rows), j * CHUNK : (j + 1) * CHUNK]
            if adds:
                outs[piece][here, :] = rounded(value + as_float(got[piece, here, :]))
            else:
                outs[0][piece, here, :] = rounded(value)


def row_gradient(
    place, left, right, width, first, steps, pieces, cuts, got=None, spare=0, into=None
):
    rows = D // pieces
    block = width // CHUNK * rows
    specs = [
        constant((LEN, D)),
        pl.BlockSpec((LEN, width), lambda i, p: (0, first(p) + i)),
    ]
    operands, aliases, at = [left, right], {}, 0
    if got is None:
        outs = shape((pieces, steps * block, CHUNK))
        out_specs = pl.BlockSpec((pieces, block, CHUNK), lambda i, p: (0, i, 0))
    else:
        specs.append(pl.BlockSpec((pieces, block, CHUNK), lambda i, p: (0, i, 0)))
        operands.append(got)
        height = steps * block + spare * rows
        if into is not None:
            height = into[0].shape[0]
            at = height // block - steps
            aliases = {len(operands) + 1 + n: n for n in range(pieces)}
            operands += into
            specs += [ANYWHERE] * pieces
        outs = (shape((height, CHUNK)),) * pieces
        out_specs = [pl.BlockSpec((block, CHUNK), lambda i, p: (at + i, 0))] * pieces
    return call(
        functools.partial(
            row_gradient_body,
            pieces=pieces,
            cuts=cuts,
            adds=got is not None,
            extends=into is not None,
        ),
        "row_gradient",
        outs,
        (steps,),
        specs,
        out_specs,
        [pltpu.VMEM((D, width), F32)],
        flops=2 * LEN * D * width * steps,
        aliases=aliases,
    )(place, *operands)


class Place:
    def __init__(self, replicas, shards):
        self.replicas, self.shards, self.depth = replicas, shards, replicas // 4
        replica = lax.axis_index("replica")
        self.index = [replica % 2, replica // 2 % 2, replica // 4, lax.axis_index("shard")]
        self.core, self.x, self.z, self.y = self.index
        self.z_bits = self.depth.bit_length() - 1
        self.index += [self.z >> bit & 1 for bit in range(self.z_bits)]
        self.vector = jnp.stack(self.index).astype(jnp.int32)

    def shard(self, value, mask):
        return lax.ppermute(value, "shard", [(i, i ^ mask) for i in range(self.shards)])

    def cross(self, value, dy, dx):
        def partner(i):
            replica, shard = divmod(i, self.shards)
            return (replica ^ (2 * dx)) * self.shards + (shard ^ dy)

        pairs = [(i, partner(i)) for i in range(self.replicas * self.shards)]
        return lax.ppermute(value, ("replica", "shard"), pairs)

    def replica(self, value, mask):
        return lax.ppermute(value, "replica", [(i, i ^ mask) for i in range(self.replicas)])


def tie(value, *first):
    return lax.optimization_barrier((value,) + first)[0]


def pick(options, index):
    chosen = options[-1]
    for at in range(len(options) - 2, -1, -1):
        chosen = jnp.where(index == at, options[at], chosen)
    return chosen


def gather_shards(value, at):
    found = {0: value}
    mask = 1
    while mask < at.shards:
        for d in range(mask):
            found[d | mask] = at.shard(found[d], mask)
        mask *= 2
    return [found[d] for d in range(at.shards)]


def half_rows(weight, at):
    half = weight.shape[0] // 2
    return lax.dynamic_slice_in_dim(weight, at.core * half, half, 0)


def weight_pieces(weight, near, at):
    pieces = [weight]
    for block in near[1:]:
        pieces += [block, at.replica(block, 1)]
    return pieces


def exchange_pieces(parts, at):
    return [parts[0]] + [at.cross(parts[n], *divmod(n, 2)) for n in range(1, len(parts))]


def exchange_shards(parts, at):
    mask = at.shards // 2
    while mask > 1:
        parts = [
            rounded(as_float(parts[d]) + as_float(at.shard(parts[d | mask], mask)))
            for d in range(mask)
        ]
        mask //= 2
    return parts[0], at.shard(parts[1], 1)


def add_job(at, groups, parts, block, plain_block):
    heights = [rows // parts for _, rows, _ in groups]
    if any(h % 16 or first % h for h, (_, _, first) in zip(heights, groups)):
        found = []
        for n in range(parts):
            cuts = []
            for (terms, _, first), h in zip(groups, heights):
                start = first + plain_block(n) * h
                cut = [as_float(lax.dynamic_slice_in_dim(t, start, h, 0)) for t in terms]
                cuts.append(rounded(sum(cut)))
            found.append(jnp.concatenate(cuts) if len(cuts) > 1 else cuts[0])
        return found

    def body(place, ins, outs):
        for n in range(parts):
            at_term, row = 0, 0
            for (terms, _, first), h in zip(groups, heights):
                here = pl.ds(pl.multiple_of(first + block(n, place) * h, 16), h)
                total = as_float(ins[at_term][here, :])
                for term in range(1, len(terms)):
                    total += as_float(ins[at_term + term][here, :])
                outs[n][row : row + h, :] = rounded(total)
                at_term, row = at_term + len(terms), row + h

    operands = [term for terms, _, _ in groups for term in terms]
    results = [jax.ShapeDtypeStruct((sum(heights), CHUNK), LOW)] * parts
    return body, operands, results


def all_rows(terms):
    return terms, terms[0].shape[0], 0


def halve(at, which, *groups):
    return add_job(
        at,
        groups,
        2,
        lambda n, p: jnp.bitwise_xor(p[which], n),
        lambda n: at.index[which] ^ n,
    )


def add_small(value, got):
    def body(place, ins, outs):
        outs[0][...] = ins[0][...] + ins[1][...]

    return body, [value, got], [jax.ShapeDtypeStruct(value.shape, F32)]


def split_z(at, terms):
    return add_job(
        at, [all_rows(terms)], at.depth, lambda n, p: jnp.bitwise_xor(p[Z], n), lambda n: at.z ^ n
    )


def total(at, terms):
    return add_job(at, [all_rows(terms)], 1, lambda n, p: 0, lambda n: 0)


def join(at, pieces, block, plain_block):
    rows = pieces[0].shape[0]
    count = len(pieces)
    if rows % 16:
        where = [plain_block(n) for n in range(count)]
        joined = []
        for j in range(count):
            chosen = pieces[0]
            for n in range(1, count):
                chosen = jnp.where(where[n] == j, pieces[n], chosen)
            joined.append(chosen)
        return [jnp.concatenate(joined)]

    def body(place, ins, outs):
        for n in range(count):
            start = pl.multiple_of(block(n, place) * rows, 16)
            outs[0][pl.ds(start, rows), :] = ins[n][...]

    result = jax.ShapeDtypeStruct((rows * count, CHUNK), LOW)
    return body, list(pieces), [result]


def join_z(at, pieces):
    return join(at, pieces, lambda n, p: jnp.bitwise_xor(p[Z], n), lambda n: at.z ^ n)


def bit_order(at):
    order = [0]
    for bit in reversed(range(at.z_bits)):
        order += [d | 1 << bit for d in order]
    return order


def join_bits(at, pieces):
    order, top = bit_order(at), at.z_bits - 1

    def place_of(n, bits):
        return sum((bits[bit] ^ (order[n] >> bit & 1)) << (top - bit) for bit in range(at.z_bits))

    return join(
        at,
        pieces,
        lambda n, p: place_of(n, [p[Z_BITS + bit] for bit in range(at.z_bits)]),
        lambda n: place_of(n, at.index[Z_BITS:]),
    )


def join_split(at, pieces):
    order = bit_order(at)
    return join(
        at, pieces, lambda n, p: jnp.bitwise_xor(p[Z], order[n]), lambda n: at.z ^ order[n]
    )


def kept_near(operands):
    return [pltpu.with_memory_space_constraint(value, pltpu.VMEM) for value in operands]


def run_jobs(at, *jobs, near=False):
    results = [job if isinstance(job, list) else None for job in jobs]
    todo = [n for n, job in enumerate(jobs) if not isinstance(job, list)]
    if todo:
        operands, outs = [], []
        for n in todo:
            operands += jobs[n][1]
            outs += jobs[n][2]

        def body(place, *refs):
            ins, outs = refs[: len(operands)], refs[len(operands) :]
            for n in todo:
                job_body, job_ins, job_outs = jobs[n]
                job_body(place, ins[: len(job_ins)], outs[: len(job_outs)])
                ins, outs = ins[len(job_ins) :], outs[len(job_outs) :]

        found = call(
            body,
            "exchange_step",
            outs,
            (1,),
            [LOCAL] * len(operands),
            [LOCAL] * len(outs),
        )(at.vector, *(kept_near(operands) if near else operands))
        for n in todo:
            count = len(jobs[n][2])
            results[n], found = list(found[:count]), found[count:]
    return results


def send_x(halves, at):
    return halves[0], at.replica(halves[1], 2)


def send_bit(halves, bit, at):
    return halves[0], at.replica(halves[1], 4 << bit)


def send_z(blocks, at):
    return [blocks[0]] + [at.replica(blocks[d], 4 * d) for d in range(1, at.depth)]


def spread_z(whole, at):
    return [whole] + [at.replica(whole, 4 * d) for d in range(1, at.depth)]


def spread_bit(found, bit, at):
    return found + [at.replica(piece, 4 << bit) for piece in found]


def spread_x(mine, at):
    return mine, at.replica(mine, 2)


def spread_core(mine, other, at):
    return [mine, other, at.replica(mine, 1), at.replica(other, 1)]


def finish_down_body(place, *refs):
    for index in range(4):

        @pl.when(pl.program_id(0) == index)
        def _(index=index):
            refs[4][...] = as_float(refs[index][...])


def finish_up_body(place, *refs, rows, blocks):
    sources, (up, out) = refs[:4], refs[4:]
    for index in range(4):

        @pl.when(pl.program_id(0) == index)
        def _(index=index):
            source = sources[index]
            for j in range(blocks):
                up[:, j * CHUNK : (j + 1) * CHUNK] = as_float(source[j * rows : (j + 1) * rows, :])
            out[...] = as_float(source[blocks * rows :, :])


def finish_down(at, sources):
    rows = FF // at.shards
    half = lambda i, p: jnp.bitwise_xor(p[X], i % 2)
    core = lambda i, p: jnp.bitwise_xor(p[CORE], i // 2)
    return call(
        finish_down_body,
        "finish_down",
        shape((rows, D), F32),
        (4,),
        [LOCAL] * len(sources),
        pl.BlockSpec((rows // 2, CHUNK), lambda i, p: (half(i, p), core(i, p))),
    )(at.vector, *sources)


def finish_up(at, sources):
    rows = D // at.shards
    blocks = FF // (4 * CHUNK)
    half = lambda i, p: jnp.bitwise_xor(p[X], i % 2)
    core = lambda i, p: jnp.bitwise_xor(p[CORE], i // 2)
    return call(
        functools.partial(finish_up_body, rows=rows, blocks=blocks),
        "finish_up",
        (shape((rows, FF), F32), shape((rows, D), F32)),
        (4,),
        [LOCAL] * len(sources),
        [
            pl.BlockSpec((rows, blocks * CHUNK), lambda i, p: (0, core(i, p) * 2 + half(i, p))),
            pl.BlockSpec((rows // 2, CHUNK), lambda i, p: (half(i, p), core(i, p))),
        ],
    )(at.vector, *sources)


def finish_attention_body(place, *refs, rows):
    sources, qkv = refs[:4], refs[4]
    half = rows // 2
    for index in range(4):
        source = sources[index]
        core = jnp.bitwise_xor(place[CORE], index // 2)
        start = pl.multiple_of(jnp.bitwise_xor(place[X], index % 2) * half, 16)
        for pair in range(HALF_PAIRS):
            value = as_float(source[pair * half : (pair + 1) * half, :])
            for part in range(3):
                lane = pl.multiple_of(part * D + (core * HALF_PAIRS + pair) * WIDE, WIDE)
                qkv[pl.ds(start, half), pl.ds(lane, WIDE)] = value[
                    :, part * WIDE : (part + 1) * WIDE
                ]


def finish_attention(at, sources):
    rows = D // at.shards
    return call(
        functools.partial(finish_attention_body, rows=rows),
        "finish_attention",
        shape((rows, 3 * D), F32),
        (1,),
        [LOCAL] * len(sources),
        constant((rows, 3 * D)),
    )(at.vector, *kept_near(sources))


def local(
    replicas,
    shards,
    inputs,
    segments,
    w_qkv,
    b_qv,
    w_out,
    b_out,
    attn_gain,
    attn_shift,
    w_up,
    b_up,
    w_down,
    b_down,
    ffn_gain,
    ffn_shift,
    cotangent,
):
    at = Place(replicas, shards)
    place = at.vector
    segments = segments.reshape(LEN)

    near_qkv = gather_shards(half_rows(w_qkv, at), at)
    vectors = (b_qv, b_out, attn_gain, attn_shift, b_up, b_down, ffn_gain, ffn_shift)
    sizes = [vector.shape[0] for vector in vectors]
    small = gather_shards(jnp.concatenate(vectors), at)
    small = as_float(jnp.stack([pick(small, at.y ^ j) for j in range(shards)]))
    full, offset = [], 0
    for size in sizes:
        full.append(small[:, offset : offset + size].reshape(-1))
        offset += size
    full = jnp.concatenate(full).reshape(1, VECTORS)
    feature_q, feature_k = document_features(segments)
    forward_ranges = key_ranges(segments, FORWARD_ROWS)
    backward_ranges = key_ranges(segments, BACKWARD_ROWS)

    pieces_qkv = weight_pieces(w_qkv, near_qkv, at)
    half_out, half_up = (half_rows(w, at) for w in (w_out, w_up))
    half_out, half_up, *_ = lax.optimization_barrier((half_out, half_up, near_qkv[-1]))
    near_out, near_up = gather_shards(half_out, at), gather_shards(half_up, at)
    projected, weight_qkv = project(place, inputs, full, pieces_qkv)
    context, log_total = attn_fwd(
        forward_ranges, projected, feature_q, feature_k, 6
    )
    near_out, near_up, context = lax.optimization_barrier((near_out, near_up, context))
    half_down = tie(half_rows(w_down, at), near_up[-1])
    near_down = gather_shards(half_down, at)
    pieces_out = weight_pieces(w_out, near_out, at)
    pieces_up = weight_pieces(w_up, near_up, at)
    normal, inverse, low, activated, slope = up_block(
        place, context, inputs, full, pieces_out, pieces_up
    )
    near_down, activated = lax.optimization_barrier((near_down, activated))
    pieces_down = weight_pieces(w_down, near_down, at)
    layer_output, d_sum_two, d_down, d_up, sums_two = down_block(
        place, activated, slope, normal, cotangent, full, pieces_down
    )

    barrier = lax.optimization_barrier
    other_half, own_half = (lambda p: 2 * (1 - p[CORE])), (lambda p: 2 * p[CORE])
    wide = FF // 4

    down_send = down_gradient(place, activated, d_down, True, shards)
    down_got = at.replica(down_send, 1)
    up_send = row_gradient(place, low, d_up, wide, other_half, 2, shards, 1)
    up_got = at.replica(up_send, 1)
    down_parts = down_gradient(place, activated, d_down, False, shards, down_got)
    down = exchange_shards(down_parts, at)
    up_parts = row_gradient(place, low, d_up, wide, own_half, 2, shards, 1, up_got)
    up_parts, d_up = barrier((up_parts, d_up))
    d_sum_one, d_context, sums_one, out_sends, out_keeps = back_block(
        place, d_up, d_sum_two, normal, inverse, full, context, pieces_up, pieces_out, shards
    )

    def attention_back(half, d_context, pieces):
        return attn_bwd(
            jnp.concatenate([backward_ranges, jnp.stack([half, at.x, at.y]).astype(jnp.int32)]),
            projected,
            context,
            d_context,
            log_total,
            feature_q,
            feature_k,
            inputs,
            pieces,
        )

    bits = at.z_bits
    pieces = 2 * shards
    out_gots = [at.replica(send, 1) for send in out_sends]
    down, out_keeps = barrier((down, out_keeps))
    down, *out_parts = run_jobs(
        at,
        halve(at, X, all_rows(down)),
        *[total(at, [keep, got]) for keep, got in zip(out_keeps, out_gots)],
    )
    down = send_x(down, at)
    out_parts, up_parts = barrier(([part[0] for part in out_parts], up_parts))
    up, out = exchange_shards(up_parts, at), exchange_shards(out_parts, at)
    out_parts, up_parts, d_context = barrier((out_parts, up_parts, d_context))
    d_other, bias_other, send = attention_back(1 - at.core, d_context, pieces)
    got = at.replica(send, 1)
    down, up, out, d_other, d_context = barrier((down, up, out, d_other, d_context))
    down, up = run_jobs(at, split_z(at, down), halve(at, X, all_rows(up), all_rows(out)))
    down = send_z(down, at)
    up = send_x(up, at)
    d_own, bias_own = attention_back(at.core, tie(d_context, up[0]), 0)
    up, down, d_own, got = barrier((up, down, d_own, got))
    (up,) = run_jobs(at, halve(at, Z_BITS, all_rows(up)), near=True)
    parts = row_gradient(
        place, inputs, tie(d_own, up[0]), HALF_PAIRS * TRIPLE, lambda p: 0, 1, pieces, 2, got
    )
    up = send_bit(up, 0, at)
    mine = exchange_pieces(parts, at)

    bias = jnp.concatenate(
        [pick([bias_own, bias_other], at.core), pick([bias_other, bias_own], at.core)], axis=1
    )
    sums_one, sums_two = sums_one[0], sums_two[0]
    grads = (
        bias.reshape(-1),
        sums_one[2 * D :],
        sums_one[:D],
        sums_one[D : 2 * D],
        sums_two[3 * D :],
        sums_two[2 * D : 3 * D],
        sums_two[:D],
        sums_two[D : 2 * D],
    )
    packed = jnp.concatenate([grad.reshape(shards, -1) for grad in grads], axis=1)
    packed = packed.reshape(shards, -1, 128)
    small = [lax.dynamic_index_in_dim(packed, at.y ^ d, 0, False) for d in range(shards)]
    mask = shards // 2
    while mask > 1:
        small = [small[d] + at.shard(small[d | mask], mask) for d in range(mask)]
        mask //= 2

    down, up, d_own, small, parts = barrier((down, up, d_own, small, parts))
    if bits > 1:
        down, up = run_jobs(at, total(at, down), halve(at, Z_BITS + 1, all_rows(up)))
        up = send_bit(up, 1, at)
        for bit in range(2, bits):
            (up,) = run_jobs(at, halve(at, Z_BITS + bit, all_rows(up)))
            up = send_bit(up, bit, at)
    else:
        (down,) = run_jobs(at, total(at, down))
    down, d_own = barrier((down, d_own))
    down = spread_bit(down, bits - 1, at)
    input_grad = input_gradient(
        place,
        weight_qkv,
        d_sum_one,
        [d_other, d_own],
        ((True, 0, HALF_PAIRS), (False, 0, HALF_PAIRS)),
    )
    down, up, input_grad = barrier((down, up, input_grad))
    (up,) = run_jobs(at, total(at, up), near=True)
    mine, up = barrier((mine, up))
    (mine,) = run_jobs(at, split_z(at, mine), near=True)
    mine = send_z(mine, at)
    for bit in reversed(range(bits - 1)):
        down = spread_bit(down, bit, at)
    up = spread_bit(up, bits - 1, at)
    small = (small[0], at.shard(small[1], 1))
    down, up, small, kept = barrier((down, up, small, mine[0]))
    down, small = run_jobs(at, join_split(at, down), add_small(*small), near=True)
    small = (small[0], at.replica(small[0], 1))
    mine, small, kept = barrier((mine, small, down))
    mine, small = run_jobs(at, total(at, mine), add_small(*small), near=True)
    down = spread_x(kept[0], at)
    mine = spread_z(mine[0], at)
    for bit in reversed(range(bits - 1)):
        up = spread_bit(up, bit, at)
    small = (small[0], at.replica(small[0], 2))
    up, small, kept = barrier((up, small, mine[0]))
    up, small = run_jobs(at, join_bits(at, up), add_small(*small), near=True)
    mine, up, small = barrier((mine, up, small))
    (mine,) = run_jobs(at, join_z(at, mine), near=True)
    mine = spread_x(mine[0], at)
    up = spread_x(up[0], at)
    small = [small[0]] + [at.replica(small[0], 4 * d) for d in range(1, at.depth)]
    down, kept = barrier((down, mine[0]))
    grad_w_down = finish_down(at, spread_core(*down, at))
    up, grad_w_down, small = barrier((up, grad_w_down, small))
    small = sum(small)
    grad_w_up, grad_w_out = finish_up(at, spread_core(*up, at))
    mine, grad_w_up = barrier((mine, grad_w_up))
    grad_w_qkv = finish_attention(at, spread_core(*mine, at))

    packed = small.reshape(-1)
    owned, offset = [], 0
    for size in sizes:
        owned.append(packed[offset : offset + size])
        offset += size
    return (
        layer_output,
        input_grad,
        grad_w_qkv,
        owned[0],
        grad_w_out,
        owned[1],
        owned[2],
        owned[3],
        grad_w_up,
        owned[4],
        grad_w_down,
        owned[5],
        owned[6],
        owned[7],
    )


def solution(mesh):
    token, matrix, vector = P(("replica", "shard"), None), P("shard", None), P("shard")
    weights = (matrix, vector, matrix, vector, vector, vector)
    weights += (matrix, vector, matrix, vector, vector, vector)
    return jax.shard_map(
        functools.partial(local, mesh.shape["replica"], mesh.shape["shard"]),
        mesh=mesh,
        in_specs=(token, token) + weights + (token,),
        out_specs=(token, token) + weights,
        check_vma=False,
    )
```

```python
import functools

import jax
import jax.numpy as jnp
from jax import lax
from jax.experimental import pallas as pl
from jax.experimental.pallas import tpu as pltpu
from jax.sharding import PartitionSpec as P

D = 768
FF = 3072
HEADS = 12
HEAD_DIM = 64
LEN = 1024
PAIRS = HEADS // 2
HALF_PAIRS = PAIRS // 2
WIDE = 2 * HEAD_DIM
TRIPLE = 3 * WIDE
KEY_TILE = 128
FORWARD_ROWS = 128
BACKWARD_ROWS = 256
TOKEN_ROWS = 256
CHUNK = 384
BIG = float(2**30)
EPSILON = 1e-12
F32 = jnp.float32
LOW = jnp.bfloat16
B_QV, B_OUT, ATTN_GAIN, ATTN_SHIFT = 0, 2 * D, 3 * D, 4 * D
B_UP, B_DOWN, FFN_GAIN, FFN_SHIFT = 5 * D, 5 * D + FF, 6 * D + FF, 7 * D + FF
VECTORS = 8 * D + FF
CORE, X, Z, Y, Z_BITS = 0, 1, 2, 3, 4


def matmul(left, right):
    return jnp.dot(left, right, preferred_element_type=F32)


def matmul_right_t(left, right):
    return lax.dot_general(left, right, (((1,), (1,)), ((), ())), preferred_element_type=F32)


def matmul_left_t(left, right):
    return lax.dot_general(left, right, (((0,), (0,)), ((), ())), preferred_element_type=F32)


def as_float(value):
    return value.astype(F32)


def rounded(value):
    return value.astype(LOW)


def shape(dims, kind=LOW):
    return jax.ShapeDtypeStruct(dims, kind)


def constant(dims):
    return pl.BlockSpec(dims, lambda *at: (0,) * len(dims))


def tokens(width):
    return pl.BlockSpec((TOKEN_ROWS, width), lambda i, *place: (i, 0))


ANYWHERE = pl.BlockSpec(memory_space=pl.ANY)
LOCAL = pl.BlockSpec(memory_space=pltpu.VMEM)


def call(
    body, name, out_shape, grid, in_specs, out_specs, scratch=(), flops=0, exps=0, aliases=None
):
    return pl.pallas_call(
        body,
        out_shape=out_shape,
        grid_spec=pltpu.PrefetchScalarGridSpec(
            num_scalar_prefetch=1,
            grid=grid,
            in_specs=in_specs,
            out_specs=out_specs,
            scratch_shapes=list(scratch),
        ),
        cost_estimate=pl.CostEstimate(flops=flops, transcendentals=exps, bytes_accessed=1 << 20),
        input_output_aliases=aliases or {},
        name=name,
    )


def piece_rows(place, count, own_rows):
    half = own_rows // 2
    core, y = place[CORE], place[Y]
    found = [pl.multiple_of(y * own_rows, half)]
    for d in range(1, (count + 1) // 2):
        base = jnp.bitwise_xor(y, d) * own_rows
        found.append(pl.multiple_of(base + core * half, half))
        found.append(pl.multiple_of(base + (1 - core) * half, half))
    return found


def assemble(place, pieces, buffer, semaphores):
    starts = piece_rows(place, len(pieces), pieces[0].shape[0])
    return [
        pltpu.make_async_copy(
            piece, buffer.at[pl.ds(start, piece.shape[0]), :], semaphores.at[at]
        )
        for at, (piece, start) in enumerate(zip(pieces, starts))
    ]


def start_all(copies):
    for copy in copies:
        copy.start()


def wait_all(copies):
    for copy in copies:
        copy.wait()


def project_body(place, inputs, vectors, *refs):
    pieces, (projected, weight) = refs[:-2], refs[-2:]
    count = len(pieces) // 3
    starts = piece_rows(place, count, pieces[0].shape[0])
    for part in range(3):
        for at in range(count):
            block = pieces[part * count + at]
            rows = pl.ds(starts[at], block.shape[0])
            for j in range(2):
                lanes = slice(j * TRIPLE + part * WIDE, j * TRIPLE + (part + 1) * WIDE)
                weight[rows, lanes] = block[:, j * WIDE : (j + 1) * WIDE]
    first = pl.program_id(0) * 2 * WIDE
    bias = []
    for j in range(2):
        at = pl.multiple_of(first + j * WIDE, WIDE)
        bias.append(vectors[:, pl.ds(B_QV + at, WIDE)])
        bias.append(jnp.zeros((1, WIDE), F32))
        bias.append(vectors[:, pl.ds(B_QV + D + at, WIDE)])
    bias = jnp.concatenate(bias, axis=1)
    projected[...] = rounded(matmul(inputs[...], weight[...]) + bias)


def project(place, inputs, vectors, pieces):
    steps = PAIRS // 2
    column = pl.BlockSpec((LEN, 2 * TRIPLE), lambda i, p: (0, i))
    specs, operands = [], []
    for part in range(3):
        for piece in pieces:
            specs.append(
                pl.BlockSpec(
                    (piece.shape[0], 2 * WIDE), lambda i, p, part=part: (0, part * steps + i)
                )
            )
            operands.append(piece)
    return call(
        project_body,
        "project",
        (shape((LEN, 3 * D)), shape((D, 3 * D))),
        (steps,),
        [constant((LEN, D)), constant((1, VECTORS))] + specs,
        [column, pl.BlockSpec((D, 2 * TRIPLE), lambda i, p: (0, i))],
        flops=2 * LEN * D * 3 * D,
    )(place, inputs, vectors, *operands)


def key_ranges(segments, rows):
    tiles = segments.reshape(LEN // rows, rows)
    below = jnp.sum(segments[None, :] < tiles[:, :1], axis=1, dtype=jnp.int32)
    upto = jnp.sum(segments[None, :] <= tiles[:, -1:], axis=1, dtype=jnp.int32)
    start = below // KEY_TILE
    count = (upto + KEY_TILE - 1) // KEY_TILE - start
    return jnp.concatenate([start, count])
def document_features(segments):
    lane = jnp.arange(WIDE, dtype=jnp.int32) % HEAD_DIM
    hot = segments[:, None] == lane[None, :]
    q = jnp.where((lane < 16) & hot, 1.0, 0.0).astype(LOW)
    k = jnp.where(lane < 16, jnp.where(hot, 0.0, -BIG), jnp.where(lane < 19, 1.0, 0.0)).astype(LOW)
    return q,k
def stack_heads(pair, side_a, side_b, left):
    zero=jnp.zeros_like(pair)
    a=jnp.concatenate([jnp.where(left,pair,zero),side_a],axis=1)
    b=jnp.concatenate([jnp.where(left,zero,pair),side_b],axis=1)
    return jnp.concatenate([a,b],axis=0)


def fwd_body(ranges, packed, feature_q, feature_k, context, log_total, key_side, value_t, *, group):
    tiles=LEN//FORWARD_ROWS
    for g in range(group):
        at=3*WIDE*g
        key_side[g,:,:WIDE]=packed[:,at+WIDE:at+2*WIDE]
        key_side[g,:,WIDE:]=feature_k[...]
        value_t[g,:WIDE,:]=packed[:,at+2*WIDE:at+3*WIDE].T
        value_t[g,WIDE:,:]=jnp.ones((16,LEN),LOW)
    left=lax.broadcasted_iota(jnp.int32,(FORWARD_ROWS,WIDE),1)<HEAD_DIM
    def tile(index,carry):
        here=pl.ds(pl.multiple_of(index*FORWARD_ROWS,FORWARD_ROWS),FORWARD_ROWS)
        side=feature_q[here,:]
        zero=jnp.zeros_like(side)
        sa=jnp.where(left,side,zero); sb=jnp.where(left,zero,side)
        stats=[stack_heads(packed[here,3*WIDE*g:3*WIDE*g+WIDE]*jnp.asarray(HEAD_DIM**-0.5,LOW),sa,sb,left) for g in range(group)]
        start=pl.multiple_of(ranges[index]*KEY_TILE,KEY_TILE)
        def over(width):
            def run():
                span=pl.ds(start,width)
                ss=[matmul_right_t(key_side[g,span,:],stats[g]) for g in range(group)]
                for g in range(group):
                    s=ss[g]
                    m=jnp.max(s,axis=0,keepdims=True)
                    p=jnp.exp(s-m).astype(LOW)
                    o=matmul(value_t[g,:,span],p)
                    total=o[WIDE:WIDE+1,:]
                    inv=1.0/total
                    lse=m+jnp.log(total)
                    log_total[g,0:1,here]=lse[:,:FORWARD_ROWS]
                    log_total[g,1:2,here]=lse[:,FORWARD_ROWS:]
                    both=jnp.concatenate([o[:HEAD_DIM,:FORWARD_ROWS]*inv[:,:FORWARD_ROWS],o[HEAD_DIM:WIDE,FORWARD_ROWS:]*inv[:,FORWARD_ROWS:]],axis=0)
                    context[here,g*WIDE:(g+1)*WIDE]=both.T.astype(LOW)
            return run
        lax.switch(ranges[tiles+index]-1,[over(KEY_TILE*(n+1)) for n in range(LEN//KEY_TILE)])
        return carry
    lax.fori_loop(0,tiles,tile,0)

def attn_fwd(r,packed,fq,fk,group=2):
    whole=pl.BlockSpec((LEN,WIDE),lambda h,r:(0,0))
    return pl.pallas_call(lambda *a: fwd_body(*a,group=group),
        out_shape=(jax.ShapeDtypeStruct((LEN,D),LOW),jax.ShapeDtypeStruct((PAIRS,2,LEN),F32)),
        grid_spec=pltpu.PrefetchScalarGridSpec(num_scalar_prefetch=1,grid=(PAIRS//group,),
          in_specs=[pl.BlockSpec((LEN,3*WIDE*group),lambda h,r:(0,h)),whole,whole],
          out_specs=[pl.BlockSpec((LEN,WIDE*group),lambda h,r:(0,h)),pl.BlockSpec((group,2,LEN),lambda h,r:(h,0,0))],
          scratch_shapes=[pltpu.VMEM((group,LEN,2*WIDE),LOW),pltpu.VMEM((group,WIDE+16,LEN),LOW)]),
        name="attention_forward")(r,packed,fq,fk)

def bwd_body(ranges,packed,context,d_context,log_total,feature_q,feature_k,*refs,group,pieces):
    if pieces:
        inputs,refs=refs[0],refs[1:]
        out,total=refs[2],refs[-1]
    d_packed,bias_sums=refs[:2]
    key_side,value_side,key_t,d_key,d_value=refs[3:8] if pieces else refs[2:]
    tiles=LEN//BACKWARD_ROWS
    lane=lax.broadcasted_iota(jnp.int32,(LEN,WIDE),1)
    ones=jnp.where(lane%HEAD_DIM<3,1.0,0.0).astype(LOW)
    for g in range(group):
        at=3*WIDE*g
        keys=packed[:,at+WIDE:at+2*WIDE]
        key_side[g,:,:WIDE]=keys
        key_side[g,:,WIDE:]=feature_k[...]
        value_side[g,:,:WIDE]=packed[:,at+2*WIDE:at+3*WIDE]
        value_side[g,:,WIDE:]=ones
        key_t[g]=keys.T
    d_key[...]=jnp.zeros_like(d_key); d_value[...]=jnp.zeros_like(d_value)
    lane_q=lax.broadcasted_iota(jnp.int32,(BACKWARD_ROWS,WIDE),1)
    left=lane_q<HEAD_DIM; inner=lane_q%HEAD_DIM
    zero=jnp.zeros((BACKWARD_ROWS,WIDE),LOW)
    def spread(value,base):
        high=as_float(value.astype(LOW)); rest=value-high
        middle=as_float(rest.astype(LOW)); tail=rest-middle
        return jnp.where(inner==base,high,jnp.where(inner==base+1,middle,jnp.where(inner==base+2,tail,0.0))).astype(LOW)
    def tile(index,sums):
        here=pl.ds(pl.multiple_of(index*BACKWARD_ROWS,BACKWARD_ROWS),BACKWARD_ROWS)
        hot=feature_q[here,:]
        qs=[];gs=[]
        for g in range(group):
            queries=packed[here,3*WIDE*g:3*WIDE*g+WIDE]*jnp.asarray(HEAD_DIM**-0.5,LOW)
            logs=log_total[g,:,here]
            cols=jnp.concatenate([logs,jnp.zeros((6,BACKWARD_ROWS),F32)],axis=0).T
            lse=jnp.where(left,cols[:,0:1],cols[:,1:2])
            side=hot+spread(-lse,16)
            qs.append(stack_heads(queries,jnp.where(left,side,zero),jnp.where(left,zero,side),left))
            grad=d_context[here,g*WIDE:(g+1)*WIDE]
            product=as_float(grad)*as_float(context[here,g*WIDE:(g+1)*WIDE])
            dot_a=jnp.sum(jnp.where(left,product,0.0),axis=1,keepdims=True)
            dot_b=jnp.sum(jnp.where(left,0.0,product),axis=1,keepdims=True)
            side_g=spread(-jnp.where(left,dot_a,dot_b),0)
            gs.append(stack_heads(grad,jnp.where(left,side_g,zero),jnp.where(left,zero,side_g),left))
        start=pl.multiple_of(ranges[index]*KEY_TILE,KEY_TILE)
        def over(width):
            def run():
                span=pl.ds(start,width)
                for g in range(group):
                    p=jnp.exp(matmul_right_t(key_side[g,span,:],qs[g]))
                    dp=matmul_right_t(value_side[g,span,:],gs[g])
                    pb=p.astype(LOW); ds=(p*dp).astype(LOW)
                    d_value[g,span,:]+=matmul(pb,gs[g][:,:WIDE])
                    d_key[g,span,:]+=matmul(ds,qs[g][:,:WIDE])
                    dq=matmul(key_t[g,:,span],ds)
                    dq=jnp.concatenate([dq[:HEAD_DIM,:BACKWARD_ROWS],dq[HEAD_DIM:,BACKWARD_ROWS:]],axis=0)
                    d_packed[here,3*WIDE*g:3*WIDE*g+WIDE]=(dq.T*HEAD_DIM**-0.5).astype(LOW)
            return run
        lax.switch(ranges[tiles+index]-1,[over(KEY_TILE*(n+1)) for n in range(LEN//KEY_TILE)])
        return tuple(sums[g]+jnp.sum(as_float(d_packed[here,3*WIDE*g:3*WIDE*g+WIDE]),axis=0,keepdims=True) for g in range(group))
    sums=lax.fori_loop(0,tiles,tile,(jnp.zeros((1,WIDE),F32),)*group)
    for g in range(group):
        at=3*WIDE*g
        low=d_value[g].astype(LOW)
        d_packed[:,at+WIDE:at+2*WIDE]=d_key[g].astype(LOW)
        d_packed[:,at+2*WIDE:at+3*WIDE]=low
        bias_sums[0:1,g*WIDE:(g+1)*WIDE]=sums[g]
        bias_sums[1:2,g*WIDE:(g+1)*WIDE]=jnp.sum(as_float(low),axis=0,keepdims=True)
    if not pieces:
        return
    total[...]=matmul_left_t(inputs[...],d_packed[...])
    rows=D//pieces
    base=2*(LEN//BACKWARD_ROWS)+1
    x,y=ranges[base],ranges[base+1]
    for piece in range(pieces):
        dy,dx=divmod(piece,2)
        start=pl.multiple_of((jnp.bitwise_xor(y,dy)*2+jnp.bitwise_xor(x,dx))*rows,16)
        for j in range(group):
            here=slice(j*rows,(j+1)*rows)
            out[piece,here,:]=rounded(total[pl.ds(start,rows),j*CHUNK:(j+1)*CHUNK])


def attn_bwd(ranges,packed,ctx,dctx,lse,fq,fk,inputs,pieces):
    group=HALF_PAIRS
    whole=pl.BlockSpec((LEN,WIDE),lambda h,r:(0,0))
    half=2*(LEN//BACKWARD_ROWS)
    col=lambda w: pl.BlockSpec((LEN,w*group),lambda h,r:(0,r[half]+h))
    specs=[col(3*WIDE),col(WIDE),col(WIDE),pl.BlockSpec((group,2,LEN),lambda h,r:(r[half]+h,0,0)),whole,whole]
    operands=[packed,ctx,dctx,lse,fq,fk]
    outs=[shape((LEN,group*3*WIDE)),shape((2,group*WIDE),F32)]
    scratch=[pltpu.VMEM((group,LEN,2*WIDE),LOW)]*2+[pltpu.VMEM((group,WIDE,LEN),LOW)]+[pltpu.VMEM((group,LEN,WIDE),F32)]*2
    if pieces:
        specs.append(constant((LEN,D)))
        operands.append(inputs)
        outs.append(shape((pieces,group*(D//pieces),CHUNK)))
        scratch.append(pltpu.VMEM((D,group*CHUNK),F32))
    return pl.pallas_call(functools.partial(bwd_body,group=group,pieces=pieces),
        out_shape=outs,
        grid_spec=pltpu.PrefetchScalarGridSpec(num_scalar_prefetch=1,grid=(1,),
          in_specs=specs,
          out_specs=[constant(out.shape) for out in outs],
          scratch_shapes=scratch),
        name="attention_backward")(ranges,*operands)


def normalize(hidden):
    average = jnp.mean(hidden, axis=-1, keepdims=True)
    centered = hidden - average
    variance = jnp.mean(centered * centered, axis=-1, keepdims=True)
    inverse = lax.rsqrt(variance + EPSILON)
    return centered * inverse, inverse


def normalize_back(grad, normal, inverse):
    first = jnp.mean(grad, axis=-1, keepdims=True)
    second = jnp.mean(grad * normal, axis=-1, keepdims=True)
    return (grad - first - normal * second) * inverse


def column_sum(value):
    return jnp.sum(value, axis=0, keepdims=True)


def up_body(place, context, inputs, vectors, *refs):
    count = (len(refs) - 9) // 2
    out_pieces, up_pieces = refs[:count], refs[count : 2 * count]
    normal, inverse, low, activated, slope, w_out, w_up, out_sem, up_sem = refs[2 * count :]
    out_copies = assemble(place, out_pieces, w_out, out_sem)
    up_copies = assemble(place, up_pieces, w_up, up_sem)
    step = pl.program_id(0)

    @pl.when(step == 0)
    def _():
        start_all(out_copies)
        start_all(up_copies)
        wait_all(out_copies)

    attended = matmul(context[...], w_out[...]) + vectors[:, B_OUT : B_OUT + D]
    value, scale = normalize(as_float(inputs[...]) + attended)
    normal[...] = value
    inverse[...] = jnp.broadcast_to(scale, inverse.shape)
    normed = rounded(
        value * vectors[:, ATTN_GAIN : ATTN_GAIN + D] + vectors[:, ATTN_SHIFT : ATTN_SHIFT + D]
    )
    low[...] = normed

    @pl.when(step == 0)
    def _():
        wait_all(up_copies)

    for at in range(0, FF, D):
        up = matmul(normed, w_up[:, at : at + D]) + vectors[:, B_UP + at : B_UP + at + D]
        below = 0.5 + 0.5 * lax.erf(up * (0.5**0.5))
        density = jnp.exp(-0.5 * up * up) * 0.3989422804014327
        activated[:, at : at + D] = rounded(up * below)
        slope[:, at : at + D] = rounded(below + up * density)


def up_block(place, context, inputs, vectors, out_pieces, up_pieces):
    count = len(out_pieces)
    return call(
        up_body,
        "out_norm_up",
        (
            shape((LEN, D), F32),
            shape((LEN, WIDE), F32),
            shape((LEN, D)),
            shape((LEN, FF)),
            shape((LEN, FF)),
        ),
        (LEN // TOKEN_ROWS,),
        [tokens(D), tokens(D), constant((1, VECTORS))] + [ANYWHERE] * (2 * count),
        [tokens(D), tokens(WIDE), tokens(D), tokens(FF), tokens(FF)],
        [
            pltpu.VMEM((D, D), LOW),
            pltpu.VMEM((D, FF), LOW),
            pltpu.SemaphoreType.DMA((count,)),
            pltpu.SemaphoreType.DMA((count,)),
        ],
        flops=2 * LEN * D * (D + FF),
        exps=2 * LEN * FF,
    )(place, context, inputs, vectors, *out_pieces, *up_pieces)


def down_body(place, activated, slope, normal, cotangent, vectors, *refs):
    count = len(refs) - 7
    pieces = refs[:count]
    output, d_sum, d_down, d_up, sums, w_down, sem = refs[count:]
    copies = assemble(place, pieces, w_down, sem)
    step = pl.program_id(0)

    @pl.when(step == 0)
    def _():
        start_all(copies)
        sums[...] = jnp.zeros_like(sums)
        wait_all(copies)

    down = matmul(activated[...], w_down[...]) + vectors[:, B_DOWN : B_DOWN + D]
    gain = vectors[:, ATTN_GAIN : ATTN_GAIN + D]
    normed = normal[...] * gain + vectors[:, ATTN_SHIFT : ATTN_SHIFT + D]
    value, scale = normalize(normed + down)
    gain = vectors[:, FFN_GAIN : FFN_GAIN + D]
    output[...] = rounded(value * gain + vectors[:, FFN_SHIFT : FFN_SHIFT + D])
    grad = as_float(cotangent[...])
    sums[:, :D] += column_sum(grad * value)
    sums[:, D : 2 * D] += column_sum(grad)
    d_two = normalize_back(grad * gain, value, scale)
    d_sum[...] = d_two
    d_low = rounded(d_two)
    d_down[...] = d_low
    sums[:, 2 * D : 3 * D] += column_sum(as_float(d_low))
    for at in range(0, FF, D):
        d_activated = matmul_right_t(d_low, w_down[at : at + D, :])
        part = rounded(d_activated * as_float(slope[:, at : at + D]))
        d_up[:, at : at + D] = part
        sums[:, 3 * D + at : 4 * D + at] += column_sum(as_float(part))


def down_block(place, activated, slope, normal, cotangent, vectors, pieces):
    count = len(pieces)
    return call(
        down_body,
        "down_norm_back",
        (
            shape((LEN, D)),
            shape((LEN, D), F32),
            shape((LEN, D)),
            shape((LEN, FF)),
            shape((1, 3 * D + FF), F32),
        ),
        (LEN // TOKEN_ROWS,),
        [tokens(FF), tokens(FF), tokens(D), tokens(D), constant((1, VECTORS))]
        + [ANYWHERE] * count,
        [tokens(D), tokens(D), tokens(D), tokens(FF), constant((1, 3 * D + FF))],
        [pltpu.VMEM((FF, D), LOW), pltpu.SemaphoreType.DMA((count,))],
        flops=4 * LEN * D * FF,
    )(place, activated, slope, normal, cotangent, vectors, *pieces)


def back_body(place, d_up, d_sum_two, normal, inverse, vectors, *refs, shards):
    context, refs = refs[0], refs[1:]
    count = (len(refs) - 8 - 2 * shards) // 2
    up_pieces, out_pieces = refs[:count], refs[count : 2 * count]
    refs = refs[2 * count :]
    d_sum, d_context, sums = refs[:3]
    sends, keeps = refs[3 : 3 + shards], refs[3 + shards : 3 + 2 * shards]
    w_up, w_out, total, up_sem, out_sem = refs[-5:]
    up_copies = assemble(place, up_pieces, w_up, up_sem)
    out_copies = assemble(place, out_pieces, w_out, out_sem)
    step = pl.program_id(0)

    @pl.when(step == 0)
    def _():
        start_all(up_copies)
        start_all(out_copies)
        sums[...] = jnp.zeros_like(sums)
        wait_all(up_copies)
        wait_all(out_copies)

    d_normed = d_sum_two[...] + matmul_right_t(d_up[...], w_up[...])
    value = normal[...]
    sums[:, :D] += column_sum(d_normed * value)
    sums[:, D : 2 * D] += column_sum(d_normed)
    d_one = normalize_back(
        d_normed * vectors[:, ATTN_GAIN : ATTN_GAIN + D], value, inverse[:, :1]
    )
    d_sum[...] = d_one
    low = rounded(d_one)
    sums[:, 2 * D :] += column_sum(as_float(low))
    d_context[...] = rounded(matmul_right_t(low, w_out[...]))
    product = matmul_left_t(context[...], low)

    @pl.when(step == 0)
    def _():
        total[...] = product

    @pl.when(step > 0)
    def _():
        total[...] += product

    @pl.when(step == pl.num_programs(0) - 1)
    def _():
        rows = D // shards
        for d in range(shards):
            start = pl.multiple_of(jnp.bitwise_xor(place[Y], d) * rows, 16)
            for out, core in ((sends[d], 1 - place[CORE]), (keeps[d], place[CORE])):
                lane = pl.multiple_of(core * CHUNK, WIDE)
                out[...] = rounded(total[pl.ds(start, rows), pl.ds(lane, CHUNK)])


def back_block(
    place, d_up, d_sum_two, normal, inverse, vectors, context, up_pieces, out_pieces, shards
):
    count = len(up_pieces)
    half = (D // shards, CHUNK)
    found = call(
        functools.partial(back_body, shards=shards),
        "norm_back",
        [shape((LEN, D), F32), shape((LEN, D)), shape((1, 3 * D), F32)]
        + [shape(half)] * (2 * shards),
        (LEN // TOKEN_ROWS,),
        [tokens(FF), tokens(D), tokens(D), tokens(WIDE), constant((1, VECTORS)), tokens(D)]
        + [ANYWHERE] * (2 * count),
        [tokens(D), tokens(D), constant((1, 3 * D))] + [constant(half)] * (2 * shards),
        [
            pltpu.VMEM((D, FF), LOW),
            pltpu.VMEM((D, D), LOW),
            pltpu.VMEM((D, D), F32),
            pltpu.SemaphoreType.DMA((count,)),
            pltpu.SemaphoreType.DMA((count,)),
        ],
        flops=2 * LEN * D * (FF + 2 * D),
    )(place, d_up, d_sum_two, normal, inverse, vectors, context, *up_pieces, *out_pieces)
    return found[0], found[1], found[2], found[3 : 3 + shards], found[3 + shards :]


def input_body(place, weight, d_sum, *refs, spans):
    output, pieces = refs[-1], refs[:-1]
    total = d_sum[...]
    for piece, (partner, first, count) in zip(pieces, spans):
        block = 1 - place[CORE] if partner else place[CORE]
        at = pl.multiple_of((first + block * count) * TRIPLE, WIDE)
        total += matmul_right_t(piece[...], weight[:, pl.ds(at, count * TRIPLE)])
    output[...] = rounded(total)


def input_gradient(place, weight, d_sum, pieces, spans):
    return call(
        functools.partial(input_body, spans=spans),
        "input_gradient",
        shape((LEN, D)),
        (LEN // TOKEN_ROWS,),
        [constant((D, 3 * D)), tokens(D)] + [tokens(piece.shape[1]) for piece in pieces],
        tokens(D),
        flops=6 * LEN * D * D,
    )(place, weight, d_sum, *pieces)


def piece_row(place, piece, rows, cuts):
    dy, dx = divmod(piece, cuts)
    start = jnp.bitwise_xor(place[Y], dy) * (cuts * rows)
    if cuts == 2:
        start += jnp.bitwise_xor(place[X], dx) * rows
    return pl.multiple_of(start, 16)


def down_gradient_body(place, left, right, *refs, shards, adds):
    value = matmul_left_t(left[...], right[...])
    if not adds:
        refs[0][0] = rounded(value)
        return
    value = rounded(value + as_float(refs[0][0]))
    for at in range(shards):

        @pl.when(pl.program_id(0) == at)
        def _(at=at):
            refs[1 + at][...] = value


def down_gradient(place, activated, d_down, partner, shards, got=None):
    rows = FF // shards
    pick_column = lambda i, p: (0, 1 - p[CORE] if partner else p[CORE])
    one = pl.BlockSpec((1, rows, CHUNK), lambda i, p: (i, 0, 0))
    operands, specs = [activated, d_down], []
    if got is None:
        outs, out_specs = shape((shards, rows, CHUNK)), one
    else:
        operands.append(got)
        specs.append(one)
        outs, out_specs = (shape((rows, CHUNK)),) * shards, [constant((rows, CHUNK))] * shards
    return call(
        functools.partial(down_gradient_body, shards=shards, adds=got is not None),
        "down_gradient",
        outs,
        (shards,),
        [
            pl.BlockSpec((LEN, rows), lambda i, p: (0, jnp.bitwise_xor(p[Y], i))),
            pl.BlockSpec((LEN, CHUNK), pick_column),
        ]
        + specs,
        out_specs,
        flops=LEN * D * FF,
    )(place, *operands)


def row_gradient_body(place, left, right, *refs, pieces, cuts, adds, extends):
    got, refs = (refs[0], refs[1:]) if adds else (None, refs)
    outs, total = refs[pieces if extends else 0 : -1], refs[-1]
    rows = D // pieces
    total[...] = matmul_left_t(left[...], right[...])
    for j in range(right.shape[1] // CHUNK):
        here = slice(j * rows, (j + 1) * rows)
        for piece in range(pieces):
            start = piece_row(place, piece, rows, cuts)
            value = total[pl.ds(start, rows), j * CHUNK : (j + 1) * CHUNK]
            if adds:
                outs[piece][here, :] = rounded(value + as_float(got[piece, here, :]))
            else:
                outs[0][piece, here, :] = rounded(value)


def row_gradient(
    place, left, right, width, first, steps, pieces, cuts, got=None, spare=0, into=None
):
    rows = D // pieces
    block = width // CHUNK * rows
    specs = [
        constant((LEN, D)),
        pl.BlockSpec((LEN, width), lambda i, p: (0, first(p) + i)),
    ]
    operands, aliases, at = [left, right], {}, 0
    if got is None:
        outs = shape((pieces, steps * block, CHUNK))
        out_specs = pl.BlockSpec((pieces, block, CHUNK), lambda i, p: (0, i, 0))
    else:
        specs.append(pl.BlockSpec((pieces, block, CHUNK), lambda i, p: (0, i, 0)))
        operands.append(got)
        height = steps * block + spare * rows
        if into is not None:
            height = into[0].shape[0]
            at = height // block - steps
            aliases = {len(operands) + 1 + n: n for n in range(pieces)}
            operands += into
            specs += [ANYWHERE] * pieces
        outs = (shape((height, CHUNK)),) * pieces
        out_specs = [pl.BlockSpec((block, CHUNK), lambda i, p: (at + i, 0))] * pieces
    return call(
        functools.partial(
            row_gradient_body,
            pieces=pieces,
            cuts=cuts,
            adds=got is not None,
            extends=into is not None,
        ),
        "row_gradient",
        outs,
        (steps,),
        specs,
        out_specs,
        [pltpu.VMEM((D, width), F32)],
        flops=2 * LEN * D * width * steps,
        aliases=aliases,
    )(place, *operands)


class Place:
    def __init__(self, replicas, shards):
        self.replicas, self.shards, self.depth = replicas, shards, replicas // 4
        replica = lax.axis_index("replica")
        self.index = [replica % 2, replica // 2 % 2, replica // 4, lax.axis_index("shard")]
        self.core, self.x, self.z, self.y = self.index
        self.z_bits = self.depth.bit_length() - 1
        self.index += [self.z >> bit & 1 for bit in range(self.z_bits)]
        self.vector = jnp.stack(self.index).astype(jnp.int32)

    def shard(self, value, mask):
        return lax.ppermute(value, "shard", [(i, i ^ mask) for i in range(self.shards)])

    def cross(self, value, dy, dx):
        def partner(i):
            replica, shard = divmod(i, self.shards)
            return (replica ^ (2 * dx)) * self.shards + (shard ^ dy)

        pairs = [(i, partner(i)) for i in range(self.replicas * self.shards)]
        return lax.ppermute(value, ("replica", "shard"), pairs)

    def replica(self, value, mask):
        return lax.ppermute(value, "replica", [(i, i ^ mask) for i in range(self.replicas)])


def tie(value, *first):
    return lax.optimization_barrier((value,) + first)[0]


def pick(options, index):
    chosen = options[-1]
    for at in range(len(options) - 2, -1, -1):
        chosen = jnp.where(index == at, options[at], chosen)
    return chosen


def gather_shards(value, at):
    found = {0: value}
    mask = 1
    while mask < at.shards:
        for d in range(mask):
            found[d | mask] = at.shard(found[d], mask)
        mask *= 2
    return [found[d] for d in range(at.shards)]


def half_rows(weight, at):
    half = weight.shape[0] // 2
    return lax.dynamic_slice_in_dim(weight, at.core * half, half, 0)


def weight_pieces(weight, near, at):
    pieces = [weight]
    for block in near[1:]:
        pieces += [block, at.replica(block, 1)]
    return pieces


def exchange_pieces(parts, at):
    return [parts[0]] + [at.cross(parts[n], *divmod(n, 2)) for n in range(1, len(parts))]


def exchange_shards(parts, at):
    mask = at.shards // 2
    while mask > 1:
        parts = [
            rounded(as_float(parts[d]) + as_float(at.shard(parts[d | mask], mask)))
            for d in range(mask)
        ]
        mask //= 2
    return parts[0], at.shard(parts[1], 1)


def add_job(at, groups, parts, block, plain_block):
    heights = [rows // parts for _, rows, _ in groups]
    if any(h % 16 or first % h for h, (_, _, first) in zip(heights, groups)):
        found = []
        for n in range(parts):
            cuts = []
            for (terms, _, first), h in zip(groups, heights):
                start = first + plain_block(n) * h
                cut = [as_float(lax.dynamic_slice_in_dim(t, start, h, 0)) for t in terms]
                cuts.append(rounded(sum(cut)))
            found.append(jnp.concatenate(cuts) if len(cuts) > 1 else cuts[0])
        return found

    def body(place, ins, outs):
        for n in range(parts):
            at_term, row = 0, 0
            for (terms, _, first), h in zip(groups, heights):
                here = pl.ds(pl.multiple_of(first + block(n, place) * h, 16), h)
                total = as_float(ins[at_term][here, :])
                for term in range(1, len(terms)):
                    total += as_float(ins[at_term + term][here, :])
                outs[n][row : row + h, :] = rounded(total)
                at_term, row = at_term + len(terms), row + h

    operands = [term for terms, _, _ in groups for term in terms]
    results = [jax.ShapeDtypeStruct((sum(heights), CHUNK), LOW)] * parts
    return body, operands, results


def all_rows(terms):
    return terms, terms[0].shape[0], 0


def halve(at, which, *groups):
    return add_job(
        at,
        groups,
        2,
        lambda n, p: jnp.bitwise_xor(p[which], n),
        lambda n: at.index[which] ^ n,
    )


def add_small(value, got):
    def body(place, ins, outs):
        outs[0][...] = ins[0][...] + ins[1][...]

    return body, [value, got], [jax.ShapeDtypeStruct(value.shape, F32)]


def split_z(at, terms):
    return add_job(
        at, [all_rows(terms)], at.depth, lambda n, p: jnp.bitwise_xor(p[Z], n), lambda n: at.z ^ n
    )


def total(at, terms):
    return add_job(at, [all_rows(terms)], 1, lambda n, p: 0, lambda n: 0)


def join(at, pieces, block, plain_block):
    rows = pieces[0].shape[0]
    count = len(pieces)
    if rows % 16:
        where = [plain_block(n) for n in range(count)]
        joined = []
        for j in range(count):
            chosen = pieces[0]
            for n in range(1, count):
                chosen = jnp.where(where[n] == j, pieces[n], chosen)
            joined.append(chosen)
        return [jnp.concatenate(joined)]

    def body(place, ins, outs):
        for n in range(count):
            start = pl.multiple_of(block(n, place) * rows, 16)
            outs[0][pl.ds(start, rows), :] = ins[n][...]

    result = jax.ShapeDtypeStruct((rows * count, CHUNK), LOW)
    return body, list(pieces), [result]


def join_z(at, pieces):
    return join(at, pieces, lambda n, p: jnp.bitwise_xor(p[Z], n), lambda n: at.z ^ n)


def bit_order(at):
    order = [0]
    for bit in reversed(range(at.z_bits)):
        order += [d | 1 << bit for d in order]
    return order


def join_bits(at, pieces):
    order, top = bit_order(at), at.z_bits - 1

    def place_of(n, bits):
        return sum((bits[bit] ^ (order[n] >> bit & 1)) << (top - bit) for bit in range(at.z_bits))

    return join(
        at,
        pieces,
        lambda n, p: place_of(n, [p[Z_BITS + bit] for bit in range(at.z_bits)]),
        lambda n: place_of(n, at.index[Z_BITS:]),
    )


def join_split(at, pieces):
    order = bit_order(at)
    return join(
        at, pieces, lambda n, p: jnp.bitwise_xor(p[Z], order[n]), lambda n: at.z ^ order[n]
    )


def kept_near(operands):
    return [pltpu.with_memory_space_constraint(value, pltpu.VMEM) for value in operands]


def run_jobs(at, *jobs, near=False):
    results = [job if isinstance(job, list) else None for job in jobs]
    todo = [n for n, job in enumerate(jobs) if not isinstance(job, list)]
    if todo:
        operands, outs = [], []
        for n in todo:
            operands += jobs[n][1]
            outs += jobs[n][2]

        def body(place, *refs):
            ins, outs = refs[: len(operands)], refs[len(operands) :]
            for n in todo:
                job_body, job_ins, job_outs = jobs[n]
                job_body(place, ins[: len(job_ins)], outs[: len(job_outs)])
                ins, outs = ins[len(job_ins) :], outs[len(job_outs) :]

        found = call(
            body,
            "exchange_step",
            outs,
            (1,),
            [LOCAL] * len(operands),
            [LOCAL] * len(outs),
        )(at.vector, *(kept_near(operands) if near else operands))
        for n in todo:
            count = len(jobs[n][2])
            results[n], found = list(found[:count]), found[count:]
    return results


def send_x(halves, at):
    return halves[0], at.replica(halves[1], 2)


def send_bit(halves, bit, at):
    return halves[0], at.replica(halves[1], 4 << bit)


def send_z(blocks, at):
    return [blocks[0]] + [at.replica(blocks[d], 4 * d) for d in range(1, at.depth)]


def spread_z(whole, at):
    return [whole] + [at.replica(whole, 4 * d) for d in range(1, at.depth)]


def spread_bit(found, bit, at):
    return found + [at.replica(piece, 4 << bit) for piece in found]


def spread_x(mine, at):
    return mine, at.replica(mine, 2)


def spread_core(mine, other, at):
    return [mine, other, at.replica(mine, 1), at.replica(other, 1)]


def finish_down_body(place, *refs):
    for index in range(4):

        @pl.when(pl.program_id(0) == index)
        def _(index=index):
            refs[4][...] = as_float(refs[index][...])


def finish_up_body(place, *refs, rows, blocks):
    sources, (up, out) = refs[:4], refs[4:]
    for index in range(4):

        @pl.when(pl.program_id(0) == index)
        def _(index=index):
            source = sources[index]
            for j in range(blocks):
                up[:, j * CHUNK : (j + 1) * CHUNK] = as_float(source[j * rows : (j + 1) * rows, :])
            out[...] = as_float(source[blocks * rows :, :])


def finish_down(at, sources):
    rows = FF // at.shards
    half = lambda i, p: jnp.bitwise_xor(p[X], i % 2)
    core = lambda i, p: jnp.bitwise_xor(p[CORE], i // 2)
    return call(
        finish_down_body,
        "finish_down",
        shape((rows, D), F32),
        (4,),
        [LOCAL] * len(sources),
        pl.BlockSpec((rows // 2, CHUNK), lambda i, p: (half(i, p), core(i, p))),
    )(at.vector, *sources)


def finish_up(at, sources):
    rows = D // at.shards
    blocks = FF // (4 * CHUNK)
    half = lambda i, p: jnp.bitwise_xor(p[X], i % 2)
    core = lambda i, p: jnp.bitwise_xor(p[CORE], i // 2)
    return call(
        functools.partial(finish_up_body, rows=rows, blocks=blocks),
        "finish_up",
        (shape((rows, FF), F32), shape((rows, D), F32)),
        (4,),
        [LOCAL] * len(sources),
        [
            pl.BlockSpec((rows, blocks * CHUNK), lambda i, p: (0, core(i, p) * 2 + half(i, p))),
            pl.BlockSpec((rows // 2, CHUNK), lambda i, p: (half(i, p), core(i, p))),
        ],
    )(at.vector, *sources)


def finish_attention_body(place, *refs, rows):
    sources, qkv = refs[:4], refs[4]
    half = rows // 2
    for index in range(4):
        source = sources[index]
        core = jnp.bitwise_xor(place[CORE], index // 2)
        start = pl.multiple_of(jnp.bitwise_xor(place[X], index % 2) * half, 16)
        for pair in range(HALF_PAIRS):
            value = as_float(source[pair * half : (pair + 1) * half, :])
            for part in range(3):
                lane = pl.multiple_of(part * D + (core * HALF_PAIRS + pair) * WIDE, WIDE)
                qkv[pl.ds(start, half), pl.ds(lane, WIDE)] = value[
                    :, part * WIDE : (part + 1) * WIDE
                ]


def finish_attention(at, sources):
    rows = D // at.shards
    return call(
        functools.partial(finish_attention_body, rows=rows),
        "finish_attention",
        shape((rows, 3 * D), F32),
        (1,),
        [LOCAL] * len(sources),
        constant((rows, 3 * D)),
    )(at.vector, *kept_near(sources))


def local(
    replicas,
    shards,
    inputs,
    segments,
    w_qkv,
    b_qv,
    w_out,
    b_out,
    attn_gain,
    attn_shift,
    w_up,
    b_up,
    w_down,
    b_down,
    ffn_gain,
    ffn_shift,
    cotangent,
):
    at = Place(replicas, shards)
    place = at.vector
    segments = segments.reshape(LEN)

    near_qkv = gather_shards(half_rows(w_qkv, at), at)
    vectors = (b_qv, b_out, attn_gain, attn_shift, b_up, b_down, ffn_gain, ffn_shift)
    sizes = [vector.shape[0] for vector in vectors]
    small = gather_shards(jnp.concatenate(vectors), at)
    small = as_float(jnp.stack([pick(small, at.y ^ j) for j in range(shards)]))
    full, offset = [], 0
    for size in sizes:
        full.append(small[:, offset : offset + size].reshape(-1))
        offset += size
    full = jnp.concatenate(full).reshape(1, VECTORS)
    feature_q, feature_k = document_features(segments)
    forward_ranges = key_ranges(segments, FORWARD_ROWS)
    backward_ranges = key_ranges(segments, BACKWARD_ROWS)

    pieces_qkv = weight_pieces(w_qkv, near_qkv, at)
    half_out, half_up = (half_rows(w, at) for w in (w_out, w_up))
    half_out, half_up, *_ = lax.optimization_barrier((half_out, half_up, near_qkv[-1]))
    near_out, near_up = gather_shards(half_out, at), gather_shards(half_up, at)
    projected, weight_qkv = project(place, inputs, full, pieces_qkv)
    context, log_total = attn_fwd(
        forward_ranges, projected, feature_q, feature_k, 6
    )
    near_out, near_up, context = lax.optimization_barrier((near_out, near_up, context))
    half_down = tie(half_rows(w_down, at), near_up[-1])
    near_down = gather_shards(half_down, at)
    pieces_out = weight_pieces(w_out, near_out, at)
    pieces_up = weight_pieces(w_up, near_up, at)
    normal, inverse, low, activated, slope = up_block(
        place, context, inputs, full, pieces_out, pieces_up
    )
    near_down, activated = lax.optimization_barrier((near_down, activated))
    pieces_down = weight_pieces(w_down, near_down, at)
    layer_output, d_sum_two, d_down, d_up, sums_two = down_block(
        place, activated, slope, normal, cotangent, full, pieces_down
    )

    barrier = lax.optimization_barrier
    other_half, own_half = (lambda p: 2 * (1 - p[CORE])), (lambda p: 2 * p[CORE])
    wide = FF // 4

    down_send = down_gradient(place, activated, d_down, True, shards)
    down_got = at.replica(down_send, 1)
    up_send = row_gradient(place, low, d_up, wide, other_half, 2, shards, 1)
    up_got = at.replica(up_send, 1)
    down_parts = down_gradient(place, activated, d_down, False, shards, down_got)
    down = exchange_shards(down_parts, at)
    up_parts = row_gradient(place, low, d_up, wide, own_half, 2, shards, 1, up_got)
    up_parts, d_up = barrier((up_parts, d_up))
    d_sum_one, d_context, sums_one, out_sends, out_keeps = back_block(
        place, d_up, d_sum_two, normal, inverse, full, context, pieces_up, pieces_out, shards
    )

    def attention_back(half, d_context, pieces):
        return attn_bwd(
            jnp.concatenate([backward_ranges, jnp.stack([half, at.x, at.y]).astype(jnp.int32)]),
            projected,
            context,
            d_context,
            log_total,
            feature_q,
            feature_k,
            inputs,
            pieces,
        )

    bits = at.z_bits
    pieces = 2 * shards
    out_gots = [at.replica(send, 1) for send in out_sends]
    down, out_keeps = barrier((down, out_keeps))
    down, *out_parts = run_jobs(
        at,
        halve(at, X, all_rows(down)),
        *[total(at, [keep, got]) for keep, got in zip(out_keeps, out_gots)],
    )
    down = send_x(down, at)
    out_parts, up_parts = barrier(([part[0] for part in out_parts], up_parts))
    up, out = exchange_shards(up_parts, at), exchange_shards(out_parts, at)
    out_parts, up_parts, d_context = barrier((out_parts, up_parts, d_context))
    d_other, bias_other, send = attention_back(1 - at.core, d_context, pieces)
    got = at.replica(send, 1)
    down, up, out, d_other, d_context = barrier((down, up, out, d_other, d_context))
    down, up = run_jobs(at, split_z(at, down), halve(at, X, all_rows(up), all_rows(out)))
    down = send_z(down, at)
    up = send_x(up, at)
    d_own, bias_own = attention_back(at.core, tie(d_context, up[0]), 0)
    up, down, d_own, got = barrier((up, down, d_own, got))
    (up,) = run_jobs(at, halve(at, Z_BITS, all_rows(up)), near=True)
    parts = row_gradient(
        place, inputs, tie(d_own, up[0]), HALF_PAIRS * TRIPLE, lambda p: 0, 1, pieces, 2, got
    )
    up = send_bit(up, 0, at)
    mine = exchange_pieces(parts, at)

    bias = jnp.concatenate(
        [pick([bias_own, bias_other], at.core), pick([bias_other, bias_own], at.core)], axis=1
    )
    sums_one, sums_two = sums_one[0], sums_two[0]
    grads = (
        bias.reshape(-1),
        sums_one[2 * D :],
        sums_one[:D],
        sums_one[D : 2 * D],
        sums_two[3 * D :],
        sums_two[2 * D : 3 * D],
        sums_two[:D],
        sums_two[D : 2 * D],
    )
    packed = jnp.concatenate([grad.reshape(shards, -1) for grad in grads], axis=1)
    packed = packed.reshape(shards, -1, 128)
    small = [lax.dynamic_index_in_dim(packed, at.y ^ d, 0, False) for d in range(shards)]
    mask = shards // 2
    while mask > 1:
        small = [small[d] + at.shard(small[d | mask], mask) for d in range(mask)]
        mask //= 2

    down, up, d_own, small, parts = barrier((down, up, d_own, small, parts))
    if bits > 1:
        down, up = run_jobs(
            at, total(at, down), halve(at, Z_BITS + 1, all_rows(up)), near=True
        )
        up = send_bit(up, 1, at)
        for bit in range(2, bits):
            (up,) = run_jobs(at, halve(at, Z_BITS + bit, all_rows(up)))
            up = send_bit(up, bit, at)
    else:
        (down,) = run_jobs(at, total(at, down))
    down, d_own = barrier((down, d_own))
    down = spread_bit(down, bits - 1, at)
    input_grad = input_gradient(
        place,
        weight_qkv,
        d_sum_one,
        [d_other, d_own],
        ((True, 0, HALF_PAIRS), (False, 0, HALF_PAIRS)),
    )
    down, up, input_grad = barrier((down, up, input_grad))
    (up,) = run_jobs(at, total(at, up), near=True)
    mine, up = barrier((mine, up))
    (mine,) = run_jobs(at, split_z(at, mine), near=True)
    mine = send_z(mine, at)
    for bit in reversed(range(bits - 1)):
        down = spread_bit(down, bit, at)
    up = spread_bit(up, bits - 1, at)
    small = (small[0], at.shard(small[1], 1))
    down, up, small, kept = barrier((down, up, small, mine[0]))
    down, small = run_jobs(at, join_split(at, down), add_small(*small), near=True)
    small = (small[0], at.replica(small[0], 1))
    mine, small, kept = barrier((mine, small, down))
    mine, small = run_jobs(at, total(at, mine), add_small(*small), near=True)
    down = spread_x(kept[0], at)
    mine = spread_z(mine[0], at)
    for bit in reversed(range(bits - 1)):
        up = spread_bit(up, bit, at)
    small = (small[0], at.replica(small[0], 2))
    up, small, kept = barrier((up, small, mine[0]))
    up, small = run_jobs(at, join_bits(at, up), add_small(*small), near=True)
    mine, up, small = barrier((mine, up, small))
    (mine,) = run_jobs(at, join_z(at, mine), near=True)
    mine = spread_x(mine[0], at)
    up = spread_x(up[0], at)
    small = [small[0]] + [at.replica(small[0], 4 * d) for d in range(1, at.depth)]
    down, kept = barrier((down, mine[0]))
    grad_w_down = finish_down(at, spread_core(*down, at))
    up, grad_w_down, small = barrier((up, grad_w_down, small))
    small = sum(small)
    grad_w_up, grad_w_out = finish_up(at, spread_core(*up, at))
    mine, grad_w_up = barrier((mine, grad_w_up))
    grad_w_qkv = finish_attention(at, spread_core(*mine, at))

    packed = small.reshape(-1)
    owned, offset = [], 0
    for size in sizes:
        owned.append(packed[offset : offset + size])
        offset += size
    return (
        layer_output,
        input_grad,
        grad_w_qkv,
        owned[0],
        grad_w_out,
        owned[1],
        owned[2],
        owned[3],
        grad_w_up,
        owned[4],
        grad_w_down,
        owned[5],
        owned[6],
        owned[7],
    )


def solution(mesh):
    token, matrix, vector = P(("replica", "shard"), None), P("shard", None), P("shard")
    weights = (matrix, vector, matrix, vector, vector, vector)
    weights += (matrix, vector, matrix, vector, vector, vector)
    return jax.shard_map(
        functools.partial(local, mesh.shape["replica"], mesh.shape["shard"]),
        mesh=mesh,
        in_specs=(token, token) + weights + (token,),
        out_specs=(token, token) + weights,
        check_vma=False,
    )
```
